32 devices in a mesh: parts: 2 (over y), seq: 4 (over z), chan: 2 (over x), rep: 2 (over core).
Axes of the slice: x: 2, y: 2, z: 4, core: 2. Of those that a mesh axis runs over, the one named last changes fastest.
Arguments:
- tokens: bfloat16 [4096, 4096], P(('parts', 'seq'), ('chan', 'rep')), parts along dimension 0, may hold values from -6 to 6
- w_query: bfloat16 [4096, 4096], P('seq', ('chan', 'rep')), may hold values from -0.09375 to 0.09375
- w_key: bfloat16 [4096, 4096], P('seq', ('chan', 'rep')), may hold values from -0.09375 to 0.09375
- w_value: bfloat16 [4096, 4096], P('seq', ('chan', 'rep')), may hold values from -0.09375 to 0.09375
- decay_rate: float32 [4096, 16], P(('chan', 'rep', 'seq')), may hold values from 4.8828125e-06 to 0.04, as said below
- residue: float32 [4096, 16], P(('chan', 'rep', 'seq')), may hold values from -1.5 to 1.5
- carried: float32 [8192, 16], P(('parts', 'chan', 'rep', 'seq')), parts along dimension 0, may hold values from -6 to 6
Outputs:
- gated_output: bfloat16 [4096, 4096], P(('parts', 'seq'), ('chan', 'rep')), parts along dimension 0
- new_state: float32 [8192, 16], P(('parts', 'chan', 'rep', 'seq')), parts along dimension 0
The draws below stay inside these ranges and needn't reach their ends.
There are 2 independent parts, one for each index of `parts`. The reference program is written for one: setup_inputs(seed, part) draws one part's arguments, and reference() takes and returns one part's arrays. A program takes and returns all parts, laid end to end along the dimension named above; an argument that names none is the same for every part. Nothing has to cross between parts.
Inputs may be any that keep to these rules, and one draw needn't show every extreme that they name: `decay_rate`: each rate lies between 0.01 / 2048 and 0.04.
All inputs are finite; a program needn't handle non-finite values.
Results may differ from the reference program's by a relative error of at most 0.0066.
Values may be sent and summed in bfloat16 or wider, within the bound.
A program may use at most 128 MiB of HBM per device.

```python
import math
import jax
import jax.numpy as jnp
from jax import lax

D = 4096
MODES = 16
LENGTH = 2048


def draw_decay_rate(key, part):
    lowest = 0.01 / LENGTH
    subkeys = jax.random.split(key, 1)
    return jnp.exp(jax.random.uniform(subkeys[0], (D, MODES), jnp.float32, math.log(lowest), math.log(0.04))).astype(jnp.float32)


def level_of(own_key, extent, cuts, least, top_value):
    def one(dim, parts):
        heights = jax.random.uniform(jax.random.fold_in(jax.random.fold_in(own_key, 6), dim), (parts,), jnp.float32, least / len(cuts), top_value / len(cuts))
        return jnp.repeat(jnp.exp(heights), extent[dim] // parts).reshape((-1,) + (1,) * (len(extent) - dim - 1))

    gain = one(*cuts[0])
    for cut in cuts[1:]:
        gain = gain * one(*cut)
    return gain


def noise(stream_key, extent, scale, bound, cuts=(), kind=jnp.bfloat16):
    loudness = level_of(stream_key, extent, cuts, -0.22, 0.18) if cuts else 1.0
    values = jax.random.normal(stream_key, extent, jnp.float32) * scale * loudness
    return jnp.minimum(jnp.maximum(values, -bound), bound).astype(kind)


def setup_inputs(seed: int = 0, part: int = 0) -> dict:
    key_of = jax.random.split(jax.random.key(seed), 8)
    part_keys = jax.random.split(jax.random.fold_in(key_of[7], part), 8)
    tokens = noise(part_keys[0], (LENGTH, D), 1.0, 6.0, ((0, 4), (1, 4)))
    w_query = noise(key_of[1], (D, D), D ** -0.5, 0.09375, ((0, 4), (1, 4)))
    w_key = noise(key_of[2], (D, D), D ** -0.5, 0.09375, ((0, 4), (1, 4)))
    w_value = noise(key_of[3], (D, D), D ** -0.5, 0.09375, ((0, 4), (1, 4)))
    decay_rate = draw_decay_rate(jax.random.fold_in(key_of[7], 71), part)
    residue = noise(key_of[5], (D, MODES), 0.25, 1.5, ((0, 16),), jnp.float32)
    carried = noise(part_keys[6], (D, MODES), 1.0, 6.0, ((0, 16),), jnp.float32)
    return {"tokens": tokens, "w_query": w_query, "w_key": w_key, "w_value": w_value, "decay_rate": decay_rate, "residue": residue, "carried": carried}


def channel_group(operands):
    signal, decay_rates, residues, start_state = operands
    seq_length = signal.shape[1]
    offsets = jnp.arange(seq_length, dtype=jnp.float32)
    scaling = jnp.sqrt(-jnp.expm1(-2.0 * decay_rates))
    powers = jnp.exp(-decay_rates[:, :, None] * offsets[None, None, :])
    kernel = lax.optimization_barrier(jnp.sum((residues * scaling)[:, :, None] * powers, axis=1))
    padded_size = 2 * seq_length
    spectrum = jnp.fft.rfft(signal, padded_size) * jnp.fft.rfft(kernel, padded_size)
    direct = jnp.fft.irfft(spectrum, padded_size)[:, :seq_length]
    carried_part = lax.optimization_barrier(jnp.sum((residues * start_state * jnp.exp(-decay_rates))[:, :, None] * powers, axis=1))
    final_state = jnp.exp(-decay_rates * seq_length) * start_state + scaling * lax.optimization_barrier(jnp.sum(powers[:, :, ::-1] * signal[:, None, :], axis=2))
    return (direct + carried_part, final_state)

def reference(tokens, w_query, w_key, w_value, decay_rate, residue, carried):
    query_rows = jnp.dot(tokens, w_query, preferred_element_type=jnp.float32).astype(jnp.bfloat16)
    key_rows = jnp.dot(tokens, w_key, preferred_element_type=jnp.float32).astype(jnp.bfloat16)
    value_rows = jnp.dot(tokens, w_value, preferred_element_type=jnp.float32).astype(jnp.bfloat16)
    query_rows, key_rows, value_rows = lax.optimization_barrier((query_rows, key_rows, value_rows))
    product = (key_rows.astype(jnp.float32) * value_rows.astype(jnp.float32)).astype(jnp.bfloat16)
    product = lax.optimization_barrier(product)
    signal = product.astype(jnp.float32).T
    groups = D // 256
    conv, final_state = lax.map(channel_group, (signal.reshape(groups, 256, -1), decay_rate.reshape(groups, 256, -1), residue.reshape(groups, 256, -1), carried.reshape(groups, 256, -1)))
    conv = conv.reshape(D, -1).astype(jnp.bfloat16)
    conv = lax.optimization_barrier(conv)
    gated_output = (query_rows.astype(jnp.float32) * conv.T.astype(jnp.float32)).astype(jnp.bfloat16)
    return (gated_output, final_state.reshape(D, -1))
```

```python
import functools

import jax
import jax.numpy as jnp
from jax import lax
from jax.experimental import pallas as pl
from jax.experimental.pallas import tpu as pltpu
from jax.sharding import PartitionSpec as P

BLOCK = 128
LANES = 128
CHUNKS = 8
MESH = pl.DeviceIdType.MESH


HIGHEST_PRECISION = lax.Precision.HIGHEST


def mode_scale(decay_rates):
    return jnp.sqrt(-jnp.expm1(-2.0 * decay_rates))


def local_ends(blocks, decay_rates):
    block_width = blocks.shape[2]
    offsets = jnp.arange(block_width, dtype=jnp.float32)
    tail_powers = jnp.exp(-decay_rates[:, :, None] * (block_width - 1.0 - offsets)[None, None, :])
    sums_here = jnp.einsum("cnb,cmb->cnm", blocks, tail_powers, precision=HIGHEST_PRECISION)
    return mode_scale(decay_rates)[:, None, :] * sums_here


def combine_states(earlier, later):
    return (earlier[0] * later[0], later[0] * earlier[1] + later[1])


def block_sums(block_ends, decay_rates, block_width):
    step_decay = jnp.broadcast_to(jnp.exp(-decay_rates * block_width)[:, None, :], block_ends.shape)
    unused_decay, running = lax.associative_scan(combine_states, (step_decay, block_ends), axis=1)
    return running


def entering_states(running, decay_rates, start_state, block_width):
    count_blocks = running.shape[1]
    block_starts = jnp.arange(count_blocks, dtype=jnp.float32) * block_width
    decayed = (
        jnp.exp(-decay_rates[:, None, :] * block_starts[None, :, None]) * start_state[:, None, :]
    )
    earlier_sums = jnp.concatenate([jnp.zeros_like(running[:, :1]), running[:, :-1]], axis=1)
    final_state = (
        jnp.exp(-decay_rates * (count_blocks * block_width)) * start_state + running[:, -1]
    )
    return (decayed + earlier_sums, final_state)


def block_convolve(blocks, decay_rates, residues, entering):
    block_width = blocks.shape[2]
    offsets = jnp.arange(block_width, dtype=jnp.float32)
    powers = jnp.exp(-decay_rates[:, :, None] * offsets[None, None, :])
    kernel = jnp.sum((residues * mode_scale(decay_rates))[:, :, None] * powers, axis=1)
    out_index = jnp.arange(block_width, dtype=jnp.int32)[:, None]
    in_index = jnp.arange(block_width, dtype=jnp.int32)[None, :]
    lag = jnp.maximum(out_index - in_index, 0)
    causal = (out_index >= in_index).astype(jnp.float32)
    toeplitz = kernel[:, lag] * causal[None, :, :]
    direct = jnp.einsum("cij,cnj->cni", toeplitz, blocks, precision=HIGHEST_PRECISION)
    leading = residues[:, :, None] * jnp.exp(
        -decay_rates[:, :, None] * (offsets + 1.0)[None, None, :]
    )
    return direct + jnp.einsum("cnm,cmb->cnb", entering, leading, precision=HIGHEST_PRECISION)


def per_device(tokens, w_query, w_key, w_value, decay_rate, residue, carried):
    gathered = lax.all_gather(tokens, ("chan", "rep"), axis=1, tiled=True)
    pieces = (
        lax.all_gather(w_query, "seq", axis=0, tiled=True),
        lax.all_gather(w_key, "seq", axis=0, tiled=True),
        lax.all_gather(w_value, "seq", axis=0, tiled=True),
    )
    query_acc, key_acc, value_acc = tuple(
        (
            lax.dot_general(
                weight_piece, gathered, (((0,), (1,)), ((), ())), preferred_element_type=jnp.float32
            )
            for weight_piece in pieces
        )
    )
    query_rows = query_acc.astype(jnp.bfloat16)
    key_rows = key_acc.astype(jnp.bfloat16)
    value_rows = value_acc.astype(jnp.bfloat16)
    query_rows, key_rows, value_rows = lax.optimization_barrier((query_rows, key_rows, value_rows))
    product = (key_rows.astype(jnp.float32) * value_rows.astype(jnp.float32)).astype(jnp.bfloat16)
    owned = lax.all_to_all(product, "seq", split_axis=0, concat_axis=1, tiled=True)
    own_chan = owned.shape[0]
    blocks = owned.astype(jnp.float32).reshape(own_chan, -1, BLOCK)
    block_end = local_ends(blocks, decay_rate)
    running = block_sums(block_end, decay_rate, BLOCK)
    entering, new_state = entering_states(running, decay_rate, carried, BLOCK)
    conv_out = (
        block_convolve(blocks, decay_rate, residue, entering)
        .reshape(own_chan, -1)
        .astype(jnp.bfloat16)
    )
    conv_back = lax.all_to_all(conv_out, "seq", split_axis=1, concat_axis=0, tiled=True)
    conv_back = lax.optimization_barrier(conv_back)
    gated_rows = (query_rows.astype(jnp.float32) * conv_back.astype(jnp.float32)).astype(
        jnp.bfloat16
    )
    return (gated_rows.T, new_state)


PIECES = 4
EARLY = 2


def layer_kernel(count, tokens_ref, query_ref, key_ref, value_ref, rate_hbm, scale_hbm, residue_hbm,
                 carried_hbm, out_ref, state_ref,
                 all_ref, weights_ref, query_rows, signal, conv, gated_ref, ends, entering,
                 rate_ref, scale_ref, residue_ref, carried_ref,
                 fill_sem, hop_send, hop_recv, side_send, side_recv, core_send, core_recv,
                 part_send, part_recv, layer_send, layer_recv, out_send, out_recv, own_sem):
    part, seq, chan, rep = (lax.axis_index(a) for a in ("parts", "seq", "chan", "rep"))
    rows, columns = tokens_ref.shape
    depth, outer = query_ref.shape
    width = outer // count
    half = depth // 2
    piece = rows // PIECES
    modes = rate_ref.shape[0]
    own_columns = pl.ds(pl.multiple_of(seq * width, width), width)
    matrices = (query_ref, key_ref, value_ref)

    barrier = pltpu.get_barrier_semaphore()
    mates = ({"parts": 1 - part}, {"chan": 1 - chan}, {"rep": 1 - rep})
    for mate in mates:
        pl.semaphore_signal(barrier, inc=1, device_id=mate, device_id_type=MESH)
    for step in range(1, count):
        pl.semaphore_signal(
            barrier, inc=1, device_id={"seq": lax.rem(seq + step, count)}, device_id_type=MESH
        )

    fills = [
        pltpu.make_async_copy(
            tokens_ref,
            all_ref.at[pl.ds(pl.multiple_of(seq * rows, rows), rows),
                       pl.ds(pl.multiple_of((chan * 2 + rep) * columns, columns), columns)],
            fill_sem.at[0])
    ] + [
        pltpu.make_async_copy(
            matrices[m].at[:, own_columns],
            weights_ref.at[pl.ds(pl.multiple_of(seq * depth, depth), depth), pl.ds(m * width, width)],
            fill_sem.at[1 + m])
        for m in range(3)
    ] + [
        pltpu.make_async_copy(source, target, fill_sem.at[4 + n])
        for n, (source, target) in enumerate((
            (rate_hbm, rate_ref), (scale_hbm, scale_ref),
            (residue_hbm, residue_ref), (carried_hbm, carried_ref),
        ))
    ]

    def remote(source, target, send, recv, device):
        return pltpu.make_async_remote_copy(
            src_ref=source, dst_ref=target, send_sem=send, recv_sem=recv,
            device_id=device, device_id_type=MESH,
        )

    def token_block(block, side, core, p):
        top = pl.multiple_of(block * rows + p * piece, piece)
        left = pl.multiple_of((side * 2 + core) * columns, columns)
        return all_ref.at[pl.ds(top, piece), pl.ds(left, columns)]

    def own_piece(p):
        return tokens_ref.at[pl.ds(p * piece, piece), :]

    def hop(block, p, way, source=None):
        here = token_block(block, chan, rep, p)
        return remote(here if source is None else source, here,
                      hop_send.at[block, p, (1 - way) // 2], hop_recv.at[block, p], {"seq": seq + way})

    def side(block, p, source=None):
        here = token_block(block, chan, rep, p)
        return remote(here if source is None else source, here,
                      side_send.at[block, p], side_recv.at[block, p], {"chan": 1 - chan})

    def side_arrival(block, p):
        there = token_block(block, 1 - chan, rep, p)
        return remote(there, there, side_send.at[block, p], side_recv.at[block, p], {"chan": 1 - chan})

    def core(block, which, p, source=None):
        here = token_block(block, chan if which == 0 else 1 - chan, rep, p)
        return remote(here if source is None else source, here,
                      core_send.at[block, which, p], core_recv.at[block, which, p], {"rep": 1 - rep})

    def core_arrival(block, which, p):
        there = token_block(block, chan if which == 0 else 1 - chan, 1 - rep, p)
        return remote(there, there,
                      core_send.at[block, which, p], core_recv.at[block, which, p], {"rep": 1 - rep})

    def weight_block(block, m, part_of):
        top = pl.multiple_of(block * depth + part_of * half, half)
        return weights_ref.at[pl.ds(top, half), pl.ds(m * width, width)]

    def spread(target, m):
        source = matrices[m].at[
            pl.ds(pl.multiple_of(part * half, half), half),
            pl.ds(pl.multiple_of(target * width, width), width),
        ]
        return remote(source, weight_block(seq, m, part),
                      layer_send.at[target, m], layer_recv.at[seq, m], {"seq": target})

    def spread_arrival(block, m):
        here = weight_block(block, m, part)
        return remote(here, here, layer_send.at[block, m], layer_recv.at[block, m], {"seq": block})

    def swap(block, m):
        here = weight_block(block, m, part)
        return remote(here, here, part_send.at[block, m], part_recv.at[block, m], {"parts": 1 - part})

    def swap_arrival(block, m):
        there = weight_block(block, m, 1 - part)
        return remote(there, there, part_send.at[block, m], part_recv.at[block, m], {"parts": 1 - part})

    def result_rows(p):
        return pl.ds(pl.multiple_of(p * piece, piece), piece)

    def result_columns(source):
        return pl.ds(pl.multiple_of(source * width, width), width)

    def gated_rows(block, p):
        return gated_ref.at[pl.ds(pl.multiple_of(block * rows + p * piece, piece), piece), :]

    def give(block, p):
        return remote(gated_rows(block, p), out_ref.at[result_rows(p), result_columns(seq)],
                      out_send.at[block, p], out_recv.at[seq, p], {"seq": block})

    def take(source, p):
        here = out_ref.at[result_rows(p), result_columns(source)]
        return remote(here, here, out_send.at[source, p], out_recv.at[source, p], {"seq": source})

    def keep(p):
        return pltpu.make_async_copy(
            gated_rows(seq, p), out_ref.at[result_rows(p), result_columns(seq)], own_sem.at[p]
        )

    def inside(other):
        return (other >= 0) & (other < count)

    left_total = seq * PIECES
    right_total = (count - 1 - seq) * PIECES

    for fill in fills:
        fill.start()
    pl.semaphore_wait(barrier, count - 1 + len(mates))

    inward = 1 - 2 * ((2 * seq) // count)
    for distance in range(count - 1, 0, -1):
        for other in (seq + inward * distance, seq - inward * distance):
            @pl.when(inside(other))
            def _():
                for m in range(3):
                    spread(other, m).start()
    for p in range(PIECES):
        @pl.when(seq > 0)
        def _():
            hop(seq, p, -1, own_piece(p)).start()

        if p >= PIECES - EARLY:
            @pl.when(seq + 1 < count)
            def _():
                hop(seq, p, 1, own_piece(p)).start()
        else:
            @pl.when(seq == 0)
            def _():
                hop(seq, p, 1, own_piece(p)).start()
        side(seq, p, own_piece(p)).start()
        core(seq, 0, p, own_piece(p)).start()
    for p in range(PIECES):
        side_arrival(seq, p).wait_recv()
        core(seq, 1, p).start()
    for distance in range(1, count):
        for m in range(3):
            for other in (seq - distance, seq + distance):
                @pl.when(inside(other))
                def _():
                    spread_arrival(other, m).wait_recv()
                    swap(other, m).start()
    for fill in fills:
        fill.wait()

    lane_groups = width // LANES
    chunk = piece // CHUNKS

    def project(block, p):
        for which in range(2):
            core_arrival(block, which, p).wait_recv()
        top = pl.ds(pl.multiple_of(block * rows + p * piece, piece), piece)
        found = jnp.dot(all_ref[top, :], weights_ref[...], preferred_element_type=jnp.float32)
        found = found.astype(jnp.bfloat16)
        query_rows[top, :] = found[:, :width]
        product = (
            found[:, width : 2 * width].astype(jnp.float32) * found[:, 2 * width :].astype(jnp.float32)
        )
        product = product.astype(jnp.bfloat16).astype(jnp.float32)
        for group in range(lane_groups):
            signal[group, top, :] = product[:, group * LANES : (group + 1) * LANES]

    def scan(g, _):
        block, p = g // PIECES, lax.rem(g, PIECES)
        top = pl.multiple_of(g * piece, piece)
        for group in range(lane_groups):
            lanes = pl.ds(group * LANES, LANES)
            rates = rate_ref[:, lanes]
            residues = residue_ref[:, lanes]
            scale = scale_ref[:, lanes]
            decay = jnp.exp(-rates)
            weight = residues * scale
            chunk_decay = jnp.exp(-rates * chunk)

            def rows_of(array):
                return [jnp.broadcast_to(array[m : m + 1, :], (CHUNKS, LANES)) for m in range(modes)]

            decays = rows_of(decay)
            weights = rows_of(weight)

            def sums(step, states):
                here = signal[group, pl.ds(top + step, CHUNKS, stride=chunk), :]
                return tuple(d * s + here for d, s in zip(decays, states))

            zero = jnp.zeros((CHUNKS, LANES), jnp.float32)
            finals = lax.fori_loop(0, chunk, sums, (zero,) * modes, unroll=4)
            for m in range(modes):
                ends[m] = finals[m]
            state = carried_ref[:, lanes]
            for c in range(CHUNKS):
                entering[:, c, :] = residues * state
                state = chunk_decay * state + scale * ends[:, c, :]
            carried_ref[:, lanes] = state

            def outputs(step, states):
                here = signal[group, pl.ds(top + step, CHUNKS, stride=chunk), :]
                states = tuple(d * s + w * here for d, s, w in zip(decays, states, weights))
                terms = list(states)
                while len(terms) > 1:
                    terms = [a + b for a, b in zip(terms[::2], terms[1::2])] + (
                        [terms[-1]] if len(terms) % 2 else []
                    )
                conv[group, pl.ds(step, CHUNKS, stride=chunk), :] = terms[0]
                return states

            starts = tuple(entering[m] for m in range(modes))
            lax.fori_loop(0, chunk, outputs, starts, unroll=4)
            rounded = conv[group].astype(jnp.bfloat16).astype(jnp.float32)
            gated_ref[pl.ds(top, piece), lanes] = (
                query_rows[pl.ds(top, piece), lanes].astype(jnp.float32) * rounded
            ).astype(jnp.bfloat16)

        @pl.when(block == seq)
        def _():
            keep(p).start()

        @pl.when(block != seq)
        def _():
            give(block, p).start()

        return 0

    def left_of(i):
        return i // PIECES, lax.rem(i, PIECES)

    def right_of(i):
        return seq + 1 + i // PIECES, lax.rem(i, PIECES)

    def scanned(n):
        reach = jnp.maximum(seq, 1) * PIECES
        whole = jnp.minimum((seq + 1) * PIECES + n, count * PIECES)
        return jnp.where(n < reach, n, whole)

    def slot(k, _):
        @pl.when(k < left_total)
        def _():
            block, p = left_of(k)
            hop(block, p, 1).wait_recv()

            @pl.when(seq + 1 < count)
            def _():
                hop(block, p, 1).start()

            side(block, p).start()
            core(block, 0, p).start()

            @pl.when((k == left_total - 1) & (seq + 1 < count))
            def _():
                for q in range(PIECES - EARLY):
                    hop(seq, q, 1, own_piece(q)).start()

        @pl.when(k < right_total)
        def _():
            block, p = right_of(k)
            hop(block, p, -1).wait_recv()

            @pl.when(seq > 0)
            def _():
                hop(block, p, -1).start()

            side(block, p).start()
            core(block, 0, p).start()

        before = k - 1

        @pl.when((before >= 0) & (before < left_total))
        def _():
            block, p = left_of(before)
            side_arrival(block, p).wait_recv()
            core(block, 1, p).start()

        @pl.when((before >= 0) & (before < right_total))
        def _():
            block, p = right_of(before)
            side_arrival(block, p).wait_recv()
            core(block, 1, p).start()

        @pl.when(k == 2)
        def _():
            for distance in range(1, count):
                for other in (seq - distance, seq + distance):
                    @pl.when(inside(other))
                    def _():
                        for m in range(3):
                            swap_arrival(other, m).wait_recv()

        @pl.when(k >= 2)
        def _():
            n = k - 2

            def one(which, _):
                block = jnp.where(which == 0, n // PIECES,
                                  jnp.where(which == 1, seq + 1 + n // PIECES, seq))
                limit = jnp.where(which == 0, left_total,
                                  jnp.where(which == 1, right_total, PIECES))

                @pl.when(n < limit)
                def _():
                    project(block, lax.rem(n, PIECES))

                return 0

            lax.fori_loop(0, 3, one, 0)
            lax.fori_loop(scanned(n), scanned(n + 1), scan, 0)

        return 0

    lax.fori_loop(0, (count - 1) * PIECES + 2, slot, 0)
    state_ref[...] = carried_ref[...]

    for p in range(PIECES):
        keep(p).wait()
        @pl.when(seq > 0)
        def _():
            hop(seq, p, -1, own_piece(p)).wait_send()

        @pl.when(seq + 1 < count)
        def _():
            hop(seq, p, 1, own_piece(p)).wait_send()

        side(seq, p, own_piece(p)).wait_send()
        core(seq, 0, p, own_piece(p)).wait_send()
        core(seq, 1, p).wait_send()
    for distance in range(1, count):
        for other, way in ((seq - distance, 1), (seq + distance, -1)):
            @pl.when(inside(other))
            def _():
                for p in range(PIECES):
                    @pl.when(inside(seq + way))
                    def _():
                        hop(other, p, way).wait_send()

                    side(other, p).wait_send()
                    for which in range(2):
                        core(other, which, p).wait_send()
                    give(other, p).wait_send()
                    take(other, p).wait_recv()
                for m in range(3):
                    spread(other, m).wait_send()
                    swap(other, m).wait_send()


def whole_layer(tokens, w_query, w_key, w_value, rate, residue, carried, count):
    rows, columns = tokens.shape
    depth, outer = w_query.shape
    width, modes = rate.shape
    length = rows * count
    vmem = pl.BlockSpec(memory_space=pltpu.VMEM)
    anywhere = pl.BlockSpec(memory_space=pl.ANY)
    dma = pltpu.SemaphoreType.DMA
    table = pltpu.VMEM((modes, width), jnp.float32)
    gated, state = pl.pallas_call(
        functools.partial(layer_kernel, count),
        out_shape=(
            jax.ShapeDtypeStruct((rows, outer), jnp.bfloat16),
            jax.ShapeDtypeStruct((modes, width), jnp.float32),
        ),
        in_specs=[anywhere] * 8,
        out_specs=(anywhere, vmem),
        scratch_shapes=[
            pltpu.VMEM((length, columns * 4), jnp.bfloat16),
            pltpu.VMEM((depth * count, 3 * width), jnp.bfloat16),
            pltpu.VMEM((length, width), jnp.bfloat16),
            pltpu.VMEM((width // LANES, length, LANES), jnp.float32),
            pltpu.VMEM((width // LANES, rows // PIECES, LANES), jnp.float32),
            pltpu.VMEM((length, width), jnp.bfloat16),
            pltpu.VMEM((modes, CHUNKS, LANES), jnp.float32),
            pltpu.VMEM((modes, CHUNKS, LANES), jnp.float32),
        ] + [table] * 4 + [
            dma((8,)),
            dma((count, PIECES, 2)), dma((count, PIECES)),
            dma((count, PIECES)), dma((count, PIECES)),
            dma((count, 2, PIECES)), dma((count, 2, PIECES)),
            dma((count, 3)), dma((count, 3)),
            dma((count, 3)), dma((count, 3)),
            dma((count, PIECES)), dma((count, PIECES)),
            dma((PIECES,)),
        ],
        compiler_params=pltpu.CompilerParams(
            collective_id=0, has_side_effects=True, vmem_limit_bytes=60 * 2**20
        ),
    )(tokens, w_query, w_key, w_value, rate.T, mode_scale(rate).T, residue.T, carried.T)
    return gated, state.T


def per_device_channels(tokens, w_query, w_key, w_value, decay_rate, residue, carried):
    count = lax.axis_size("seq")
    return whole_layer(tokens, w_query, w_key, w_value, decay_rate, residue, carried, count)


def solution(mesh):
    in_specs = (
        P(("parts", "seq"), ("chan", "rep")),
        P("seq", ("chan", "rep")),
        P("seq", ("chan", "rep")),
        P("seq", ("chan", "rep")),
        P(("chan", "rep", "seq"), None),
        P(("chan", "rep", "seq"), None),
        P(("parts", "chan", "rep", "seq"), None),
    )
    out_specs = (P(("parts", "seq"), ("chan", "rep")), P(("parts", "chan", "rep", "seq"), None))

    def body(*arrays):
        own_channels = arrays[4].shape[0]
        mates = all(mesh.shape[a] == 2 for a in ("parts", "chan", "rep"))
        chosen = per_device_channels if own_channels % LANES == 0 and mates else per_device
        return chosen(*arrays)

    return jax.shard_map(body, mesh=mesh, in_specs=in_specs, out_specs=out_specs, check_vma=False)
```

```python
import functools

import jax
import jax.numpy as jnp
from jax import lax
from jax.experimental import pallas as pl
from jax.experimental.pallas import tpu as pltpu
from jax.sharding import PartitionSpec as P

BLOCK = 128
LANES = 128
CHUNKS = 8
MESH = pl.DeviceIdType.MESH


HIGHEST_PRECISION = lax.Precision.HIGHEST


def mode_scale(decay_rates):
    return jnp.sqrt(-jnp.expm1(-2.0 * decay_rates))


def local_ends(blocks, decay_rates):
    block_width = blocks.shape[2]
    offsets = jnp.arange(block_width, dtype=jnp.float32)
    tail_powers = jnp.exp(-decay_rates[:, :, None] * (block_width - 1.0 - offsets)[None, None, :])
    sums_here = jnp.einsum("cnb,cmb->cnm", blocks, tail_powers, precision=HIGHEST_PRECISION)
    return mode_scale(decay_rates)[:, None, :] * sums_here


def combine_states(earlier, later):
    return (earlier[0] * later[0], later[0] * earlier[1] + later[1])


def block_sums(block_ends, decay_rates, block_width):
    step_decay = jnp.broadcast_to(jnp.exp(-decay_rates * block_width)[:, None, :], block_ends.shape)
    unused_decay, running = lax.associative_scan(combine_states, (step_decay, block_ends), axis=1)
    return running


def entering_states(running, decay_rates, start_state, block_width):
    count_blocks = running.shape[1]
    block_starts = jnp.arange(count_blocks, dtype=jnp.float32) * block_width
    decayed = (
        jnp.exp(-decay_rates[:, None, :] * block_starts[None, :, None]) * start_state[:, None, :]
    )
    earlier_sums = jnp.concatenate([jnp.zeros_like(running[:, :1]), running[:, :-1]], axis=1)
    final_state = (
        jnp.exp(-decay_rates * (count_blocks * block_width)) * start_state + running[:, -1]
    )
    return (decayed + earlier_sums, final_state)


def block_convolve(blocks, decay_rates, residues, entering):
    block_width = blocks.shape[2]
    offsets = jnp.arange(block_width, dtype=jnp.float32)
    powers = jnp.exp(-decay_rates[:, :, None] * offsets[None, None, :])
    kernel = jnp.sum((residues * mode_scale(decay_rates))[:, :, None] * powers, axis=1)
    out_index = jnp.arange(block_width, dtype=jnp.int32)[:, None]
    in_index = jnp.arange(block_width, dtype=jnp.int32)[None, :]
    lag = jnp.maximum(out_index - in_index, 0)
    causal = (out_index >= in_index).astype(jnp.float32)
    toeplitz = kernel[:, lag] * causal[None, :, :]
    direct = jnp.einsum("cij,cnj->cni", toeplitz, blocks, precision=HIGHEST_PRECISION)
    leading = residues[:, :, None] * jnp.exp(
        -decay_rates[:, :, None] * (offsets + 1.0)[None, None, :]
    )
    return direct + jnp.einsum("cnm,cmb->cnb", entering, leading, precision=HIGHEST_PRECISION)


def per_device(tokens, w_query, w_key, w_value, decay_rate, residue, carried):
    gathered = lax.all_gather(tokens, ("chan", "rep"), axis=1, tiled=True)
    pieces = (
        lax.all_gather(w_query, "seq", axis=0, tiled=True),
        lax.all_gather(w_key, "seq", axis=0, tiled=True),
        lax.all_gather(w_value, "seq", axis=0, tiled=True),
    )
    query_acc, key_acc, value_acc = tuple(
        (
            lax.dot_general(
                weight_piece, gathered, (((0,), (1,)), ((), ())), preferred_element_type=jnp.float32
            )
            for weight_piece in pieces
        )
    )
    query_rows = query_acc.astype(jnp.bfloat16)
    key_rows = key_acc.astype(jnp.bfloat16)
    value_rows = value_acc.astype(jnp.bfloat16)
    query_rows, key_rows, value_rows = lax.optimization_barrier((query_rows, key_rows, value_rows))
    product = (key_rows.astype(jnp.float32) * value_rows.astype(jnp.float32)).astype(jnp.bfloat16)
    owned = lax.all_to_all(product, "seq", split_axis=0, concat_axis=1, tiled=True)
    own_chan = owned.shape[0]
    blocks = owned.astype(jnp.float32).reshape(own_chan, -1, BLOCK)
    block_end = local_ends(blocks, decay_rate)
    running = block_sums(block_end, decay_rate, BLOCK)
    entering, new_state = entering_states(running, decay_rate, carried, BLOCK)
    conv_out = (
        block_convolve(blocks, decay_rate, residue, entering)
        .reshape(own_chan, -1)
        .astype(jnp.bfloat16)
    )
    conv_back = lax.all_to_all(conv_out, "seq", split_axis=1, concat_axis=0, tiled=True)
    conv_back = lax.optimization_barrier(conv_back)
    gated_rows = (query_rows.astype(jnp.float32) * conv_back.astype(jnp.float32)).astype(
        jnp.bfloat16
    )
    return (gated_rows.T, new_state)


PIECES = 4
SIDE_LAG = 2
LAG = 3
LEFT_HOLD = 1
RIGHT_HOLD = 0


def block_orders(count):
    if count == 4:
        return ((1, 2, 3), (0, 2, 3), (3, 0, 1), (2, 0, 1))
    return tuple(
        tuple(sorted((b for b in range(count) if b != z), key=lambda b: (abs(b - z), b)))
        for z in range(count)
    )


def reach_table(orders):
    count = len(orders)
    last = (count - 1) * PIECES
    table = []
    for z, order in enumerate(orders):
        when = {}
        for p in range(PIECES):
            when[z, p] = when[order[0], p] = PIECES + p
            for n in range(1, count - 1):
                when[order[n], p] = n * PIECES + p + LAG
        row = [0]
        for k in range(PIECES, last + LAG):
            g = row[-1]
            while g < count * PIECES and when[divmod(g, PIECES)] <= k:
                g += 1
            row.append(g)
        table.append(row)
    return table


def layer_kernel(count, tokens_ref, query_ref, key_ref, value_ref, rate_hbm, scale_hbm, residue_hbm,
                 carried_hbm, out_ref, state_ref,
                 all_ref, weights_ref, query_rows, signal, conv, gated_ref, ends, entering,
                 rate_ref, scale_ref, residue_ref, carried_ref,
                 fill_sem, hop_send, hop_recv, side_send, side_recv, core_send, core_recv,
                 part_send, part_recv, layer_send, layer_recv, out_send, out_recv, own_sem):
    part, seq, chan, rep = (lax.axis_index(a) for a in ("parts", "seq", "chan", "rep"))
    rows, columns = tokens_ref.shape
    depth, outer = query_ref.shape
    width = outer // count
    half = depth // 2
    piece = rows // PIECES
    modes = rate_ref.shape[0]
    own_columns = pl.ds(pl.multiple_of(seq * width, width), width)
    matrices = (query_ref, key_ref, value_ref)

    barrier = pltpu.get_barrier_semaphore()
    mates = ({"parts": 1 - part}, {"chan": 1 - chan}, {"rep": 1 - rep})
    for mate in mates:
        pl.semaphore_signal(barrier, inc=1, device_id=mate, device_id_type=MESH)
    for step in range(1, count):
        pl.semaphore_signal(
            barrier, inc=1, device_id={"seq": lax.rem(seq + step, count)}, device_id_type=MESH
        )

    fills = [
        pltpu.make_async_copy(
            tokens_ref,
            all_ref.at[pl.ds(pl.multiple_of(seq * rows, rows), rows),
                       pl.ds(pl.multiple_of((chan * 2 + rep) * columns, columns), columns)],
            fill_sem.at[0])
    ] + [
        pltpu.make_async_copy(
            matrices[m].at[:, own_columns],
            weights_ref.at[pl.ds(pl.multiple_of(seq * depth, depth), depth), pl.ds(m * width, width)],
            fill_sem.at[1 + m])
        for m in range(3)
    ] + [
        pltpu.make_async_copy(source, target, fill_sem.at[4 + n])
        for n, (source, target) in enumerate((
            (rate_hbm, rate_ref), (scale_hbm, scale_ref),
            (residue_hbm, residue_ref), (carried_hbm, carried_ref),
        ))
    ]

    def remote(source, target, send, recv, device):
        return pltpu.make_async_remote_copy(
            src_ref=source, dst_ref=target, send_sem=send, recv_sem=recv,
            device_id=device, device_id_type=MESH,
        )

    def token_block(block, side, core, p):
        top = pl.multiple_of(block * rows + p * piece, piece)
        left = pl.multiple_of((side * 2 + core) * columns, columns)
        return all_ref.at[pl.ds(top, piece), pl.ds(left, columns)]

    def own_piece(p):
        return tokens_ref.at[pl.ds(p * piece, piece), :]

    def hop(block, p, way, source=None):
        here = token_block(block, chan, rep, p)
        return remote(here if source is None else source, here,
                      hop_send.at[block, p, (1 - way) // 2], hop_recv.at[block, p], {"seq": seq + way})

    def side(block, p, source=None):
        here = token_block(block, chan, rep, p)
        return remote(here if source is None else source, here,
                      side_send.at[block, p], side_recv.at[block, p], {"chan": 1 - chan})

    def side_arrival(block, p):
        there = token_block(block, 1 - chan, rep, p)
        return remote(there, there, side_send.at[block, p], side_recv.at[block, p], {"chan": 1 - chan})

    def core(block, which, p, source=None):
        here = token_block(block, chan if which == 0 else 1 - chan, rep, p)
        return remote(here if source is None else source, here,
                      core_send.at[block, which, p], core_recv.at[block, which, p], {"rep": 1 - rep})

    def core_arrival(block, which, p):
        there = token_block(block, chan if which == 0 else 1 - chan, 1 - rep, p)
        return remote(there, there,
                      core_send.at[block, which, p], core_recv.at[block, which, p], {"rep": 1 - rep})

    def weight_block(block, m, part_of):
        top = pl.multiple_of(block * depth + part_of * half, half)
        return weights_ref.at[pl.ds(top, half), pl.ds(m * width, width)]

    def spread(target, m):
        source = matrices[m].at[
            pl.ds(pl.multiple_of(part * half, half), half),
            pl.ds(pl.multiple_of(target * width, width), width),
        ]
        return remote(source, weight_block(seq, m, part),
                      layer_send.at[target, m], layer_recv.at[seq, m], {"seq": target})

    def spread_arrival(block, m):
        here = weight_block(block, m, part)
        return remote(here, here, layer_send.at[block, m], layer_recv.at[block, m], {"seq": block})

    def swap(block, m):
        here = weight_block(block, m, part)
        return remote(here, here, part_send.at[block, m], part_recv.at[block, m], {"parts": 1 - part})

    def swap_arrival(block, m):
        there = weight_block(block, m, 1 - part)
        return remote(there, there, part_send.at[block, m], part_recv.at[block, m], {"parts": 1 - part})

    def result_rows(p):
        return pl.ds(pl.multiple_of(p * piece, piece), piece)

    def result_columns(source):
        return pl.ds(pl.multiple_of(source * width, width), width)

    def gated_rows(block, p):
        return gated_ref.at[pl.ds(pl.multiple_of(block * rows + p * piece, piece), piece), :]

    def give(block, p):
        return remote(gated_rows(block, p), out_ref.at[result_rows(p), result_columns(seq)],
                      out_send.at[block, p], out_recv.at[seq, p], {"seq": block})

    def take(source, p):
        here = out_ref.at[result_rows(p), result_columns(source)]
        return remote(here, here, out_send.at[source, p], out_recv.at[source, p], {"seq": source})

    def keep(p):
        return pltpu.make_async_copy(
            gated_rows(seq, p), out_ref.at[result_rows(p), result_columns(seq)], own_sem.at[p]
        )

    def inside(other):
        return (other >= 0) & (other < count)

    def pick(values, index):
        found = values[0]
        for n in range(1, len(values)):
            found = jnp.where(index == n, values[n], found)
        return found

    def by_plane(table, index):
        flat = [value for row in table for value in row]
        return pick(flat, seq * len(table[0]) + index)

    orders = block_orders(count)
    ready = reach_table(orders)
    is_first, is_last = seq == 0, seq == count - 1
    is_end = is_first | is_last
    deferred = (seq == 1) if count == 4 else (seq == count)

    for fill in fills:
        fill.start()
    pl.semaphore_wait(barrier, count - 1 + len(mates))

    def send_weights(way, distances):
        for distance in distances:
            other = seq + way * distance

            @pl.when(inside(other))
            def _():
                for m in range(3):
                    spread(other, m).start()

    def send_own(way):
        for p in range(PIECES):
            hop(seq, p, way, own_piece(p)).start()

    for p in range(PIECES):
        side(seq, p, own_piece(p)).start()
        core(seq, 0, p, own_piece(p)).start()
    for way in (1, -1):
        @pl.when(inside(seq + way))
        def _():
            send_weights(way, range(count - 1, 0, -1))
            if way == 1:
                @pl.when(jnp.logical_not(deferred))
                def _():
                    send_own(way)
            else:
                send_own(way)

    def relay(block, p):
        way = jnp.where(block < seq, 1, -1)
        hop(block, p, way).wait_recv()

        @pl.when(inside(seq + way))
        def _():
            hop(block, p, way).start()

        side(block, p).start()
        core(block, 0, p).start()

    def pass_side(block, p):
        side_arrival(block, p).wait_recv()
        core(block, 1, p).start()

    def pass_weights(other, m):
        @pl.when(inside(other))
        def _():
            spread_arrival(other, m).wait_recv()
            swap(other, m).start()

    toward = jnp.where(2 * seq < count, -1, 1)
    first_block = by_plane(orders, 0)

    @pl.when(is_end)
    def _():
        for m in range(3):
            pass_side(seq, m)
            pass_weights(seq - toward * (count - 1), m)
        for p in range(3, PIECES):
            pass_side(seq, p)
        for distance in range(1, count - 1):
            for m in range(3):
                pass_weights(seq - toward * distance, m)
        for p in range(PIECES):
            relay(first_block, p)

    @pl.when(jnp.logical_not(is_end))
    def _():
        for p in range(PIECES):
            pass_side(seq, p)
        for distance in range(count - 2, 1, -1):
            for m in range(3):
                pass_weights(seq - toward * distance, m)
        for distance in range(count - 2, 0, -1):
            for m in range(3):
                pass_weights(seq + toward * distance, m)
        for p in range(PIECES):
            relay(first_block, p)
            if p < 3:
                pass_weights(seq - toward, p)

        @pl.when(deferred)
        def _():
            send_own(1)

    for p in range(PIECES - SIDE_LAG):
        pass_side(first_block, p)
    for fill in fills:
        fill.wait()

    lane_groups = width // LANES
    chunk = piece // CHUNKS

    def project(block, p):
        for which in range(2):
            core_arrival(block, which, p).wait_recv()
        top = pl.ds(pl.multiple_of(block * rows + p * piece, piece), piece)
        found = jnp.dot(all_ref[top, :], weights_ref[...], preferred_element_type=jnp.float32)
        found = found.astype(jnp.bfloat16)
        query_rows[top, :] = found[:, :width]
        product = (
            found[:, width : 2 * width].astype(jnp.float32) * found[:, 2 * width :].astype(jnp.float32)
        )
        product = product.astype(jnp.bfloat16).astype(jnp.float32)
        for group in range(lane_groups):
            signal[group, top, :] = product[:, group * LANES : (group + 1) * LANES]

    def scan(g, _):
        block, p = g // PIECES, lax.rem(g, PIECES)
        top = pl.multiple_of(g * piece, piece)
        for group in range(lane_groups):
            lanes = pl.ds(group * LANES, LANES)
            rates = rate_ref[:, lanes]
            residues = residue_ref[:, lanes]
            scale = scale_ref[:, lanes]
            decay = jnp.exp(-rates)
            weight = residues * scale
            chunk_decay = jnp.exp(-rates * chunk)

            def rows_of(array):
                return [jnp.broadcast_to(array[m : m + 1, :], (CHUNKS, LANES)) for m in range(modes)]

            decays = rows_of(decay)
            weights = rows_of(weight)

            def sums(step, states):
                here = signal[group, pl.ds(top + step, CHUNKS, stride=chunk), :]
                return tuple(d * s + here for d, s in zip(decays, states))

            zero = jnp.zeros((CHUNKS, LANES), jnp.float32)
            finals = lax.fori_loop(0, chunk, sums, (zero,) * modes, unroll=4)
            for m in range(modes):
                ends[m] = finals[m]
            state = carried_ref[:, lanes]
            for c in range(CHUNKS):
                entering[:, c, :] = residues * state
                state = chunk_decay * state + scale * ends[:, c, :]
            carried_ref[:, lanes] = state

            def outputs(step, states):
                here = signal[group, pl.ds(top + step, CHUNKS, stride=chunk), :]
                states = tuple(d * s + w * here for d, s, w in zip(decays, states, weights))
                terms = list(states)
                while len(terms) > 1:
                    terms = [a + b for a, b in zip(terms[::2], terms[1::2])] + (
                        [terms[-1]] if len(terms) % 2 else []
                    )
                conv[group, pl.ds(step, CHUNKS, stride=chunk), :] = terms[0]
                return states

            starts = tuple(entering[m] for m in range(modes))
            lax.fori_loop(0, chunk, outputs, starts, unroll=4)
            rounded = conv[group].astype(jnp.bfloat16).astype(jnp.float32)
            gated_ref[pl.ds(top, piece), lanes] = (
                query_rows[pl.ds(top, piece), lanes].astype(jnp.float32) * rounded
            ).astype(jnp.bfloat16)

        @pl.when(block == seq)
        def _():
            keep(p).start()

        return 0

    def scan_and_send(g, k):
        scan(g, 0)

        block = g // PIECES

        @pl.when((block != seq) & (k >= release(block)))
        def _():
            give(block, lax.rem(g, PIECES)).start()

        return k

    def release(block):
        later = jnp.where(block < seq, last + LEFT_HOLD, last + RIGHT_HOLD)
        return jnp.where(is_end & ((block == seq - 1) | (block == seq + 1)), 0, later)

    def send_held(g, k):
        block = g // PIECES

        @pl.when((block != seq) & (release(block) == k))
        def _():
            give(block, lax.rem(g, PIECES)).start()

        return k

    last = (count - 1) * PIECES

    def block_of(k):
        return by_plane(orders, k // PIECES)

    def slot(k, _):
        @pl.when(k < last)
        def _():
            relay(block_of(k), lax.rem(k, PIECES))

        @pl.when(k == PIECES)
        def _():
            for distance in range(1, count):
                for other in (seq - distance, seq + distance):
                    @pl.when(inside(other))
                    def _():
                        for m in range(3):
                            swap_arrival(other, m).wait_recv()

        def one(which, _):
            early = which < 2
            n = jnp.where(early, k - PIECES, k - LAG)
            block = jnp.where(which == 0, seq, jnp.where(which == 1, first_block, block_of(k - LAG)))
            known = (early & (n < PIECES)) | (jnp.logical_not(early) & (n >= PIECES))

            @pl.when(known)
            def _():
                project(block, lax.rem(n, PIECES))

            return 0

        lax.fori_loop(0, 3, one, 0)
        done, reach = by_plane(ready, k - PIECES), by_plane(ready, k - PIECES + 1)
        lax.fori_loop(done, reach, scan_and_send, k)

        @pl.when((k == last + LEFT_HOLD) | (k == last + RIGHT_HOLD))
        def _():
            lax.fori_loop(0, done, send_held, k)

        @pl.when(k < last + SIDE_LAG)
        def _():
            pass_side(block_of(k - SIDE_LAG), lax.rem(k - SIDE_LAG, PIECES))

        return 0

    lax.fori_loop(PIECES, last + LAG, slot, 0)
    state_ref[...] = carried_ref[...]

    for p in range(PIECES):
        keep(p).wait()
        @pl.when(seq > 0)
        def _():
            hop(seq, p, -1, own_piece(p)).wait_send()

        @pl.when(seq + 1 < count)
        def _():
            hop(seq, p, 1, own_piece(p)).wait_send()

        side(seq, p, own_piece(p)).wait_send()
        core(seq, 0, p, own_piece(p)).wait_send()
        core(seq, 1, p).wait_send()
    for distance in range(1, count):
        for other, way in ((seq - distance, 1), (seq + distance, -1)):
            @pl.when(inside(other))
            def _():
                for p in range(PIECES):
                    @pl.when(inside(seq + way))
                    def _():
                        hop(other, p, way).wait_send()

                    side(other, p).wait_send()
                    for which in range(2):
                        core(other, which, p).wait_send()
                    give(other, p).wait_send()
                    take(other, p).wait_recv()
                for m in range(3):
                    spread(other, m).wait_send()
                    swap(other, m).wait_send()


def whole_layer(tokens, w_query, w_key, w_value, rate, residue, carried, count):
    rows, columns = tokens.shape
    depth, outer = w_query.shape
    width, modes = rate.shape
    length = rows * count
    vmem = pl.BlockSpec(memory_space=pltpu.VMEM)
    anywhere = pl.BlockSpec(memory_space=pl.ANY)
    dma = pltpu.SemaphoreType.DMA
    table = pltpu.VMEM((modes, width), jnp.float32)
    gated, state = pl.pallas_call(
        functools.partial(layer_kernel, count),
        out_shape=(
            jax.ShapeDtypeStruct((rows, outer), jnp.bfloat16),
            jax.ShapeDtypeStruct((modes, width), jnp.float32),
        ),
        in_specs=[anywhere] * 8,
        out_specs=(anywhere, vmem),
        scratch_shapes=[
            pltpu.VMEM((length, columns * 4), jnp.bfloat16),
            pltpu.VMEM((depth * count, 3 * width), jnp.bfloat16),
            pltpu.VMEM((length, width), jnp.bfloat16),
            pltpu.VMEM((width // LANES, length, LANES), jnp.float32),
            pltpu.VMEM((width // LANES, rows // PIECES, LANES), jnp.float32),
            pltpu.VMEM((length, width), jnp.bfloat16),
            pltpu.VMEM((modes, CHUNKS, LANES), jnp.float32),
            pltpu.VMEM((modes, CHUNKS, LANES), jnp.float32),
        ] + [table] * 4 + [
            dma((8,)),
            dma((count, PIECES, 2)), dma((count, PIECES)),
            dma((count, PIECES)), dma((count, PIECES)),
            dma((count, 2, PIECES)), dma((count, 2, PIECES)),
            dma((count, 3)), dma((count, 3)),
            dma((count, 3)), dma((count, 3)),
            dma((count, PIECES)), dma((count, PIECES)),
            dma((PIECES,)),
        ],
        compiler_params=pltpu.CompilerParams(
            collective_id=0, has_side_effects=True, vmem_limit_bytes=60 * 2**20
        ),
    )(tokens, w_query, w_key, w_value, rate.T, mode_scale(rate).T, residue.T, carried.T)
    return gated, state.T


def per_device_channels(tokens, w_query, w_key, w_value, decay_rate, residue, carried):
    count = lax.axis_size("seq")
    return whole_layer(tokens, w_query, w_key, w_value, decay_rate, residue, carried, count)


def solution(mesh):
    in_specs = (
        P(("parts", "seq"), ("chan", "rep")),
        P("seq", ("chan", "rep")),
        P("seq", ("chan", "rep")),
        P("seq", ("chan", "rep")),
        P(("chan", "rep", "seq"), None),
        P(("chan", "rep", "seq"), None),
        P(("parts", "chan", "rep", "seq"), None),
    )
    out_specs = (P(("parts", "seq"), ("chan", "rep")), P(("parts", "chan", "rep", "seq"), None))

    def body(*arrays):
        own_channels = arrays[4].shape[0]
        mates = all(mesh.shape[a] == 2 for a in ("parts", "chan", "rep"))
        chosen = per_device_channels if own_channels % LANES == 0 and mates else per_device
        return chosen(*arrays)

    return jax.shard_map(body, mesh=mesh, in_specs=in_specs, out_specs=out_specs, check_vma=False)
```

```python
import functools

import jax
import jax.numpy as jnp
from jax import lax
from jax.experimental import pallas as pl
from jax.experimental.pallas import tpu as pltpu
from jax.sharding import PartitionSpec as P

BLOCK = 128
LANES = 128
CHUNKS = 8
MESH = pl.DeviceIdType.MESH


HIGHEST_PRECISION = lax.Precision.HIGHEST


def mode_scale(decay_rates):
    return jnp.sqrt(-jnp.expm1(-2.0 * decay_rates))


def local_ends(blocks, decay_rates):
    block_width = blocks.shape[2]
    offsets = jnp.arange(block_width, dtype=jnp.float32)
    tail_powers = jnp.exp(-decay_rates[:, :, None] * (block_width - 1.0 - offsets)[None, None, :])
    sums_here = jnp.einsum("cnb,cmb->cnm", blocks, tail_powers, precision=HIGHEST_PRECISION)
    return mode_scale(decay_rates)[:, None, :] * sums_here


def combine_states(earlier, later):
    return (earlier[0] * later[0], later[0] * earlier[1] + later[1])


def block_sums(block_ends, decay_rates, block_width):
    step_decay = jnp.broadcast_to(jnp.exp(-decay_rates * block_width)[:, None, :], block_ends.shape)
    unused_decay, running = lax.associative_scan(combine_states, (step_decay, block_ends), axis=1)
    return running


def entering_states(running, decay_rates, start_state, block_width):
    count_blocks = running.shape[1]
    block_starts = jnp.arange(count_blocks, dtype=jnp.float32) * block_width
    decayed = (
        jnp.exp(-decay_rates[:, None, :] * block_starts[None, :, None]) * start_state[:, None, :]
    )
    earlier_sums = jnp.concatenate([jnp.zeros_like(running[:, :1]), running[:, :-1]], axis=1)
    final_state = (
        jnp.exp(-decay_rates * (count_blocks * block_width)) * start_state + running[:, -1]
    )
    return (decayed + earlier_sums, final_state)


def block_convolve(blocks, decay_rates, residues, entering):
    block_width = blocks.shape[2]
    offsets = jnp.arange(block_width, dtype=jnp.float32)
    powers = jnp.exp(-decay_rates[:, :, None] * offsets[None, None, :])
    kernel = jnp.sum((residues * mode_scale(decay_rates))[:, :, None] * powers, axis=1)
    out_index = jnp.arange(block_width, dtype=jnp.int32)[:, None]
    in_index = jnp.arange(block_width, dtype=jnp.int32)[None, :]
    lag = jnp.maximum(out_index - in_index, 0)
    causal = (out_index >= in_index).astype(jnp.float32)
    toeplitz = kernel[:, lag] * causal[None, :, :]
    direct = jnp.einsum("cij,cnj->cni", toeplitz, blocks, precision=HIGHEST_PRECISION)
    leading = residues[:, :, None] * jnp.exp(
        -decay_rates[:, :, None] * (offsets + 1.0)[None, None, :]
    )
    return direct + jnp.einsum("cnm,cmb->cnb", entering, leading, precision=HIGHEST_PRECISION)


def per_device(tokens, w_query, w_key, w_value, decay_rate, residue, carried):
    gathered = lax.all_gather(tokens, ("chan", "rep"), axis=1, tiled=True)
    pieces = (
        lax.all_gather(w_query, "seq", axis=0, tiled=True),
        lax.all_gather(w_key, "seq", axis=0, tiled=True),
        lax.all_gather(w_value, "seq", axis=0, tiled=True),
    )
    query_acc, key_acc, value_acc = tuple(
        (
            lax.dot_general(
                weight_piece, gathered, (((0,), (1,)), ((), ())), preferred_element_type=jnp.float32
            )
            for weight_piece in pieces
        )
    )
    query_rows = query_acc.astype(jnp.bfloat16)
    key_rows = key_acc.astype(jnp.bfloat16)
    value_rows = value_acc.astype(jnp.bfloat16)
    query_rows, key_rows, value_rows = lax.optimization_barrier((query_rows, key_rows, value_rows))
    product = (key_rows.astype(jnp.float32) * value_rows.astype(jnp.float32)).astype(jnp.bfloat16)
    owned = lax.all_to_all(product, "seq", split_axis=0, concat_axis=1, tiled=True)
    own_chan = owned.shape[0]
    blocks = owned.astype(jnp.float32).reshape(own_chan, -1, BLOCK)
    block_end = local_ends(blocks, decay_rate)
    running = block_sums(block_end, decay_rate, BLOCK)
    entering, new_state = entering_states(running, decay_rate, carried, BLOCK)
    conv_out = (
        block_convolve(blocks, decay_rate, residue, entering)
        .reshape(own_chan, -1)
        .astype(jnp.bfloat16)
    )
    conv_back = lax.all_to_all(conv_out, "seq", split_axis=1, concat_axis=0, tiled=True)
    conv_back = lax.optimization_barrier(conv_back)
    gated_rows = (query_rows.astype(jnp.float32) * conv_back.astype(jnp.float32)).astype(
        jnp.bfloat16
    )
    return (gated_rows.T, new_state)


PIECES = 4
SIDE_LAG = 2
LAG = 3
CAP = 2


def block_orders(count):
    if count == 4:
        return ((1, 2, 3), (0, 2, 3), (3, 0, 1), (2, 0, 1))
    return tuple(
        tuple(sorted((b for b in range(count) if b != z), key=lambda b: (abs(b - z), b)))
        for z in range(count)
    )


def one_less_exp(x):
    series = jnp.ones_like(x)
    for n in range(9, 1, -1):
        series = 1.0 - series * x * (1.0 / n)
    return jnp.where(x < 0.25, x * series, 1.0 - jnp.exp(-x))


def release_table(count):
    if count != 4:
        return ((0,) * count,) * count
    last = (count - 1) * PIECES
    return (
        (0, 0, last - 2, 0),
        (last, 0, 0, last),
        (last, 0, 0, last),
        (last - 1, 0, 0, 0),
    )


def reach_table(orders):
    count = len(orders)
    last = (count - 1) * PIECES
    table = []
    for z, order in enumerate(orders):
        when = {}
        for p in range(PIECES):
            when[z, p] = when[order[0], p] = PIECES + p
            for n in range(1, count - 1):
                when[order[n], p] = n * PIECES + p + LAG
        row = [0]
        for k in range(PIECES, last + LAG):
            g = row[-1]
            top = g + CAP if k < last else count * PIECES
            while g < min(top, count * PIECES) and when[divmod(g, PIECES)] <= k:
                g += 1
            row.append(g)
        table.append(row)
    return table


def layer_kernel(count, tokens_ref, query_ref, key_ref, value_ref, rate_hbm, residue_hbm,
                 carried_hbm, out_ref, state_ref,
                 all_ref, weights_ref, query_rows, signal, conv, gated_ref, ends, entering,
                 rate_ref, scale_ref, residue_ref, carried_ref,
                 fill_sem, hop_send, hop_recv, side_send, side_recv, core_send, core_recv,
                 part_send, part_recv, layer_send, layer_recv, out_send, out_recv, own_sem):
    part, seq, chan, rep = (lax.axis_index(a) for a in ("parts", "seq", "chan", "rep"))
    rows, columns = tokens_ref.shape
    depth, outer = query_ref.shape
    width = outer // count
    half = depth // 2
    piece = rows // PIECES
    modes = rate_ref.shape[0]
    own_columns = pl.ds(pl.multiple_of(seq * width, width), width)
    matrices = (query_ref, key_ref, value_ref)

    barrier = pltpu.get_barrier_semaphore()
    mates = ({"parts": 1 - part}, {"chan": 1 - chan}, {"rep": 1 - rep})
    for mate in mates:
        pl.semaphore_signal(barrier, inc=1, device_id=mate, device_id_type=MESH)
    for step in range(1, count):
        pl.semaphore_signal(
            barrier, inc=1, device_id={"seq": lax.rem(seq + step, count)}, device_id_type=MESH
        )

    fills = [
        pltpu.make_async_copy(
            tokens_ref,
            all_ref.at[pl.ds(pl.multiple_of(seq * rows, rows), rows),
                       pl.ds(pl.multiple_of((chan * 2 + rep) * columns, columns), columns)],
            fill_sem.at[0])
    ] + [
        pltpu.make_async_copy(
            matrices[m].at[:, own_columns],
            weights_ref.at[pl.ds(pl.multiple_of(seq * depth, depth), depth), pl.ds(m * width, width)],
            fill_sem.at[1 + m])
        for m in range(3)
    ] + [
        pltpu.make_async_copy(source, target, fill_sem.at[4 + n])
        for n, (source, target) in enumerate((
            (rate_hbm, rate_ref), (residue_hbm, residue_ref), (carried_hbm, carried_ref),
        ))
    ]

    def remote(source, target, send, recv, device):
        return pltpu.make_async_remote_copy(
            src_ref=source, dst_ref=target, send_sem=send, recv_sem=recv,
            device_id=device, device_id_type=MESH,
        )

    def token_block(block, side, core, p):
        top = pl.multiple_of(block * rows + p * piece, piece)
        left = pl.multiple_of((side * 2 + core) * columns, columns)
        return all_ref.at[pl.ds(top, piece), pl.ds(left, columns)]

    def own_piece(p):
        return tokens_ref.at[pl.ds(p * piece, piece), :]

    def hop(block, p, way, source=None):
        here = token_block(block, chan, rep, p)
        return remote(here if source is None else source, here,
                      hop_send.at[block, p, (1 - way) // 2], hop_recv.at[block, p], {"seq": seq + way})

    def side(block, p, source=None):
        here = token_block(block, chan, rep, p)
        return remote(here if source is None else source, here,
                      side_send.at[block, p], side_recv.at[block, p], {"chan": 1 - chan})

    def side_arrival(block, p):
        there = token_block(block, 1 - chan, rep, p)
        return remote(there, there, side_send.at[block, p], side_recv.at[block, p], {"chan": 1 - chan})

    def core(block, which, p, source=None):
        here = token_block(block, chan if which == 0 else 1 - chan, rep, p)
        return remote(here if source is None else source, here,
                      core_send.at[block, which, p], core_recv.at[block, which, p], {"rep": 1 - rep})

    def core_arrival(block, which, p):
        there = token_block(block, chan if which == 0 else 1 - chan, 1 - rep, p)
        return remote(there, there,
                      core_send.at[block, which, p], core_recv.at[block, which, p], {"rep": 1 - rep})

    def weight_block(block, m, part_of):
        top = pl.multiple_of(block * depth + part_of * half, half)
        return weights_ref.at[pl.ds(top, half), pl.ds(m * width, width)]

    def spread(target, m):
        source = matrices[m].at[
            pl.ds(pl.multiple_of(part * half, half), half),
            pl.ds(pl.multiple_of(target * width, width), width),
        ]
        return remote(source, weight_block(seq, m, part),
                      layer_send.at[target, m], layer_recv.at[seq, m], {"seq": target})

    def spread_arrival(block, m):
        here = weight_block(block, m, part)
        return remote(here, here, layer_send.at[block, m], layer_recv.at[block, m], {"seq": block})

    def swap(block, m):
        here = weight_block(block, m, part)
        return remote(here, here, part_send.at[block, m], part_recv.at[block, m], {"parts": 1 - part})

    def swap_arrival(block, m):
        there = weight_block(block, m, 1 - part)
        return remote(there, there, part_send.at[block, m], part_recv.at[block, m], {"parts": 1 - part})

    def result_rows(p):
        return pl.ds(pl.multiple_of(p * piece, piece), piece)

    def result_columns(source):
        return pl.ds(pl.multiple_of(source * width, width), width)

    def gated_rows(block, p):
        return gated_ref.at[pl.ds(pl.multiple_of(block * rows + p * piece, piece), piece), :]

    def give(block, p):
        return remote(gated_rows(block, p), out_ref.at[result_rows(p), result_columns(seq)],
                      out_send.at[block, p], out_recv.at[seq, p], {"seq": block})

    def take(source, p):
        here = out_ref.at[result_rows(p), result_columns(source)]
        return remote(here, here, out_send.at[source, p], out_recv.at[source, p], {"seq": source})

    def keep(p):
        return pltpu.make_async_copy(
            gated_rows(seq, p), out_ref.at[result_rows(p), result_columns(seq)], own_sem.at[p]
        )

    def inside(other):
        return (other >= 0) & (other < count)

    def pick(values, index):
        found = values[0]
        for n in range(1, len(values)):
            found = jnp.where(index == n, values[n], found)
        return found

    def by_plane(table, index):
        flat = [value for row in table for value in row]
        return pick(flat, seq * len(table[0]) + index)

    orders = block_orders(count)
    ready = reach_table(orders)
    is_first, is_last = seq == 0, seq == count - 1
    is_end = is_first | is_last
    deferred = (seq == 1) if count == 4 else (seq == count)

    for fill in fills:
        fill.start()
    pl.semaphore_wait(barrier, count - 1 + len(mates))

    def send_weights(way, distances):
        for distance in distances:
            other = seq + way * distance

            @pl.when(inside(other))
            def _():
                for m in range(3):
                    spread(other, m).start()

    def send_own(way):
        for p in range(PIECES):
            hop(seq, p, way, own_piece(p)).start()

    for way in (1, -1):
        @pl.when(inside(seq + way))
        def _():
            send_weights(way, range(count - 1, 0, -1))
            if way == 1:
                @pl.when(jnp.logical_not(deferred))
                def _():
                    send_own(way)
            else:
                send_own(way)

    for p in range(PIECES):
        side(seq, p, own_piece(p)).start()
        core(seq, 0, p, own_piece(p)).start()

    def relay(block, p):
        way = jnp.where(block < seq, 1, -1)
        hop(block, p, way).wait_recv()

        @pl.when(inside(seq + way))
        def _():
            hop(block, p, way).start()

        side(block, p).start()
        core(block, 0, p).start()

    def pass_side(block, p):
        side_arrival(block, p).wait_recv()
        core(block, 1, p).start()

    def pass_weights(other, m):
        @pl.when(inside(other))
        def _():
            spread_arrival(other, m).wait_recv()
            swap(other, m).start()

    toward = jnp.where(2 * seq < count, -1, 1)
    first_block = by_plane(orders, 0)

    @pl.when(is_end)
    def _():
        for m in range(3):
            pass_side(seq, m)
            pass_weights(seq - toward * (count - 1), m)
        for p in range(3, PIECES):
            pass_side(seq, p)
        for distance in range(1, count - 1):
            for m in range(3):
                pass_weights(seq - toward * distance, m)
        for p in range(PIECES):
            relay(first_block, p)

    @pl.when(jnp.logical_not(is_end))
    def _():
        for p in range(PIECES):
            pass_side(seq, p)
        for distance in range(count - 2, 1, -1):
            for m in range(3):
                pass_weights(seq - toward * distance, m)
        for distance in range(count - 2, 0, -1):
            for m in range(3):
                pass_weights(seq + toward * distance, m)
        for p in range(PIECES):
            relay(first_block, p)
            if p < 3:
                pass_weights(seq - toward, p)

        @pl.when(deferred)
        def _():
            send_own(1)

    for p in range(PIECES - SIDE_LAG):
        pass_side(first_block, p)
    for fill in fills:
        fill.wait()

    scale_ref[...] = jnp.sqrt(one_less_exp(2.0 * rate_ref[...]))
    lane_groups = width // LANES
    chunk = piece // CHUNKS

    def project(block, p):
        for which in range(2):
            core_arrival(block, which, p).wait_recv()
        top = pl.ds(pl.multiple_of(block * rows + p * piece, piece), piece)
        found = jnp.dot(all_ref[top, :], weights_ref[...], preferred_element_type=jnp.float32)
        found = found.astype(jnp.bfloat16)
        query_rows[top, :] = found[:, :width]
        product = (
            found[:, width : 2 * width].astype(jnp.float32) * found[:, 2 * width :].astype(jnp.float32)
        )
        product = product.astype(jnp.bfloat16).astype(jnp.float32)
        for group in range(lane_groups):
            signal[group, top, :] = product[:, group * LANES : (group + 1) * LANES]

    def scan(g, _):
        block, p = g // PIECES, lax.rem(g, PIECES)
        top = pl.multiple_of(g * piece, piece)
        for group in range(lane_groups):
            lanes = pl.ds(group * LANES, LANES)
            rates = rate_ref[:, lanes]
            residues = residue_ref[:, lanes]
            scale = scale_ref[:, lanes]
            decay = jnp.exp(-rates)
            weight = residues * scale
            chunk_decay = jnp.exp(-rates * chunk)

            def rows_of(array):
                return [jnp.broadcast_to(array[m : m + 1, :], (CHUNKS, LANES)) for m in range(modes)]

            decays = rows_of(decay)
            weights = rows_of(weight)

            def sums(step, states):
                here = signal[group, pl.ds(top + step, CHUNKS, stride=chunk), :]
                return tuple(d * s + here for d, s in zip(decays, states))

            zero = jnp.zeros((CHUNKS, LANES), jnp.float32)
            finals = lax.fori_loop(0, chunk, sums, (zero,) * modes, unroll=4)
            for m in range(modes):
                ends[m] = finals[m]
            state = carried_ref[:, lanes]
            for c in range(CHUNKS):
                entering[:, c, :] = residues * state
                state = chunk_decay * state + scale * ends[:, c, :]
            carried_ref[:, lanes] = state

            def outputs(step, states):
                here = signal[group, pl.ds(top + step, CHUNKS, stride=chunk), :]
                states = tuple(d * s + w * here for d, s, w in zip(decays, states, weights))
                terms = list(states)
                while len(terms) > 1:
                    terms = [a + b for a, b in zip(terms[::2], terms[1::2])] + (
                        [terms[-1]] if len(terms) % 2 else []
                    )
                conv[group, pl.ds(step, CHUNKS, stride=chunk), :] = terms[0]
                return states

            starts = tuple(entering[m] for m in range(modes))
            lax.fori_loop(0, chunk, outputs, starts, unroll=4)
            rounded = conv[group].astype(jnp.bfloat16).astype(jnp.float32)
            gated_ref[pl.ds(top, piece), lanes] = (
                query_rows[pl.ds(top, piece), lanes].astype(jnp.float32) * rounded
            ).astype(jnp.bfloat16)

        @pl.when(block == seq)
        def _():
            keep(p).start()

        return 0

    def scan_and_send(g, k):
        scan(g, 0)

        block = g // PIECES

        @pl.when((block != seq) & (k >= release(block)))
        def _():
            give(block, lax.rem(g, PIECES)).start()

        return k

    releases = release_table(count)

    def release(block):
        return by_plane(releases, block)

    def send_held(g, k):
        block = g // PIECES

        @pl.when((block != seq) & (release(block) == k))
        def _():
            give(block, lax.rem(g, PIECES)).start()

        return k

    last = (count - 1) * PIECES

    def block_of(k):
        return by_plane(orders, k // PIECES)

    def slot(k, _):
        @pl.when(k < last)
        def _():
            relay(block_of(k), lax.rem(k, PIECES))

        @pl.when(k == PIECES)
        def _():
            for distance in range(1, count):
                for other in (seq - distance, seq + distance):
                    @pl.when(inside(other))
                    def _():
                        for m in range(3):
                            swap_arrival(other, m).wait_recv()

        def one(which, _):
            early = which < 2
            n = jnp.where(early, k - PIECES, k - LAG)
            block = jnp.where(which == 0, seq, jnp.where(which == 1, first_block, block_of(k - LAG)))
            known = (early & (n < PIECES)) | (jnp.logical_not(early) & (n >= PIECES))

            @pl.when(known)
            def _():
                project(block, lax.rem(n, PIECES))

            return 0

        lax.fori_loop(0, 3, one, 0)
        done, reach = by_plane(ready, k - PIECES), by_plane(ready, k - PIECES + 1)
        lax.fori_loop(done, reach, scan_and_send, k)

        @pl.when(k >= last - 2)
        def _():
            lax.fori_loop(0, done, send_held, k)

        @pl.when(k < last + SIDE_LAG)
        def _():
            pass_side(block_of(k - SIDE_LAG), lax.rem(k - SIDE_LAG, PIECES))

        return 0

    lax.fori_loop(PIECES, last + LAG, slot, 0)
    state_ref[...] = carried_ref[...]

    for p in range(PIECES):
        @pl.when(seq > 0)
        def _():
            hop(seq, p, -1, own_piece(p)).wait_send()

        @pl.when(seq + 1 < count)
        def _():
            hop(seq, p, 1, own_piece(p)).wait_send()

        side(seq, p, own_piece(p)).wait_send()
        core(seq, 0, p, own_piece(p)).wait_send()
        core(seq, 1, p).wait_send()
    others = [
        (other, way)
        for distance in range(1, count)
        for other, way in ((seq - distance, 1), (seq + distance, -1))
    ]
    for other, way in others:
        @pl.when(inside(other))
        def _():
            for m in range(3):
                spread(other, m).wait_send()
                swap(other, m).wait_send()
            for p in range(PIECES):
                @pl.when(inside(seq + way))
                def _():
                    hop(other, p, way).wait_send()

                side(other, p).wait_send()
                for which in range(2):
                    core(other, which, p).wait_send()
    for p in range(PIECES):
        keep(p).wait()
    for other, way in others:
        @pl.when(inside(other))
        def _():
            for p in range(PIECES):
                give(other, p).wait_send()
    for other, way in others:
        @pl.when(inside(other))
        def _():
            for p in range(PIECES):
                take(other, p).wait_recv()


def whole_layer(tokens, w_query, w_key, w_value, rate, residue, carried, count):
    rows, columns = tokens.shape
    depth, outer = w_query.shape
    width, modes = rate.shape
    length = rows * count
    vmem = pl.BlockSpec(memory_space=pltpu.VMEM)
    anywhere = pl.BlockSpec(memory_space=pl.ANY)
    dma = pltpu.SemaphoreType.DMA
    table = pltpu.VMEM((modes, width), jnp.float32)
    operands = (tokens, w_query, w_key, w_value, rate.T, residue.T, carried.T)
    gated, state = pl.pallas_call(
        functools.partial(layer_kernel, count),
        out_shape=(
            jax.ShapeDtypeStruct((rows, outer), jnp.bfloat16),
            jax.ShapeDtypeStruct((modes, width), jnp.float32),
        ),
        in_specs=[anywhere] * 7,
        out_specs=(anywhere, vmem),
        scratch_shapes=[
            pltpu.VMEM((length, columns * 4), jnp.bfloat16),
            pltpu.VMEM((depth * count, 3 * width), jnp.bfloat16),
            pltpu.VMEM((length, width), jnp.bfloat16),
            pltpu.VMEM((width // LANES, length, LANES), jnp.float32),
            pltpu.VMEM((width // LANES, rows // PIECES, LANES), jnp.float32),
            pltpu.VMEM((length, width), jnp.bfloat16),
            pltpu.VMEM((modes, CHUNKS, LANES), jnp.float32),
            pltpu.VMEM((modes, CHUNKS, LANES), jnp.float32),
        ] + [table] * 4 + [
            dma((7,)),
            dma((count, PIECES, 2)), dma((count, PIECES)),
            dma((count, PIECES)), dma((count, PIECES)),
            dma((count, 2, PIECES)), dma((count, 2, PIECES)),
            dma((count, 3)), dma((count, 3)),
            dma((count, 3)), dma((count, 3)),
            dma((count, PIECES)), dma((count, PIECES)),
            dma((PIECES,)),
        ],
        compiler_params=pltpu.CompilerParams(
            collective_id=0, has_side_effects=True, vmem_limit_bytes=40 * 2**20
        ),
    )(*(pltpu.with_memory_space_constraint(array, pltpu.HBM) for array in operands))
    return gated, state.T


def per_device_channels(tokens, w_query, w_key, w_value, decay_rate, residue, carried):
    count = lax.axis_size("seq")
    return whole_layer(tokens, w_query, w_key, w_value, decay_rate, residue, carried, count)


def solution(mesh):
    in_specs = (
        P(("parts", "seq"), ("chan", "rep")),
        P("seq", ("chan", "rep")),
        P("seq", ("chan", "rep")),
        P("seq", ("chan", "rep")),
        P(("chan", "rep", "seq"), None),
        P(("chan", "rep", "seq"), None),
        P(("parts", "chan", "rep", "seq"), None),
    )
    out_specs = (P(("parts", "seq"), ("chan", "rep")), P(("parts", "chan", "rep", "seq"), None))

    def body(*arrays):
        own_channels = arrays[4].shape[0]
        mates = all(mesh.shape[a] == 2 for a in ("parts", "chan", "rep"))
        chosen = per_device_channels if own_channels % LANES == 0 and mates else per_device
        return chosen(*arrays)

    return jax.shard_map(body, mesh=mesh, in_specs=in_specs, out_specs=out_specs, check_vma=False)
```

```python
import functools

import jax
import jax.numpy as jnp
from jax import lax
from jax.experimental import pallas as pl
from jax.experimental.pallas import tpu as pltpu
from jax.sharding import PartitionSpec as P

BLOCK = 128
LANES = 128
CHUNKS = 8
MESH = pl.DeviceIdType.MESH


HIGHEST_PRECISION = lax.Precision.HIGHEST


def mode_scale(decay_rates):
    return jnp.sqrt(-jnp.expm1(-2.0 * decay_rates))


def local_ends(blocks, decay_rates):
    block_width = blocks.shape[2]
    offsets = jnp.arange(block_width, dtype=jnp.float32)
    tail_powers = jnp.exp(-decay_rates[:, :, None] * (block_width - 1.0 - offsets)[None, None, :])
    sums_here = jnp.einsum("cnb,cmb->cnm", blocks, tail_powers, precision=HIGHEST_PRECISION)
    return mode_scale(decay_rates)[:, None, :] * sums_here


def combine_states(earlier, later):
    return (earlier[0] * later[0], later[0] * earlier[1] + later[1])


def block_sums(block_ends, decay_rates, block_width):
    step_decay = jnp.broadcast_to(jnp.exp(-decay_rates * block_width)[:, None, :], block_ends.shape)
    unused_decay, running = lax.associative_scan(combine_states, (step_decay, block_ends), axis=1)
    return running


def entering_states(running, decay_rates, start_state, block_width):
    count_blocks = running.shape[1]
    block_starts = jnp.arange(count_blocks, dtype=jnp.float32) * block_width
    decayed = (
        jnp.exp(-decay_rates[:, None, :] * block_starts[None, :, None]) * start_state[:, None, :]
    )
    earlier_sums = jnp.concatenate([jnp.zeros_like(running[:, :1]), running[:, :-1]], axis=1)
    final_state = (
        jnp.exp(-decay_rates * (count_blocks * block_width)) * start_state + running[:, -1]
    )
    return (decayed + earlier_sums, final_state)


def block_convolve(blocks, decay_rates, residues, entering):
    block_width = blocks.shape[2]
    offsets = jnp.arange(block_width, dtype=jnp.float32)
    powers = jnp.exp(-decay_rates[:, :, None] * offsets[None, None, :])
    kernel = jnp.sum((residues * mode_scale(decay_rates))[:, :, None] * powers, axis=1)
    out_index = jnp.arange(block_width, dtype=jnp.int32)[:, None]
    in_index = jnp.arange(block_width, dtype=jnp.int32)[None, :]
    lag = jnp.maximum(out_index - in_index, 0)
    causal = (out_index >= in_index).astype(jnp.float32)
    toeplitz = kernel[:, lag] * causal[None, :, :]
    direct = jnp.einsum("cij,cnj->cni", toeplitz, blocks, precision=HIGHEST_PRECISION)
    leading = residues[:, :, None] * jnp.exp(
        -decay_rates[:, :, None] * (offsets + 1.0)[None, None, :]
    )
    return direct + jnp.einsum("cnm,cmb->cnb", entering, leading, precision=HIGHEST_PRECISION)


def per_device(tokens, w_query, w_key, w_value, decay_rate, residue, carried):
    gathered = lax.all_gather(tokens, ("chan", "rep"), axis=1, tiled=True)
    pieces = (
        lax.all_gather(w_query, "seq", axis=0, tiled=True),
        lax.all_gather(w_key, "seq", axis=0, tiled=True),
        lax.all_gather(w_value, "seq", axis=0, tiled=True),
    )
    query_acc, key_acc, value_acc = tuple(
        (
            lax.dot_general(
                weight_piece, gathered, (((0,), (1,)), ((), ())), preferred_element_type=jnp.float32
            )
            for weight_piece in pieces
        )
    )
    query_rows = query_acc.astype(jnp.bfloat16)
    key_rows = key_acc.astype(jnp.bfloat16)
    value_rows = value_acc.astype(jnp.bfloat16)
    query_rows, key_rows, value_rows = lax.optimization_barrier((query_rows, key_rows, value_rows))
    product = (key_rows.astype(jnp.float32) * value_rows.astype(jnp.float32)).astype(jnp.bfloat16)
    owned = lax.all_to_all(product, "seq", split_axis=0, concat_axis=1, tiled=True)
    own_chan = owned.shape[0]
    blocks = owned.astype(jnp.float32).reshape(own_chan, -1, BLOCK)
    block_end = local_ends(blocks, decay_rate)
    running = block_sums(block_end, decay_rate, BLOCK)
    entering, new_state = entering_states(running, decay_rate, carried, BLOCK)
    conv_out = (
        block_convolve(blocks, decay_rate, residue, entering)
        .reshape(own_chan, -1)
        .astype(jnp.bfloat16)
    )
    conv_back = lax.all_to_all(conv_out, "seq", split_axis=1, concat_axis=0, tiled=True)
    conv_back = lax.optimization_barrier(conv_back)
    gated_rows = (query_rows.astype(jnp.float32) * conv_back.astype(jnp.float32)).astype(
        jnp.bfloat16
    )
    return (gated_rows.T, new_state)


PIECES = 4
SIDE_LAG = (1, 2)
LAG = (2, 3)
CAP = 2
UNROLL = 8


def block_orders(count):
    if count == 4:
        return ((1, 2, 3), (0, 2, 3), (3, 0, 1), (2, 0, 1))
    return tuple(
        tuple(sorted((b for b in range(count) if b != z), key=lambda b: (abs(b - z), b)))
        for z in range(count)
    )


def one_less_exp(x):
    series = jnp.ones_like(x)
    for n in range(9, 1, -1):
        series = 1.0 - series * x * (1.0 / n)
    return jnp.where(x < 0.25, x * series, 1.0 - jnp.exp(-x))


def release_table(count):
    if count != 4:
        return ((0,) * count,) * count
    last = (count - 1) * PIECES
    return (
        (0, 0, last - 2, 0),
        (last - 1, 0, 0, last - 1),
        (last, 0, 0, last - 1),
        (last - 1, 0, 0, 0),
    )


def reach_table(orders):
    count = len(orders)
    last = (count - 1) * PIECES
    table = []
    for z, order in enumerate(orders):
        when = {}
        for p in range(PIECES):
            when[z, p] = when[order[0], p] = PIECES + p
            for n in range(1, count - 1):
                when[order[n], p] = n * PIECES + p + LAG[0 if z in (0, count - 1) else 1]
        row = [0]
        for k in range(PIECES, last + LAG[1]):
            g = row[-1]
            top = g + CAP if k < last else count * PIECES
            while g < min(top, count * PIECES) and when[divmod(g, PIECES)] <= k:
                g += 1
            row.append(g)
        table.append(row)
    return table


def layer_kernel(count, tokens_ref, query_ref, key_ref, value_ref, rate_hbm, residue_hbm,
                 carried_hbm, out_ref, state_ref,
                 all_ref, weights_ref, query_rows, signal, conv, gated_ref, ends, entering,
                 rate_ref, scale_ref, residue_ref, carried_ref, decay_ref, weight_ref, step_ref,
                 fill_sem, hop_send, hop_recv, side_send, side_recv, core_send, core_recv,
                 part_send, part_recv, layer_send, layer_recv, out_send, out_recv, own_sem):
    part, seq, chan, rep = (lax.axis_index(a) for a in ("parts", "seq", "chan", "rep"))
    rows, columns = tokens_ref.shape
    depth, outer = query_ref.shape
    width = outer // count
    half = depth // 2
    piece = rows // PIECES
    modes = rate_ref.shape[0]
    own_columns = pl.ds(pl.multiple_of(seq * width, width), width)
    matrices = (query_ref, key_ref, value_ref)

    barrier = pltpu.get_barrier_semaphore()
    mates = ({"parts": 1 - part}, {"chan": 1 - chan}, {"rep": 1 - rep})
    for mate in mates:
        pl.semaphore_signal(barrier, inc=1, device_id=mate, device_id_type=MESH)
    for step in range(1, count):
        pl.semaphore_signal(
            barrier, inc=1, device_id={"seq": lax.rem(seq + step, count)}, device_id_type=MESH
        )

    fills = [
        pltpu.make_async_copy(
            tokens_ref,
            all_ref.at[pl.ds(pl.multiple_of(seq * rows, rows), rows),
                       pl.ds(pl.multiple_of((chan * 2 + rep) * columns, columns), columns)],
            fill_sem.at[0])
    ] + [
        pltpu.make_async_copy(
            matrices[m].at[:, own_columns],
            weights_ref.at[pl.ds(pl.multiple_of(seq * depth, depth), depth), pl.ds(m * width, width)],
            fill_sem.at[1 + m])
        for m in range(3)
    ] + [
        pltpu.make_async_copy(source, target, fill_sem.at[4 + n])
        for n, (source, target) in enumerate((
            (rate_hbm, rate_ref), (residue_hbm, residue_ref), (carried_hbm, carried_ref),
        ))
    ]

    def remote(source, target, send, recv, device):
        return pltpu.make_async_remote_copy(
            src_ref=source, dst_ref=target, send_sem=send, recv_sem=recv,
            device_id=device, device_id_type=MESH,
        )

    def token_block(block, side, core, p):
        top = pl.multiple_of(block * rows + p * piece, piece)
        left = pl.multiple_of((side * 2 + core) * columns, columns)
        return all_ref.at[pl.ds(top, piece), pl.ds(left, columns)]

    def own_piece(p):
        return tokens_ref.at[pl.ds(p * piece, piece), :]

    def hop(block, p, way, source=None):
        here = token_block(block, chan, rep, p)
        return remote(here if source is None else source, here,
                      hop_send.at[block, (1 - way) // 2], hop_recv.at[block, p], {"seq": seq + way})

    def side(block, p, source=None):
        here = token_block(block, chan, rep, p)
        return remote(here if source is None else source, here,
                      side_send.at[block], side_recv.at[block, p], {"chan": 1 - chan})

    def side_arrival(block, p):
        there = token_block(block, 1 - chan, rep, p)
        return remote(there, there, side_send.at[block], side_recv.at[block, p], {"chan": 1 - chan})

    def core(block, which, p, source=None):
        here = token_block(block, chan if which == 0 else 1 - chan, rep, p)
        return remote(here if source is None else source, here,
                      core_send.at[block], core_recv.at[block, p], {"rep": 1 - rep})

    def core_arrivals(block, p):
        top = pl.multiple_of(block * rows + p * piece, piece)
        there = all_ref.at[pl.ds(top, piece), pl.ds(0, 2 * columns)]
        return remote(there, there, core_send.at[block], core_recv.at[block, p], {"rep": 1 - rep})

    def sent(semaphore, other, wide):
        there = all_ref.at[pl.ds(0, rows), pl.ds(0, wide * columns)]
        return remote(there, there, semaphore, hop_recv.at[other, 0], {"rep": 1 - rep})

    def swapped(other):
        there = weights_ref.at[pl.ds(pl.multiple_of(other * depth + (1 - part) * half, half), half), :]
        return remote(there, there, part_send.at[other], part_recv.at[other], {"parts": 1 - part})

    def spread_out(other):
        there = weights_ref.at[pl.ds(pl.multiple_of(other * depth + part * half, half), half), :]
        return remote(there, there, layer_send.at[other], layer_recv.at[other, 0], {"seq": other})

    def weight_block(block, m, part_of):
        top = pl.multiple_of(block * depth + part_of * half, half)
        return weights_ref.at[pl.ds(top, half), pl.ds(m * width, width)]

    def spread(target, m):
        source = matrices[m].at[
            pl.ds(pl.multiple_of(part * half, half), half),
            pl.ds(pl.multiple_of(target * width, width), width),
        ]
        return remote(source, weight_block(seq, m, part),
                      layer_send.at[target], layer_recv.at[seq, m], {"seq": target})

    def spread_arrival(block, m):
        here = weight_block(block, m, part)
        return remote(here, here, layer_send.at[block], layer_recv.at[block, m], {"seq": block})

    def swap(block, m):
        here = weight_block(block, m, part)
        return remote(here, here, part_send.at[block], part_recv.at[block], {"parts": 1 - part})

    def result_rows(p):
        return pl.ds(pl.multiple_of(p * piece, piece), piece)

    def result_columns(source):
        return pl.ds(pl.multiple_of(source * width, width), width)

    def gated_rows(block, p):
        return gated_ref.at[pl.ds(pl.multiple_of(block * rows + p * piece, piece), piece), :]

    def give(block, p):
        return remote(gated_rows(block, p), out_ref.at[result_rows(p), result_columns(seq)],
                      out_send.at[block], out_recv.at[seq], {"seq": block})

    def take(source):
        here = out_ref.at[:, result_columns(source)]
        return remote(here, here, out_send.at[source], out_recv.at[source], {"seq": source})

    def keep(p):
        return pltpu.make_async_copy(
            gated_rows(seq, p), out_ref.at[result_rows(p), result_columns(seq)], own_sem.at[0]
        )

    def inside(other):
        return (other >= 0) & (other < count)

    def pick(values, index):
        found = values[0]
        for n in range(1, len(values)):
            found = jnp.where(index == n, values[n], found)
        return found

    def by_plane(table, index):
        flat = [value for row in table for value in row]
        return pick(flat, seq * len(table[0]) + index)

    orders = block_orders(count)
    ready = reach_table(orders)
    is_first, is_last = seq == 0, seq == count - 1
    is_end = is_first | is_last
    deferred = (seq == 1) if count == 4 else (seq == count)

    for fill in fills:
        fill.start()
    pl.semaphore_wait(barrier, count - 1 + len(mates))

    def send_weights(way, distances):
        for distance in distances:
            other = seq + way * distance

            @pl.when(inside(other))
            def _():
                for m in range(3):
                    spread(other, m).start()

    def send_own(way):
        for p in range(PIECES):
            hop(seq, p, way, own_piece(p)).start()

    for way in (1, -1):
        @pl.when(inside(seq + way))
        def _():
            send_weights(way, range(count - 1, 0, -1))
            if way == 1:
                @pl.when(jnp.logical_not(deferred))
                def _():
                    send_own(way)
            else:
                send_own(way)

    for p in range(PIECES):
        side(seq, p, own_piece(p)).start()
        core(seq, 0, p, own_piece(p)).start()

    def relay(block, p):
        way = jnp.where(block < seq, 1, -1)
        hop(block, p, way).wait_recv()

        @pl.when(inside(seq + way))
        def _():
            hop(block, p, way).start()

        side(block, p).start()
        core(block, 0, p).start()

    def pass_side(block, p):
        side_arrival(block, p).wait_recv()
        core(block, 1, p).start()

    def pass_weights(other, m):
        @pl.when(inside(other))
        def _():
            spread_arrival(other, m).wait_recv()
            swap(other, m).start()

    toward = jnp.where(2 * seq < count, -1, 1)
    side_lag = jnp.where(is_end, SIDE_LAG[0], SIDE_LAG[1])
    lag = jnp.where(is_end, LAG[0], LAG[1])
    first_block = by_plane(orders, 0)

    @pl.when(is_end)
    def _():
        for m in range(3):
            pass_side(seq, m)
            pass_weights(seq - toward * (count - 1), m)
        for p in range(3, PIECES):
            pass_side(seq, p)
        for distance in range(1, count - 1):
            for m in range(3):
                pass_weights(seq - toward * distance, m)
        for p in range(PIECES):
            relay(first_block, p)

    @pl.when(jnp.logical_not(is_end))
    def _():
        for p in range(PIECES):
            pass_side(seq, p)
        for distance in range(count - 2, 1, -1):
            for m in range(3):
                pass_weights(seq - toward * distance, m)
        for distance in range(count - 2, 0, -1):
            for m in range(3):
                pass_weights(seq + toward * distance, m)
        for p in range(PIECES):
            relay(first_block, p)
            if p < 3:
                pass_weights(seq - toward, p)

        @pl.when(deferred)
        def _():
            send_own(1)

    for p in range(PIECES - SIDE_LAG[0]):
        @pl.when(p < PIECES - side_lag)
        def _():
            pass_side(first_block, p)

    for fill in fills:
        fill.wait()

    scale_ref[...] = jnp.sqrt(one_less_exp(2.0 * rate_ref[...]))
    lane_groups = width // LANES
    chunk = piece // CHUNKS
    step_ref[...] = jnp.exp(-rate_ref[...] * chunk)
    for group in range(lane_groups):
        lanes = pl.ds(group * LANES, LANES)
        decay = jnp.exp(-rate_ref[:, lanes])
        weight = residue_ref[:, lanes] * scale_ref[:, lanes]
        for m in range(modes):
            decay_ref[group, m] = jnp.broadcast_to(decay[m : m + 1, :], (CHUNKS, LANES))
            weight_ref[group, m] = jnp.broadcast_to(weight[m : m + 1, :], (CHUNKS, LANES))

    def project(block, p):
        core_arrivals(block, p).wait_recv()
        top = pl.ds(pl.multiple_of(block * rows + p * piece, piece), piece)
        found = jnp.dot(all_ref[top, :], weights_ref[...], preferred_element_type=jnp.float32)
        found = found.astype(jnp.bfloat16)
        query_rows[top, :] = found[:, :width]
        product = (
            found[:, width : 2 * width].astype(jnp.float32) * found[:, 2 * width :].astype(jnp.float32)
        )
        product = product.astype(jnp.bfloat16).astype(jnp.float32)
        for group in range(lane_groups):
            signal[group, top, :] = product[:, group * LANES : (group + 1) * LANES]

    def scan(g, _):
        block, p = g // PIECES, lax.rem(g, PIECES)
        top = pl.multiple_of(g * piece, piece)
        for group in range(lane_groups):
            lanes = pl.ds(group * LANES, LANES)
            residues = residue_ref[:, lanes]
            scale = scale_ref[:, lanes]
            chunk_decay = step_ref[:, lanes]
            decays = [decay_ref[group, m] for m in range(modes)]
            weights = [weight_ref[group, m] for m in range(modes)]

            def sums(step, states):
                here = signal[group, pl.ds(top + step, CHUNKS, stride=chunk), :]
                return tuple(d * s + here for d, s in zip(decays, states))

            zero = jnp.zeros((CHUNKS, LANES), jnp.float32)
            finals = lax.fori_loop(0, chunk, sums, (zero,) * modes, unroll=UNROLL)
            for m in range(modes):
                ends[pl.ds(m, CHUNKS, stride=modes), :] = finals[m]
            state = carried_ref[:, lanes]
            for c in range(CHUNKS):
                at = pl.ds(c * modes, modes)
                entering[at, :] = residues * state
                state = chunk_decay * state + scale * ends[at, :]
            carried_ref[:, lanes] = state

            def outputs(step, states):
                here = signal[group, pl.ds(top + step, CHUNKS, stride=chunk), :]
                states = tuple(d * s + w * here for d, s, w in zip(decays, states, weights))
                terms = list(states)
                while len(terms) > 1:
                    terms = [a + b for a, b in zip(terms[::2], terms[1::2])] + (
                        [terms[-1]] if len(terms) % 2 else []
                    )
                conv[group, pl.ds(step, CHUNKS, stride=chunk), :] = terms[0]
                return states

            starts = tuple(entering[pl.ds(m, CHUNKS, stride=modes), :] for m in range(modes))
            lax.fori_loop(0, chunk, outputs, starts, unroll=UNROLL)
            rounded = conv[group].astype(jnp.bfloat16).astype(jnp.float32)
            gated_ref[pl.ds(top, piece), lanes] = (
                query_rows[pl.ds(top, piece), lanes].astype(jnp.float32) * rounded
            ).astype(jnp.bfloat16)

        @pl.when(block == seq)
        def _():
            keep(p).start()

        return 0

    def scan_and_send(g, k):
        scan(g, 0)

        block = g // PIECES

        @pl.when((block != seq) & (k >= release(block)))
        def _():
            give(block, lax.rem(g, PIECES)).start()

        return k

    releases = release_table(count)

    def release(block):
        return by_plane(releases, block)

    def send_held(g, k):
        block = g // PIECES

        @pl.when((block != seq) & (release(block) == k))
        def _():
            give(block, lax.rem(g, PIECES)).start()

        return k

    last = (count - 1) * PIECES

    def block_of(k):
        return by_plane(orders, k // PIECES)

    def slot(k, _):
        @pl.when(k < last)
        def _():
            relay(block_of(k), lax.rem(k, PIECES))

        @pl.when(k == PIECES)
        def _():
            for distance in range(1, count):
                for other in (seq - distance, seq + distance):
                    @pl.when(inside(other))
                    def _():
                        swapped(other).wait_recv()

        def next_side():
            pass_side(block_of(k - side_lag), lax.rem(k - side_lag, PIECES))

        first = is_end & (k > last)

        @pl.when(first & (k < last + side_lag))
        def _():
            next_side()

        def one(which, _):
            early = which < 2
            n = jnp.where(early, k - PIECES, k - lag)
            block = jnp.where(which == 0, seq, jnp.where(which == 1, first_block, block_of(k - lag)))
            known = (early & (n < PIECES)) | (jnp.logical_not(early) & (n >= PIECES) & (n < last))

            @pl.when(known)
            def _():
                project(block, lax.rem(n, PIECES))

            return 0

        lax.fori_loop(0, 3, one, 0)
        done, reach = by_plane(ready, k - PIECES), by_plane(ready, k - PIECES + 1)
        lax.fori_loop(done, reach, scan_and_send, k)

        @pl.when((k >= last - 2) & (k <= last))
        def _():
            lax.fori_loop(0, done, send_held, k)

        @pl.when(jnp.logical_not(first) & (k < last + side_lag))
        def _():
            next_side()

        return 0

    lax.fori_loop(PIECES, last + LAG[1], slot, 0)
    state_ref[...] = carried_ref[...]

    @pl.when(seq > 0)
    def _():
        sent(hop_send.at[seq, 1], seq, 1).wait_send()

    @pl.when(seq + 1 < count)
    def _():
        sent(hop_send.at[seq, 0], seq, 1).wait_send()

    sent(side_send.at[seq], seq, 1).wait_send()
    sent(core_send.at[seq], seq, 2).wait_send()
    others = [
        (other, way)
        for distance in range(1, count)
        for other, way in ((seq - distance, 1), (seq + distance, -1))
    ]
    for other, way in others:
        @pl.when(inside(other))
        def _():
            @pl.when(inside(seq + way))
            def _():
                sent(hop_send.at[other, (1 - way) // 2], other, 1).wait_send()

            sent(side_send.at[other], other, 1).wait_send()
            sent(core_send.at[other], other, 2).wait_send()
            spread_out(other).wait_send()
            swapped(other).wait_send()
    kept = out_ref.at[:, result_columns(seq)]
    pltpu.make_async_copy(kept, kept, own_sem.at[0]).wait()
    for other, way in others:
        @pl.when(inside(other))
        def _():
            take(other).wait_send()
    for other, way in others:
        @pl.when(inside(other))
        def _():
            take(other).wait_recv()


def whole_layer(tokens, w_query, w_key, w_value, rate, residue, carried, count):
    rows, columns = tokens.shape
    depth, outer = w_query.shape
    width, modes = rate.shape
    length = rows * count
    vmem = pl.BlockSpec(memory_space=pltpu.VMEM)
    anywhere = pl.BlockSpec(memory_space=pl.ANY)
    dma = pltpu.SemaphoreType.DMA
    table = pltpu.VMEM((modes, width), jnp.float32)
    operands = (tokens, w_query, w_key, w_value, rate.T, residue.T, carried.T)
    gated, state = pl.pallas_call(
        functools.partial(layer_kernel, count),
        out_shape=(
            jax.ShapeDtypeStruct((rows, outer), jnp.bfloat16),
            jax.ShapeDtypeStruct((modes, width), jnp.float32),
        ),
        in_specs=[anywhere] * 7,
        out_specs=(anywhere, vmem),
        scratch_shapes=[
            pltpu.VMEM((length, columns * 4), jnp.bfloat16),
            pltpu.VMEM((depth * count, 3 * width), jnp.bfloat16),
            pltpu.VMEM((length, width), jnp.bfloat16),
            pltpu.VMEM((width // LANES, length, LANES), jnp.float32),
            pltpu.VMEM((width // LANES, rows // PIECES, LANES), jnp.float32),
            pltpu.VMEM((length, width), jnp.bfloat16),
            pltpu.VMEM((CHUNKS * modes, LANES), jnp.float32),
            pltpu.VMEM((CHUNKS * modes, LANES), jnp.float32),
        ] + [table] * 4 + [
            pltpu.VMEM((width // LANES, modes, CHUNKS, LANES), jnp.float32),
            pltpu.VMEM((width // LANES, modes, CHUNKS, LANES), jnp.float32),
            table,
            dma((7,)),
            dma((count, 2)), dma((count, PIECES)),
            dma((count,)), dma((count, PIECES)),
            dma((count,)), dma((count, PIECES)),
            dma((count,)), dma((count,)),
            dma((count,)), dma((count, 3)),
            dma((count,)), dma((count,)),
            dma((1,)),
        ],
        compiler_params=pltpu.CompilerParams(
            collective_id=0, has_side_effects=True, vmem_limit_bytes=40 * 2**20
        ),
    )(*(pltpu.with_memory_space_constraint(array, pltpu.HBM) for array in operands))
    return gated, state.T


def per_device_channels(tokens, w_query, w_key, w_value, decay_rate, residue, carried):
    count = lax.axis_size("seq")
    return whole_layer(tokens, w_query, w_key, w_value, decay_rate, residue, carried, count)


def solution(mesh):
    in_specs = (
        P(("parts", "seq"), ("chan", "rep")),
        P("seq", ("chan", "rep")),
        P("seq", ("chan", "rep")),
        P("seq", ("chan", "rep")),
        P(("chan", "rep", "seq"), None),
        P(("chan", "rep", "seq"), None),
        P(("parts", "chan", "rep", "seq"), None),
    )
    out_specs = (P(("parts", "seq"), ("chan", "rep")), P(("parts", "chan", "rep", "seq"), None))

    def body(*arrays):
        own_channels = arrays[4].shape[0]
        mates = all(mesh.shape[a] == 2 for a in ("parts", "chan", "rep"))
        chosen = per_device_channels if own_channels % LANES == 0 and mates else per_device
        return chosen(*arrays)

    return jax.shard_map(body, mesh=mesh, in_specs=in_specs, out_specs=out_specs, check_vma=False)
```

```python
import functools

import jax
import jax.numpy as jnp
from jax import lax
from jax.experimental import pallas as pl
from jax.experimental.pallas import tpu as pltpu
from jax.sharding import PartitionSpec as P

BLOCK = 128
LANES = 128
CHUNKS = 8
MESH = pl.DeviceIdType.MESH


HIGHEST_PRECISION = lax.Precision.HIGHEST


def mode_scale(decay_rates):
    return jnp.sqrt(-jnp.expm1(-2.0 * decay_rates))


def local_ends(blocks, decay_rates):
    block_width = blocks.shape[2]
    offsets = jnp.arange(block_width, dtype=jnp.float32)
    tail_powers = jnp.exp(-decay_rates[:, :, None] * (block_width - 1.0 - offsets)[None, None, :])
    sums_here = jnp.einsum("cnb,cmb->cnm", blocks, tail_powers, precision=HIGHEST_PRECISION)
    return mode_scale(decay_rates)[:, None, :] * sums_here


def combine_states(earlier, later):
    return (earlier[0] * later[0], later[0] * earlier[1] + later[1])


def block_sums(block_ends, decay_rates, block_width):
    step_decay = jnp.broadcast_to(jnp.exp(-decay_rates * block_width)[:, None, :], block_ends.shape)
    unused_decay, running = lax.associative_scan(combine_states, (step_decay, block_ends), axis=1)
    return running


def entering_states(running, decay_rates, start_state, block_width):
    count_blocks = running.shape[1]
    block_starts = jnp.arange(count_blocks, dtype=jnp.float32) * block_width
    decayed = (
        jnp.exp(-decay_rates[:, None, :] * block_starts[None, :, None]) * start_state[:, None, :]
    )
    earlier_sums = jnp.concatenate([jnp.zeros_like(running[:, :1]), running[:, :-1]], axis=1)
    final_state = (
        jnp.exp(-decay_rates * (count_blocks * block_width)) * start_state + running[:, -1]
    )
    return (decayed + earlier_sums, final_state)


def block_convolve(blocks, decay_rates, residues, entering):
    block_width = blocks.shape[2]
    offsets = jnp.arange(block_width, dtype=jnp.float32)
    powers = jnp.exp(-decay_rates[:, :, None] * offsets[None, None, :])
    kernel = jnp.sum((residues * mode_scale(decay_rates))[:, :, None] * powers, axis=1)
    out_index = jnp.arange(block_width, dtype=jnp.int32)[:, None]
    in_index = jnp.arange(block_width, dtype=jnp.int32)[None, :]
    lag = jnp.maximum(out_index - in_index, 0)
    causal = (out_index >= in_index).astype(jnp.float32)
    toeplitz = kernel[:, lag] * causal[None, :, :]
    direct = jnp.einsum("cij,cnj->cni", toeplitz, blocks, precision=HIGHEST_PRECISION)
    leading = residues[:, :, None] * jnp.exp(
        -decay_rates[:, :, None] * (offsets + 1.0)[None, None, :]
    )
    return direct + jnp.einsum("cnm,cmb->cnb", entering, leading, precision=HIGHEST_PRECISION)


def per_device(tokens, w_query, w_key, w_value, decay_rate, residue, carried):
    gathered = lax.all_gather(tokens, ("chan", "rep"), axis=1, tiled=True)
    pieces = (
        lax.all_gather(w_query, "seq", axis=0, tiled=True),
        lax.all_gather(w_key, "seq", axis=0, tiled=True),
        lax.all_gather(w_value, "seq", axis=0, tiled=True),
    )
    query_acc, key_acc, value_acc = tuple(
        (
            lax.dot_general(
                weight_piece, gathered, (((0,), (1,)), ((), ())), preferred_element_type=jnp.float32
            )
            for weight_piece in pieces
        )
    )
    query_rows = query_acc.astype(jnp.bfloat16)
    key_rows = key_acc.astype(jnp.bfloat16)
    value_rows = value_acc.astype(jnp.bfloat16)
    query_rows, key_rows, value_rows = lax.optimization_barrier((query_rows, key_rows, value_rows))
    product = (key_rows.astype(jnp.float32) * value_rows.astype(jnp.float32)).astype(jnp.bfloat16)
    owned = lax.all_to_all(product, "seq", split_axis=0, concat_axis=1, tiled=True)
    own_chan = owned.shape[0]
    blocks = owned.astype(jnp.float32).reshape(own_chan, -1, BLOCK)
    block_end = local_ends(blocks, decay_rate)
    running = block_sums(block_end, decay_rate, BLOCK)
    entering, new_state = entering_states(running, decay_rate, carried, BLOCK)
    conv_out = (
        block_convolve(blocks, decay_rate, residue, entering)
        .reshape(own_chan, -1)
        .astype(jnp.bfloat16)
    )
    conv_back = lax.all_to_all(conv_out, "seq", split_axis=1, concat_axis=0, tiled=True)
    conv_back = lax.optimization_barrier(conv_back)
    gated_rows = (query_rows.astype(jnp.float32) * conv_back.astype(jnp.float32)).astype(
        jnp.bfloat16
    )
    return (gated_rows.T, new_state)


PIECES = 4
SIDE_LAG = (1, 1)
LAG = (2, 2)
SHIFT = 1
CAP = 3
UNROLL = 8


def block_orders(count):
    if count == 4:
        return ((1, 2, 3), (0, 2, 3), (3, 0, 1), (2, 0, 1))
    return tuple(
        tuple(sorted((b for b in range(count) if b != z), key=lambda b: (abs(b - z), b)))
        for z in range(count)
    )


def one_less_exp(x):
    series = jnp.ones_like(x)
    for n in range(9, 1, -1):
        series = 1.0 - series * x * (1.0 / n)
    return jnp.where(x < 0.25, x * series, 1.0 - jnp.exp(-x))


def release_table(count):
    if count != 4:
        return ((0,) * count,) * count
    last = (count - 1) * PIECES
    return (
        (0, 0, last - 2, 0),
        (last - 1, 0, last + 1, last - 1),
        (last, 0, 0, last - 1),
        (last - 1, 0, 0, 0),
    )


def reach_table(orders):
    count = len(orders)
    last = (count - 1) * PIECES
    table = []
    for z, order in enumerate(orders):
        when = {}
        for p in range(PIECES):
            when[z, p] = when[order[0], p] = PIECES + p + (0 if z in (0, count - 1) else SHIFT)
            for n in range(1, count - 1):
                when[order[n], p] = n * PIECES + p + LAG[0 if z in (0, count - 1) else 1]
        row = [0]
        for k in range(PIECES, last + LAG[1]):
            g = row[-1]
            top = g + CAP if k < last else count * PIECES
            while g < min(top, count * PIECES) and when[divmod(g, PIECES)] <= k:
                g += 1
            row.append(g)
        table.append(row)
    return table


def layer_kernel(count, tokens_ref, query_ref, key_ref, value_ref, rate_hbm, residue_hbm,
                 carried_hbm, out_ref, state_ref,
                 all_ref, weights_ref, query_rows, signal, conv, gated_ref, ends, entering,
                 rate_ref, scale_ref, residue_ref, carried_ref, decay_ref, weight_ref, step_ref,
                 fill_sem, hop_send, hop_recv, side_send, side_recv, core_send, core_recv,
                 part_send, part_recv, layer_send, layer_recv, out_send, out_recv, own_sem):
    part, seq, chan, rep = (lax.axis_index(a) for a in ("parts", "seq", "chan", "rep"))
    rows, columns = tokens_ref.shape
    depth, outer = query_ref.shape
    width = outer // count
    half = depth // 2
    piece = rows // PIECES
    modes = rate_ref.shape[0]
    own_columns = pl.ds(pl.multiple_of(seq * width, width), width)
    matrices = (query_ref, key_ref, value_ref)

    barrier = pltpu.get_barrier_semaphore()
    mates = ({"parts": 1 - part}, {"chan": 1 - chan}, {"rep": 1 - rep})
    for mate in mates:
        pl.semaphore_signal(barrier, inc=1, device_id=mate, device_id_type=MESH)
    for step in range(1, count):
        pl.semaphore_signal(
            barrier, inc=1, device_id={"seq": lax.rem(seq + step, count)}, device_id_type=MESH
        )

    fills = [
        pltpu.make_async_copy(
            tokens_ref,
            all_ref.at[pl.ds(pl.multiple_of(seq * rows, rows), rows),
                       pl.ds(pl.multiple_of((chan * 2 + rep) * columns, columns), columns)],
            fill_sem.at[0])
    ] + [
        pltpu.make_async_copy(
            matrices[m].at[:, own_columns],
            weights_ref.at[pl.ds(pl.multiple_of(seq * depth, depth), depth), pl.ds(m * width, width)],
            fill_sem.at[1 + m])
        for m in range(3)
    ] + [
        pltpu.make_async_copy(source, target, fill_sem.at[4 + n])
        for n, (source, target) in enumerate((
            (rate_hbm, rate_ref), (residue_hbm, residue_ref), (carried_hbm, carried_ref),
        ))
    ]

    def remote(source, target, send, recv, device):
        return pltpu.make_async_remote_copy(
            src_ref=source, dst_ref=target, send_sem=send, recv_sem=recv,
            device_id=device, device_id_type=MESH,
        )

    def token_block(block, side, core, p):
        top = pl.multiple_of(block * rows + p * piece, piece)
        left = pl.multiple_of((side * 2 + core) * columns, columns)
        return all_ref.at[pl.ds(top, piece), pl.ds(left, columns)]

    def own_piece(p):
        return tokens_ref.at[pl.ds(p * piece, piece), :]

    def hop(block, p, way, source=None):
        here = token_block(block, chan, rep, p)
        return remote(here if source is None else source, here,
                      hop_send.at[block, (1 - way) // 2], hop_recv.at[block, p], {"seq": seq + way})

    def side(block, p, source=None):
        here = token_block(block, chan, rep, p)
        return remote(here if source is None else source, here,
                      side_send.at[block], side_recv.at[block, p], {"chan": 1 - chan})

    def side_arrival(block, p):
        there = token_block(block, 1 - chan, rep, p)
        return remote(there, there, side_send.at[block], side_recv.at[block, p], {"chan": 1 - chan})

    def core(block, which, p, source=None):
        here = token_block(block, chan if which == 0 else 1 - chan, rep, p)
        return remote(here if source is None else source, here,
                      core_send.at[block], core_recv.at[block, p], {"rep": 1 - rep})

    def core_arrivals(block, p):
        top = pl.multiple_of(block * rows + p * piece, piece)
        there = all_ref.at[pl.ds(top, piece), pl.ds(0, 2 * columns)]
        return remote(there, there, core_send.at[block], core_recv.at[block, p], {"rep": 1 - rep})

    def sent(semaphore, other, wide):
        there = all_ref.at[pl.ds(0, rows), pl.ds(0, wide * columns)]
        return remote(there, there, semaphore, hop_recv.at[other, 0], {"rep": 1 - rep})

    def swapped(other):
        there = weights_ref.at[pl.ds(pl.multiple_of(other * depth + (1 - part) * half, half), half), :]
        return remote(there, there, part_send.at[other], part_recv.at[other], {"parts": 1 - part})

    def spread_out(other):
        there = weights_ref.at[pl.ds(pl.multiple_of(other * depth + part * half, half), half), :]
        return remote(there, there, layer_send.at[other], layer_recv.at[other, 0], {"seq": other})

    def weight_block(block, m, part_of):
        top = pl.multiple_of(block * depth + part_of * half, half)
        return weights_ref.at[pl.ds(top, half), pl.ds(m * width, width)]

    def spread(target, m):
        source = matrices[m].at[
            pl.ds(pl.multiple_of(part * half, half), half),
            pl.ds(pl.multiple_of(target * width, width), width),
        ]
        return remote(source, weight_block(seq, m, part),
                      layer_send.at[target], layer_recv.at[seq, m], {"seq": target})

    def spread_arrival(block, m):
        here = weight_block(block, m, part)
        return remote(here, here, layer_send.at[block], layer_recv.at[block, m], {"seq": block})

    def swap(block, m):
        here = weight_block(block, m, part)
        return remote(here, here, part_send.at[block], part_recv.at[block], {"parts": 1 - part})

    def result_rows(p):
        return pl.ds(pl.multiple_of(p * piece, piece), piece)

    def result_columns(source):
        return pl.ds(pl.multiple_of(source * width, width), width)

    def gated_rows(block, p):
        return gated_ref.at[pl.ds(pl.multiple_of(block * rows + p * piece, piece), piece), :]

    def give(block, p):
        return remote(gated_rows(block, p), out_ref.at[result_rows(p), result_columns(seq)],
                      out_send.at[block], out_recv.at[seq], {"seq": block})

    def take(source):
        here = out_ref.at[:, result_columns(source)]
        return remote(here, here, out_send.at[source], out_recv.at[source], {"seq": source})

    def keep(p):
        return pltpu.make_async_copy(
            gated_rows(seq, p), out_ref.at[result_rows(p), result_columns(seq)], own_sem.at[0]
        )

    def inside(other):
        return (other >= 0) & (other < count)

    def pick(values, index):
        found = values[0]
        for n in range(1, len(values)):
            found = jnp.where(index == n, values[n], found)
        return found

    def by_plane(table, index):
        flat = [value for row in table for value in row]
        return pick(flat, seq * len(table[0]) + index)

    orders = block_orders(count)
    ready = reach_table(orders)
    is_first, is_last = seq == 0, seq == count - 1
    is_end = is_first | is_last
    deferred = (seq == 1) if count == 4 else (seq == count)

    for fill in fills:
        fill.start()
    pl.semaphore_wait(barrier, count - 1 + len(mates))

    def send_weights(way, distances):
        for distance in distances:
            other = seq + way * distance

            @pl.when(inside(other))
            def _():
                for m in range(3):
                    spread(other, m).start()

    def send_own(way):
        for p in range(PIECES):
            hop(seq, p, way, own_piece(p)).start()

    for way, at_end in ((1, is_first), (-1, is_last)):
        @pl.when(at_end)
        def _():
            send_weights(way, (1,))
            send_own(way)
            send_weights(way, range(count - 1, 1, -1))

        @pl.when(jnp.logical_not(at_end) & inside(seq + way))
        def _():
            send_weights(way, range(count - 1, 0, -1))
            if way == 1:
                @pl.when(jnp.logical_not(deferred))
                def _():
                    send_own(way)
            else:
                send_own(way)

    for p in range(PIECES):
        side(seq, p, own_piece(p)).start()
        core(seq, 0, p, own_piece(p)).start()

    def relay(block, p):
        way = jnp.where(block < seq, 1, -1)
        hop(block, p, way).wait_recv()

        @pl.when(inside(seq + way))
        def _():
            hop(block, p, way).start()

        side(block, p).start()
        core(block, 0, p).start()

    def pass_side(block, p):
        side_arrival(block, p).wait_recv()
        core(block, 1, p).start()

    def pass_weights(other, m):
        @pl.when(inside(other))
        def _():
            spread_arrival(other, m).wait_recv()
            swap(other, m).start()

    toward = jnp.where(2 * seq < count, -1, 1)
    side_lag = jnp.where(is_end, SIDE_LAG[0], SIDE_LAG[1])
    lag = jnp.where(is_end, LAG[0], LAG[1])
    shift = jnp.where(is_end, 0, SHIFT)
    first_block = by_plane(orders, 0)

    far, between = count - 1, range(count - 2, 1, -1)

    @pl.when(is_end)
    def _():
        for m in range(3):
            pass_side(seq, m)
            for distance in between:
                pass_weights(seq - toward * distance, m)
        for p in range(3, PIECES):
            pass_side(seq, p)
        for m in range(3):
            pass_weights(seq - toward, m)
        relay(first_block, 0)
        if far > 1:
            for m in range(3):
                pass_weights(seq - toward * far, m)
        for p in range(1, PIECES):
            relay(first_block, p)

    @pl.when(jnp.logical_not(is_end))
    def _():
        for m in range(3):
            pass_weights(seq + toward, m)
            pass_side(seq, m)
        for p in range(3, PIECES):
            pass_side(seq, p)
        for p in range(PIECES):
            relay(first_block, p)
            if p < 3:
                pass_weights(seq - toward, p)

        @pl.when(deferred)
        def _():
            send_own(1)

        for p in range(PIECES - SIDE_LAG[1]):
            pass_side(first_block, p)
        for m in range(3):
            if m == 2:
                relay(by_plane(orders, 1), 0)
            for distance in between:
                pass_weights(seq - toward * distance, m)
                pass_weights(seq + toward * distance, m)

    for p in range(PIECES - SIDE_LAG[0]):
        @pl.when(is_end)
        def _():
            pass_side(first_block, p)

    for fill in fills:
        fill.wait()

    scale_ref[...] = jnp.sqrt(one_less_exp(2.0 * rate_ref[...]))
    lane_groups = width // LANES
    chunk = piece // CHUNKS
    step_ref[...] = jnp.exp(-rate_ref[...] * chunk)
    for group in range(lane_groups):
        lanes = pl.ds(group * LANES, LANES)
        decay = jnp.exp(-rate_ref[:, lanes])
        weight = residue_ref[:, lanes] * scale_ref[:, lanes]
        for m in range(modes):
            decay_ref[group, m] = jnp.broadcast_to(decay[m : m + 1, :], (CHUNKS, LANES))
            weight_ref[group, m] = jnp.broadcast_to(weight[m : m + 1, :], (CHUNKS, LANES))

    def project(block, p):
        core_arrivals(block, p).wait_recv()
        top = pl.ds(pl.multiple_of(block * rows + p * piece, piece), piece)
        found = jnp.dot(all_ref[top, :], weights_ref[...], preferred_element_type=jnp.float32)
        found = found.astype(jnp.bfloat16)
        query_rows[top, :] = found[:, :width]
        product = (
            found[:, width : 2 * width].astype(jnp.float32) * found[:, 2 * width :].astype(jnp.float32)
        )
        product = product.astype(jnp.bfloat16).astype(jnp.float32)
        for group in range(lane_groups):
            signal[group, top, :] = product[:, group * LANES : (group + 1) * LANES]

    def scan(g, _):
        block, p = g // PIECES, lax.rem(g, PIECES)
        top = pl.multiple_of(g * piece, piece)
        for group in range(lane_groups):
            lanes = pl.ds(group * LANES, LANES)
            residues = residue_ref[:, lanes]
            scale = scale_ref[:, lanes]
            chunk_decay = step_ref[:, lanes]
            decays = [decay_ref[group, m] for m in range(modes)]
            weights = [weight_ref[group, m] for m in range(modes)]

            def sums(step, states):
                here = signal[group, pl.ds(top + step, CHUNKS, stride=chunk), :]
                return tuple(d * s + here for d, s in zip(decays, states))

            zero = jnp.zeros((CHUNKS, LANES), jnp.float32)
            finals = lax.fori_loop(0, chunk, sums, (zero,) * modes, unroll=UNROLL)
            for m in range(modes):
                ends[pl.ds(m, CHUNKS, stride=modes), :] = finals[m]
            state = carried_ref[:, lanes]
            for c in range(CHUNKS):
                at = pl.ds(c * modes, modes)
                entering[at, :] = residues * state
                state = chunk_decay * state + scale * ends[at, :]
            carried_ref[:, lanes] = state

            def outputs(step, states):
                here = signal[group, pl.ds(top + step, CHUNKS, stride=chunk), :]
                states = tuple(d * s + w * here for d, s, w in zip(decays, states, weights))
                terms = list(states)
                while len(terms) > 1:
                    terms = [a + b for a, b in zip(terms[::2], terms[1::2])] + (
                        [terms[-1]] if len(terms) % 2 else []
                    )
                conv[group, pl.ds(step, CHUNKS, stride=chunk), :] = terms[0]
                return states

            starts = tuple(entering[pl.ds(m, CHUNKS, stride=modes), :] for m in range(modes))
            lax.fori_loop(0, chunk, outputs, starts, unroll=UNROLL)
            rounded = conv[group].astype(jnp.bfloat16).astype(jnp.float32)
            gated_ref[pl.ds(top, piece), lanes] = (
                query_rows[pl.ds(top, piece), lanes].astype(jnp.float32) * rounded
            ).astype(jnp.bfloat16)

        @pl.when(block == seq)
        def _():
            keep(p).start()

        return 0

    def scan_and_send(g, k):
        scan(g, 0)

        block = g // PIECES

        @pl.when((block != seq) & (k >= release(block)))
        def _():
            give(block, lax.rem(g, PIECES)).start()

        return k

    releases = release_table(count)

    def release(block):
        return by_plane(releases, block)

    def send_held(g, k):
        block = g // PIECES

        @pl.when((block != seq) & (release(block) == k))
        def _():
            give(block, lax.rem(g, PIECES)).start()

        return k

    last = (count - 1) * PIECES

    def block_of(k):
        return by_plane(orders, k // PIECES)

    def slot(k, _):
        @pl.when((k < last) & (is_end | (k > PIECES)))
        def _():
            relay(block_of(k), lax.rem(k, PIECES))

        @pl.when(k == PIECES + shift)
        def _():
            for distance in range(1, count):
                for other in (seq - distance, seq + distance):
                    @pl.when(inside(other))
                    def _():
                        swapped(other).wait_recv()

        def next_side():
            pass_side(block_of(k - side_lag), lax.rem(k - side_lag, PIECES))

        first = is_end & (k > last)

        @pl.when(first & (k < last + side_lag))
        def _():
            next_side()

        def one(which, _):
            early = which < 2
            n = jnp.where(early, k - PIECES - shift, k - lag)
            block = jnp.where(which == 0, seq, jnp.where(which == 1, first_block, block_of(k - lag)))
            known = (early & (n >= 0) & (n < PIECES)) | (jnp.logical_not(early) & (n >= PIECES) & (n < last))

            @pl.when(known)
            def _():
                project(block, lax.rem(n, PIECES))

            return 0

        lax.fori_loop(0, 3, one, 0)
        done, reach = by_plane(ready, k - PIECES), by_plane(ready, k - PIECES + 1)
        lax.fori_loop(done, reach, scan_and_send, k)

        @pl.when((k >= last - 2) & (k <= last + 1))
        def _():
            lax.fori_loop(0, done, send_held, k)

        @pl.when(jnp.logical_not(first) & (k < last + side_lag))
        def _():
            next_side()

        return 0

    lax.fori_loop(PIECES, last + LAG[1], slot, 0)
    state_ref[...] = carried_ref[...]

    @pl.when(seq > 0)
    def _():
        sent(hop_send.at[seq, 1], seq, 1).wait_send()

    @pl.when(seq + 1 < count)
    def _():
        sent(hop_send.at[seq, 0], seq, 1).wait_send()

    sent(side_send.at[seq], seq, 1).wait_send()
    sent(core_send.at[seq], seq, 2).wait_send()
    others = [
        (other, way)
        for distance in range(1, count)
        for other, way in ((seq - distance, 1), (seq + distance, -1))
    ]
    for other, way in others:
        @pl.when(inside(other))
        def _():
            @pl.when(inside(seq + way))
            def _():
                sent(hop_send.at[other, (1 - way) // 2], other, 1).wait_send()

            sent(side_send.at[other], other, 1).wait_send()
            sent(core_send.at[other], other, 2).wait_send()
            spread_out(other).wait_send()
            swapped(other).wait_send()
    kept = out_ref.at[:, result_columns(seq)]
    pltpu.make_async_copy(kept, kept, own_sem.at[0]).wait()
    for other, way in others:
        @pl.when(inside(other))
        def _():
            take(other).wait_send()
    for other, way in others:
        @pl.when(inside(other))
        def _():
            take(other).wait_recv()


def whole_layer(tokens, w_query, w_key, w_value, rate, residue, carried, count):
    rows, columns = tokens.shape
    depth, outer = w_query.shape
    width, modes = rate.shape
    length = rows * count
    vmem = pl.BlockSpec(memory_space=pltpu.VMEM)
    anywhere = pl.BlockSpec(memory_space=pl.ANY)
    dma = pltpu.SemaphoreType.DMA
    table = pltpu.VMEM((modes, width), jnp.float32)
    operands = (tokens, w_query, w_key, w_value, rate.T, residue.T, carried.T)
    gated, state = pl.pallas_call(
        functools.partial(layer_kernel, count),
        out_shape=(
            jax.ShapeDtypeStruct((rows, outer), jnp.bfloat16),
            jax.ShapeDtypeStruct((modes, width), jnp.float32),
        ),
        in_specs=[anywhere] * 7,
        out_specs=(anywhere, vmem),
        scratch_shapes=[
            pltpu.VMEM((length, columns * 4), jnp.bfloat16),
            pltpu.VMEM((depth * count, 3 * width), jnp.bfloat16),
            pltpu.VMEM((length, width), jnp.bfloat16),
            pltpu.VMEM((width // LANES, length, LANES), jnp.float32),
            pltpu.VMEM((width // LANES, rows // PIECES, LANES), jnp.float32),
            pltpu.VMEM((length, width), jnp.bfloat16),
            pltpu.VMEM((CHUNKS * modes, LANES), jnp.float32),
            pltpu.VMEM((CHUNKS * modes, LANES), jnp.float32),
        ] + [table] * 4 + [
            pltpu.VMEM((width // LANES, modes, CHUNKS, LANES), jnp.float32),
            pltpu.VMEM((width // LANES, modes, CHUNKS, LANES), jnp.float32),
            table,
            dma((7,)),
            dma((count, 2)), dma((count, PIECES)),
            dma((count,)), dma((count, PIECES)),
            dma((count,)), dma((count, PIECES)),
            dma((count,)), dma((count,)),
            dma((count,)), dma((count, 3)),
            dma((count,)), dma((count,)),
            dma((1,)),
        ],
        compiler_params=pltpu.CompilerParams(
            collective_id=0, has_side_effects=True, vmem_limit_bytes=40 * 2**20
        ),
    )(*(pltpu.with_memory_space_constraint(array, pltpu.HBM) for array in operands))
    return gated, state.T


def per_device_channels(tokens, w_query, w_key, w_value, decay_rate, residue, carried):
    count = lax.axis_size("seq")
    return whole_layer(tokens, w_query, w_key, w_value, decay_rate, residue, carried, count)


def solution(mesh):
    in_specs = (
        P(("parts", "seq"), ("chan", "rep")),
        P("seq", ("chan", "rep")),
        P("seq", ("chan", "rep")),
        P("seq", ("chan", "rep")),
        P(("chan", "rep", "seq"), None),
        P(("chan", "rep", "seq"), None),
        P(("parts", "chan", "rep", "seq"), None),
    )
    out_specs = (P(("parts", "seq"), ("chan", "rep")), P(("parts", "chan", "rep", "seq"), None))

    def body(*arrays):
        own_channels = arrays[4].shape[0]
        mates = all(mesh.shape[a] == 2 for a in ("parts", "chan", "rep"))
        chosen = per_device_channels if own_channels % LANES == 0 and mates else per_device
        return chosen(*arrays)

    return jax.shard_map(body, mesh=mesh, in_specs=in_specs, out_specs=out_specs, check_vma=False)
```

```python
import functools

import jax
import jax.numpy as jnp
from jax import lax
from jax.experimental import pallas as pl
from jax.experimental.pallas import tpu as pltpu
from jax.sharding import PartitionSpec as P

BLOCK = 128
LANES = 128
CHUNKS = 8
MESH = pl.DeviceIdType.MESH


HIGHEST_PRECISION = lax.Precision.HIGHEST


def mode_scale(decay_rates):
    return jnp.sqrt(-jnp.expm1(-2.0 * decay_rates))


def local_ends(blocks, decay_rates):
    block_width = blocks.shape[2]
    offsets = jnp.arange(block_width, dtype=jnp.float32)
    tail_powers = jnp.exp(-decay_rates[:, :, None] * (block_width - 1.0 - offsets)[None, None, :])
    sums_here = jnp.einsum("cnb,cmb->cnm", blocks, tail_powers, precision=HIGHEST_PRECISION)
    return mode_scale(decay_rates)[:, None, :] * sums_here


def combine_states(earlier, later):
    return (earlier[0] * later[0], later[0] * earlier[1] + later[1])


def block_sums(block_ends, decay_rates, block_width):
    step_decay = jnp.broadcast_to(jnp.exp(-decay_rates * block_width)[:, None, :], block_ends.shape)
    unused_decay, running = lax.associative_scan(combine_states, (step_decay, block_ends), axis=1)
    return running


def entering_states(running, decay_rates, start_state, block_width):
    count_blocks = running.shape[1]
    block_starts = jnp.arange(count_blocks, dtype=jnp.float32) * block_width
    decayed = (
        jnp.exp(-decay_rates[:, None, :] * block_starts[None, :, None]) * start_state[:, None, :]
    )
    earlier_sums = jnp.concatenate([jnp.zeros_like(running[:, :1]), running[:, :-1]], axis=1)
    final_state = (
        jnp.exp(-decay_rates * (count_blocks * block_width)) * start_state + running[:, -1]
    )
    return (decayed + earlier_sums, final_state)


def block_convolve(blocks, decay_rates, residues, entering):
    block_width = blocks.shape[2]
    offsets = jnp.arange(block_width, dtype=jnp.float32)
    powers = jnp.exp(-decay_rates[:, :, None] * offsets[None, None, :])
    kernel = jnp.sum((residues * mode_scale(decay_rates))[:, :, None] * powers, axis=1)
    out_index = jnp.arange(block_width, dtype=jnp.int32)[:, None]
    in_index = jnp.arange(block_width, dtype=jnp.int32)[None, :]
    lag = jnp.maximum(out_index - in_index, 0)
    causal = (out_index >= in_index).astype(jnp.float32)
    toeplitz = kernel[:, lag] * causal[None, :, :]
    direct = jnp.einsum("cij,cnj->cni", toeplitz, blocks, precision=HIGHEST_PRECISION)
    leading = residues[:, :, None] * jnp.exp(
        -decay_rates[:, :, None] * (offsets + 1.0)[None, None, :]
    )
    return direct + jnp.einsum("cnm,cmb->cnb", entering, leading, precision=HIGHEST_PRECISION)


def per_device(tokens, w_query, w_key, w_value, decay_rate, residue, carried):
    gathered = lax.all_gather(tokens, ("chan", "rep"), axis=1, tiled=True)
    pieces = (
        lax.all_gather(w_query, "seq", axis=0, tiled=True),
        lax.all_gather(w_key, "seq", axis=0, tiled=True),
        lax.all_gather(w_value, "seq", axis=0, tiled=True),
    )
    query_acc, key_acc, value_acc = tuple(
        (
            lax.dot_general(
                weight_piece, gathered, (((0,), (1,)), ((), ())), preferred_element_type=jnp.float32
            )
            for weight_piece in pieces
        )
    )
    query_rows = query_acc.astype(jnp.bfloat16)
    key_rows = key_acc.astype(jnp.bfloat16)
    value_rows = value_acc.astype(jnp.bfloat16)
    query_rows, key_rows, value_rows = lax.optimization_barrier((query_rows, key_rows, value_rows))
    product = (key_rows.astype(jnp.float32) * value_rows.astype(jnp.float32)).astype(jnp.bfloat16)
    owned = lax.all_to_all(product, "seq", split_axis=0, concat_axis=1, tiled=True)
    own_chan = owned.shape[0]
    blocks = owned.astype(jnp.float32).reshape(own_chan, -1, BLOCK)
    block_end = local_ends(blocks, decay_rate)
    running = block_sums(block_end, decay_rate, BLOCK)
    entering, new_state = entering_states(running, decay_rate, carried, BLOCK)
    conv_out = (
        block_convolve(blocks, decay_rate, residue, entering)
        .reshape(own_chan, -1)
        .astype(jnp.bfloat16)
    )
    conv_back = lax.all_to_all(conv_out, "seq", split_axis=1, concat_axis=0, tiled=True)
    conv_back = lax.optimization_barrier(conv_back)
    gated_rows = (query_rows.astype(jnp.float32) * conv_back.astype(jnp.float32)).astype(
        jnp.bfloat16
    )
    return (gated_rows.T, new_state)


PIECES = 4
SIDE_LAG = (1, 1)
LAG = (2, 2)
SHIFT = 1
CAP = 3
UNROLL = 8


def block_orders(count):
    if count == 4:
        return ((1, 2, 3), (0, 2, 3), (3, 0, 1), (2, 0, 1))
    return tuple(
        tuple(sorted((b for b in range(count) if b != z), key=lambda b: (abs(b - z), b)))
        for z in range(count)
    )


def one_less_exp(x):
    series = jnp.ones_like(x)
    for n in range(9, 1, -1):
        series = 1.0 - series * x * (1.0 / n)
    return jnp.where(x < 0.25, x * series, 1.0 - jnp.exp(-x))


def release_table(count):
    if count != 4:
        return ((0,) * count,) * count
    last = (count - 1) * PIECES
    return (
        (0, 0, last - 2, 0),
        (last - 1, 0, last + 1, last - 1),
        (last, 0, 0, last - 1),
        (last - 1, 0, 0, 0),
    )


def reach_table(orders):
    count = len(orders)
    last = (count - 1) * PIECES
    table = []
    for z, order in enumerate(orders):
        when = {}
        for p in range(PIECES):
            when[z, p] = when[order[0], p] = PIECES + p + (0 if z in (0, count - 1) else SHIFT)
            for n in range(1, count - 1):
                when[order[n], p] = n * PIECES + p + LAG[0 if z in (0, count - 1) else 1]
        row = [0]
        for k in range(PIECES, last + LAG[1]):
            g = row[-1]
            top = g + CAP if k < last else count * PIECES
            while g < min(top, count * PIECES) and when[divmod(g, PIECES)] <= k:
                g += 1
            row.append(g)
        table.append(row)
    return table


def layer_kernel(count, tokens_ref, query_ref, key_ref, value_ref, rate_hbm, residue_hbm,
                 carried_hbm, out_ref, state_ref,
                 all_ref, weights_ref, query_rows, signal, conv, gated_ref, ends, entering,
                 rate_ref, scale_ref, residue_ref, carried_ref, decay_ref, weight_ref, step_ref,
                 fill_sem, hop_send, hop_recv, side_send, side_recv, core_send, core_recv,
                 part_send, part_recv, layer_send, layer_recv, out_send, out_recv, own_sem):
    part, seq, chan, rep = (lax.axis_index(a) for a in ("parts", "seq", "chan", "rep"))
    rows, columns = tokens_ref.shape
    depth, outer = query_ref.shape
    width = outer // count
    half = depth // 2
    piece = rows // PIECES
    modes = rate_ref.shape[0]
    own_columns = pl.ds(pl.multiple_of(seq * width, width), width)
    matrices = (query_ref, key_ref, value_ref)

    barrier = pltpu.get_barrier_semaphore()
    mates = ({"parts": 1 - part}, {"chan": 1 - chan}, {"rep": 1 - rep})
    for mate in mates:
        pl.semaphore_signal(barrier, inc=1, device_id=mate, device_id_type=MESH)
    for step in range(1, count):
        pl.semaphore_signal(
            barrier, inc=1, device_id={"seq": lax.rem(seq + step, count)}, device_id_type=MESH
        )

    fills = [
        pltpu.make_async_copy(
            tokens_ref,
            all_ref.at[pl.ds(pl.multiple_of(seq * rows, rows), rows),
                       pl.ds(pl.multiple_of((chan * 2 + rep) * columns, columns), columns)],
            fill_sem.at[0])
    ] + [
        pltpu.make_async_copy(
            matrices[m].at[:, own_columns],
            weights_ref.at[pl.ds(pl.multiple_of(seq * depth, depth), depth), pl.ds(m * width, width)],
            fill_sem.at[1 + m])
        for m in range(3)
    ] + [
        pltpu.make_async_copy(source, target, fill_sem.at[4 + n])
        for n, (source, target) in enumerate((
            (rate_hbm, rate_ref), (residue_hbm, residue_ref), (carried_hbm, carried_ref),
        ))
    ]

    def remote(source, target, send, recv, device):
        return pltpu.make_async_remote_copy(
            src_ref=source, dst_ref=target, send_sem=send, recv_sem=recv,
            device_id=device, device_id_type=MESH,
        )

    def token_block(block, side, core, p):
        top = pl.multiple_of(block * rows + p * piece, piece)
        left = pl.multiple_of((side * 2 + core) * columns, columns)
        return all_ref.at[pl.ds(top, piece), pl.ds(left, columns)]

    def own_piece(p):
        return tokens_ref.at[pl.ds(p * piece, piece), :]

    def hop(block, p, way, source=None):
        here = token_block(block, chan, rep, p)
        return remote(here if source is None else source, here,
                      hop_send.at[block, (1 - way) // 2], hop_recv.at[block, p], {"seq": seq + way})

    def side(block, p, source=None):
        here = token_block(block, chan, rep, p)
        return remote(here if source is None else source, here,
                      side_send.at[block], side_recv.at[block, p], {"chan": 1 - chan})

    def side_arrival(block, p):
        there = token_block(block, 1 - chan, rep, p)
        return remote(there, there, side_send.at[block], side_recv.at[block, p], {"chan": 1 - chan})

    def core(block, which, p, source=None):
        here = token_block(block, chan if which == 0 else 1 - chan, rep, p)
        return remote(here if source is None else source, here,
                      core_send.at[block], core_recv.at[block, p], {"rep": 1 - rep})

    def core_arrivals(block, p):
        top = pl.multiple_of(block * rows + p * piece, piece)
        there = all_ref.at[pl.ds(top, piece), pl.ds(0, 2 * columns)]
        return remote(there, there, core_send.at[block], core_recv.at[block, p], {"rep": 1 - rep})

    def sent(semaphore, other, wide):
        there = all_ref.at[pl.ds(0, rows), pl.ds(0, wide * columns)]
        return remote(there, there, semaphore, hop_recv.at[other, 0], {"rep": 1 - rep})

    def swapped(other):
        there = weights_ref.at[pl.ds(pl.multiple_of(other * depth + (1 - part) * half, half), half), :]
        return remote(there, there, part_send.at[other], part_recv.at[other], {"parts": 1 - part})

    def spread_out(other):
        there = weights_ref.at[pl.ds(pl.multiple_of(other * depth + part * half, half), half), :]
        return remote(there, there, layer_send.at[other], layer_recv.at[other, 0], {"seq": other})

    def weight_block(block, m, part_of):
        top = pl.multiple_of(block * depth + part_of * half, half)
        return weights_ref.at[pl.ds(top, half), pl.ds(m * width, width)]

    def spread(target, m):
        source = matrices[m].at[
            pl.ds(pl.multiple_of(part * half, half), half),
            pl.ds(pl.multiple_of(target * width, width), width),
        ]
        return remote(source, weight_block(seq, m, part),
                      layer_send.at[target], layer_recv.at[seq, m], {"seq": target})

    def spread_arrival(block, m):
        here = weight_block(block, m, part)
        return remote(here, here, layer_send.at[block], layer_recv.at[block, m], {"seq": block})

    def swap(block, m):
        here = weight_block(block, m, part)
        return remote(here, here, part_send.at[block], part_recv.at[block], {"parts": 1 - part})

    def result_rows(p):
        return pl.ds(pl.multiple_of(p * piece, piece), piece)

    def result_columns(source):
        return pl.ds(pl.multiple_of(source * width, width), width)

    def gated_rows(block, p):
        return gated_ref.at[pl.ds(pl.multiple_of(block * rows + p * piece, piece), piece), :]

    def give(block, p):
        return remote(gated_rows(block, p), out_ref.at[result_rows(p), result_columns(seq)],
                      out_send.at[block], out_recv.at[seq], {"seq": block})

    def take(source):
        here = out_ref.at[:, result_columns(source)]
        return remote(here, here, out_send.at[source], out_recv.at[source], {"seq": source})

    def keep(p):
        return pltpu.make_async_copy(
            gated_rows(seq, p), out_ref.at[result_rows(p), result_columns(seq)], own_sem.at[0]
        )

    def inside(other):
        return (other >= 0) & (other < count)

    def pick(values, index):
        found = values[0]
        for n in range(1, len(values)):
            found = jnp.where(index == n, values[n], found)
        return found

    def by_plane(table, index):
        flat = [value for row in table for value in row]
        return pick(flat, seq * len(table[0]) + index)

    orders = block_orders(count)
    ready = reach_table(orders)
    is_first, is_last = seq == 0, seq == count - 1
    is_end = is_first | is_last
    deferred = (seq == 1) if count == 4 else (seq == count)

    for fill in fills:
        fill.start()
    pl.semaphore_wait(barrier, count - 1 + len(mates))

    def send_weights(way, distances):
        for distance in distances:
            other = seq + way * distance

            @pl.when(inside(other))
            def _():
                for m in range(3):
                    spread(other, m).start()

    def send_own(way):
        for p in range(PIECES):
            hop(seq, p, way, own_piece(p)).start()

    for way, at_end in ((1, is_first), (-1, is_last)):
        @pl.when(at_end)
        def _():
            send_weights(way, (1,))
            send_own(way)
            send_weights(way, range(count - 1, 1, -1))

        @pl.when(jnp.logical_not(at_end) & inside(seq + way))
        def _():
            send_weights(way, range(count - 1, 0, -1))
            if way == 1:
                @pl.when(jnp.logical_not(deferred))
                def _():
                    send_own(way)
            else:
                send_own(way)

    for p in range(PIECES):
        side(seq, p, own_piece(p)).start()
        core(seq, 0, p, own_piece(p)).start()

    def relay(block, p):
        way = jnp.where(block < seq, 1, -1)
        hop(block, p, way).wait_recv()

        @pl.when(inside(seq + way))
        def _():
            hop(block, p, way).start()

        side(block, p).start()
        core(block, 0, p).start()

    def pass_side(block, p):
        side_arrival(block, p).wait_recv()
        core(block, 1, p).start()

    def pass_weights(other, m):
        @pl.when(inside(other))
        def _():
            spread_arrival(other, m).wait_recv()
            swap(other, m).start()

    toward = jnp.where(2 * seq < count, -1, 1)
    side_lag = jnp.where(is_end, SIDE_LAG[0], SIDE_LAG[1])
    lag = jnp.where(is_end, LAG[0], LAG[1])
    shift = jnp.where(is_end, 0, SHIFT)
    first_block = by_plane(orders, 0)

    far, between = count - 1, range(count - 2, 1, -1)

    @pl.when(is_end)
    def _():
        for m in range(3):
            pass_side(seq, m)
            for distance in between:
                pass_weights(seq - toward * distance, m)
        for p in range(3, PIECES):
            pass_side(seq, p)
        for m in range(3):
            pass_weights(seq - toward, m)
        relay(first_block, 0)
        if far > 1:
            for m in range(3):
                pass_weights(seq - toward * far, m)
        for p in range(1, PIECES):
            relay(first_block, p)

    @pl.when(jnp.logical_not(is_end))
    def _():
        for m in range(3):
            pass_weights(seq + toward, m)
            pass_side(seq, m)
        for p in range(3, PIECES):
            pass_side(seq, p)
        for p in range(PIECES):
            relay(first_block, p)
            if p < 3:
                pass_weights(seq - toward, p)

        @pl.when(deferred)
        def _():
            send_own(1)

        for p in range(PIECES - SIDE_LAG[1]):
            pass_side(first_block, p)
        for m in range(3):
            if m == 2:
                relay(by_plane(orders, 1), 0)
            for distance in between:
                pass_weights(seq - toward * distance, m)
                pass_weights(seq + toward * distance, m)

    for p in range(PIECES - SIDE_LAG[0]):
        @pl.when(is_end)
        def _():
            pass_side(first_block, p)

    for fill in fills:
        fill.wait()

    scale_ref[...] = jnp.sqrt(one_less_exp(2.0 * rate_ref[...]))
    lane_groups = width // LANES
    chunk = piece // CHUNKS
    step_ref[...] = jnp.exp(-rate_ref[...] * chunk)
    for group in range(lane_groups):
        lanes = pl.ds(group * LANES, LANES)
        decay = jnp.exp(-rate_ref[:, lanes])
        weight = residue_ref[:, lanes] * scale_ref[:, lanes]
        for m in range(modes):
            decay_ref[group, m] = jnp.broadcast_to(decay[m : m + 1, :], (CHUNKS, LANES))
            weight_ref[group, m] = jnp.broadcast_to(weight[m : m + 1, :], (CHUNKS, LANES))

    def project(block, p):
        core_arrivals(block, p).wait_recv()
        top = pl.ds(pl.multiple_of(block * rows + p * piece, piece), piece)
        found = jnp.dot(all_ref[top, :], weights_ref[...], preferred_element_type=jnp.float32)
        found = found.astype(jnp.bfloat16)
        query_rows[top, :] = found[:, :width]
        product = (
            found[:, width : 2 * width].astype(jnp.float32) * found[:, 2 * width :].astype(jnp.float32)
        )
        product = product.astype(jnp.bfloat16).astype(jnp.float32)
        for group in range(lane_groups):
            signal[group, top, :] = product[:, group * LANES : (group + 1) * LANES]

    def scan(g, _):
        block, p = g // PIECES, lax.rem(g, PIECES)
        top = pl.multiple_of(g * piece, piece)
        for group in range(lane_groups):
            lanes = pl.ds(group * LANES, LANES)
            residues = residue_ref[:, lanes]
            scale = scale_ref[:, lanes]
            chunk_decay = step_ref[:, lanes]
            decays = [decay_ref[group, m] for m in range(modes)]
            weights = [weight_ref[group, m] for m in range(modes)]

            def sums(step, states):
                here = signal[group, pl.ds(top + step, CHUNKS, stride=chunk), :]
                return tuple(d * s + here for d, s in zip(decays, states))

            zero = jnp.zeros((CHUNKS, LANES), jnp.float32)
            finals = lax.fori_loop(0, chunk, sums, (zero,) * modes, unroll=UNROLL)
            for m in range(modes):
                ends[pl.ds(m, CHUNKS, stride=modes), :] = finals[m]
            state = carried_ref[:, lanes]
            for c in range(CHUNKS):
                at = pl.ds(c * modes, modes)
                entering[at, :] = residues * state
                state = chunk_decay * state + scale * ends[at, :]
            carried_ref[:, lanes] = state

            def outputs(step, states):
                here = signal[group, pl.ds(top + step, CHUNKS, stride=chunk), :]
                states = tuple(d * s + w * here for d, s, w in zip(decays, states, weights))
                terms = list(states)
                while len(terms) > 1:
                    terms = [a + b for a, b in zip(terms[::2], terms[1::2])] + (
                        [terms[-1]] if len(terms) % 2 else []
                    )
                conv[group, pl.ds(step, CHUNKS, stride=chunk), :] = terms[0]
                return states

            starts = tuple(entering[pl.ds(m, CHUNKS, stride=modes), :] for m in range(modes))
            lax.fori_loop(0, chunk, outputs, starts, unroll=UNROLL)
            rounded = conv[group].astype(jnp.bfloat16).astype(jnp.float32)
            gated_ref[pl.ds(top, piece), lanes] = (
                query_rows[pl.ds(top, piece), lanes].astype(jnp.float32) * rounded
            ).astype(jnp.bfloat16)

        @pl.when(block == seq)
        def _():
            keep(p).start()

        return 0

    def scan_and_send(g, k):
        scan(g, 0)

        block = g // PIECES

        @pl.when((block != seq) & (k >= release(block)))
        def _():
            give(block, lax.rem(g, PIECES)).start()

        return k

    releases = release_table(count)

    def release(block):
        return by_plane(releases, block)

    def send_held(k, done):
        for block in range(count):
            due = pick([row[block] for row in releases], seq)

            @pl.when((seq != block) & (due == k))
            def _():
                def send(p, _):
                    @pl.when(block * PIECES + p < done)
                    def _():
                        give(block, p).start()

                    return 0

                lax.fori_loop(0, PIECES, send, 0)

    last = (count - 1) * PIECES

    def block_of(k):
        return by_plane(orders, k // PIECES)

    def slot(k, _):
        @pl.when((k < last) & (is_end | (k > PIECES)))
        def _():
            relay(block_of(k), lax.rem(k, PIECES))

        @pl.when(k == PIECES + shift)
        def _():
            for distance in range(1, count):
                for other in (seq - distance, seq + distance):
                    @pl.when(inside(other))
                    def _():
                        swapped(other).wait_recv()

        def next_side():
            pass_side(block_of(k - side_lag), lax.rem(k - side_lag, PIECES))

        first = is_end & (k > last)

        @pl.when(first & (k < last + side_lag))
        def _():
            next_side()

        def one(which, _):
            early = which < 2
            n = jnp.where(early, k - PIECES - shift, k - lag)
            block = jnp.where(which == 0, seq, jnp.where(which == 1, first_block, block_of(k - lag)))
            known = (early & (n >= 0) & (n < PIECES)) | (jnp.logical_not(early) & (n >= PIECES) & (n < last))

            @pl.when(known)
            def _():
                project(block, lax.rem(n, PIECES))

            return 0

        lax.fori_loop(0, 3, one, 0)
        done, reach = by_plane(ready, k - PIECES), by_plane(ready, k - PIECES + 1)
        lax.fori_loop(done, reach, scan_and_send, k)

        @pl.when((k >= last - 2) & (k <= last + 1))
        def _():
            send_held(k, done)

        @pl.when(jnp.logical_not(first) & (k < last + side_lag))
        def _():
            next_side()

        return 0

    lax.fori_loop(PIECES, last + LAG[1], slot, 0)
    state_ref[...] = carried_ref[...]

    @pl.when(seq > 0)
    def _():
        sent(hop_send.at[seq, 1], seq, 1).wait_send()

    @pl.when(seq + 1 < count)
    def _():
        sent(hop_send.at[seq, 0], seq, 1).wait_send()

    sent(side_send.at[seq], seq, 1).wait_send()
    sent(core_send.at[seq], seq, 2).wait_send()
    others = [
        (other, way)
        for distance in range(1, count)
        for other, way in ((seq - distance, 1), (seq + distance, -1))
    ]
    for other, way in others:
        @pl.when(inside(other))
        def _():
            @pl.when(inside(seq + way))
            def _():
                sent(hop_send.at[other, (1 - way) // 2], other, 1).wait_send()

            sent(side_send.at[other], other, 1).wait_send()
            sent(core_send.at[other], other, 2).wait_send()
            spread_out(other).wait_send()
            swapped(other).wait_send()
    kept = out_ref.at[:, result_columns(seq)]
    pltpu.make_async_copy(kept, kept, own_sem.at[0]).wait()
    for other, way in others:
        @pl.when(inside(other))
        def _():
            take(other).wait_send()
    for other, way in others:
        @pl.when(inside(other))
        def _():
            take(other).wait_recv()


def whole_layer(tokens, w_query, w_key, w_value, rate, residue, carried, count):
    rows, columns = tokens.shape
    depth, outer = w_query.shape
    width, modes = rate.shape
    length = rows * count
    vmem = pl.BlockSpec(memory_space=pltpu.VMEM)
    anywhere = pl.BlockSpec(memory_space=pl.ANY)
    dma = pltpu.SemaphoreType.DMA
    table = pltpu.VMEM((modes, width), jnp.float32)
    operands = (tokens, w_query, w_key, w_value, rate.T, residue.T, carried.T)
    gated, state = pl.pallas_call(
        functools.partial(layer_kernel, count),
        out_shape=(
            jax.ShapeDtypeStruct((rows, outer), jnp.bfloat16),
            jax.ShapeDtypeStruct((modes, width), jnp.float32),
        ),
        in_specs=[anywhere] * 7,
        out_specs=(anywhere, vmem),
        scratch_shapes=[
            pltpu.VMEM((length, columns * 4), jnp.bfloat16),
            pltpu.VMEM((depth * count, 3 * width), jnp.bfloat16),
            pltpu.VMEM((length, width), jnp.bfloat16),
            pltpu.VMEM((width // LANES, length, LANES), jnp.float32),
            pltpu.VMEM((width // LANES, rows // PIECES, LANES), jnp.float32),
            pltpu.VMEM((length, width), jnp.bfloat16),
            pltpu.VMEM((CHUNKS * modes, LANES), jnp.float32),
            pltpu.VMEM((CHUNKS * modes, LANES), jnp.float32),
        ] + [table] * 4 + [
            pltpu.VMEM((width // LANES, modes, CHUNKS, LANES), jnp.float32),
            pltpu.VMEM((width // LANES, modes, CHUNKS, LANES), jnp.float32),
            table,
            dma((7,)),
            dma((count, 2)), dma((count, PIECES)),
            dma((count,)), dma((count, PIECES)),
            dma((count,)), dma((count, PIECES)),
            dma((count,)), dma((count,)),
            dma((count,)), dma((count, 3)),
            dma((count,)), dma((count,)),
            dma((1,)),
        ],
        compiler_params=pltpu.CompilerParams(
            collective_id=0, has_side_effects=True, vmem_limit_bytes=40 * 2**20
        ),
    )(*(pltpu.with_memory_space_constraint(array, pltpu.HBM) for array in operands))
    return settle(gated, state)


def settle_kernel(gated_ref, state_ref, out_ref, final_ref, sem):
    rows = gated_ref.shape[0]
    part = rows // PIECES
    copies = [
        pltpu.make_async_copy(
            gated_ref.at[pl.ds(p * part, part), :], out_ref.at[pl.ds(p * part, part), :], sem.at[p]
        )
        for p in range(PIECES)
    ] + [pltpu.make_async_copy(state_ref, final_ref, sem.at[PIECES])]
    for copy in copies:
        copy.start()
    for copy in copies:
        copy.wait()


def settle(gated, state):
    anywhere = pl.BlockSpec(memory_space=pl.ANY)
    out, final = pl.pallas_call(
        settle_kernel,
        out_shape=(
            jax.ShapeDtypeStruct(gated.shape, gated.dtype),
            jax.ShapeDtypeStruct(state.shape, state.dtype),
        ),
        in_specs=[anywhere] * 2,
        out_specs=(anywhere, anywhere),
        scratch_shapes=[pltpu.SemaphoreType.DMA((PIECES + 1,))],
        compiler_params=pltpu.CompilerParams(vmem_limit_bytes=2**20),
    )(gated, state)
    return out, final.T


def per_device_channels(tokens, w_query, w_key, w_value, decay_rate, residue, carried):
    count = lax.axis_size("seq")
    return whole_layer(tokens, w_query, w_key, w_value, decay_rate, residue, carried, count)


def solution(mesh):
    in_specs = (
        P(("parts", "seq"), ("chan", "rep")),
        P("seq", ("chan", "rep")),
        P("seq", ("chan", "rep")),
        P("seq", ("chan", "rep")),
        P(("chan", "rep", "seq"), None),
        P(("chan", "rep", "seq"), None),
        P(("parts", "chan", "rep", "seq"), None),
    )
    out_specs = (P(("parts", "seq"), ("chan", "rep")), P(("parts", "chan", "rep", "seq"), None))

    def body(*arrays):
        own_channels = arrays[4].shape[0]
        mates = all(mesh.shape[a] == 2 for a in ("parts", "chan", "rep"))
        chosen = per_device_channels if own_channels % LANES == 0 and mates else per_device
        return chosen(*arrays)

    return jax.shard_map(body, mesh=mesh, in_specs=in_specs, out_specs=out_specs, check_vma=False)
```

```python
import functools

import jax
import jax.numpy as jnp
from jax import lax
from jax.experimental import pallas as pl
from jax.experimental.pallas import tpu as pltpu
from jax.sharding import PartitionSpec as P

BLOCK = 128
LANES = 128
CHUNKS = 8
MESH = pl.DeviceIdType.MESH


HIGHEST_PRECISION = lax.Precision.HIGHEST


def mode_scale(decay_rates):
    return jnp.sqrt(-jnp.expm1(-2.0 * decay_rates))


def local_ends(blocks, decay_rates):
    block_width = blocks.shape[2]
    offsets = jnp.arange(block_width, dtype=jnp.float32)
    tail_powers = jnp.exp(-decay_rates[:, :, None] * (block_width - 1.0 - offsets)[None, None, :])
    sums_here = jnp.einsum("cnb,cmb->cnm", blocks, tail_powers, precision=HIGHEST_PRECISION)
    return mode_scale(decay_rates)[:, None, :] * sums_here


def combine_states(earlier, later):
    return (earlier[0] * later[0], later[0] * earlier[1] + later[1])


def block_sums(block_ends, decay_rates, block_width):
    step_decay = jnp.broadcast_to(jnp.exp(-decay_rates * block_width)[:, None, :], block_ends.shape)
    unused_decay, running = lax.associative_scan(combine_states, (step_decay, block_ends), axis=1)
    return running


def entering_states(running, decay_rates, start_state, block_width):
    count_blocks = running.shape[1]
    block_starts = jnp.arange(count_blocks, dtype=jnp.float32) * block_width
    decayed = (
        jnp.exp(-decay_rates[:, None, :] * block_starts[None, :, None]) * start_state[:, None, :]
    )
    earlier_sums = jnp.concatenate([jnp.zeros_like(running[:, :1]), running[:, :-1]], axis=1)
    final_state = (
        jnp.exp(-decay_rates * (count_blocks * block_width)) * start_state + running[:, -1]
    )
    return (decayed + earlier_sums, final_state)


def block_convolve(blocks, decay_rates, residues, entering):
    block_width = blocks.shape[2]
    offsets = jnp.arange(block_width, dtype=jnp.float32)
    powers = jnp.exp(-decay_rates[:, :, None] * offsets[None, None, :])
    kernel = jnp.sum((residues * mode_scale(decay_rates))[:, :, None] * powers, axis=1)
    out_index = jnp.arange(block_width, dtype=jnp.int32)[:, None]
    in_index = jnp.arange(block_width, dtype=jnp.int32)[None, :]
    lag = jnp.maximum(out_index - in_index, 0)
    causal = (out_index >= in_index).astype(jnp.float32)
    toeplitz = kernel[:, lag] * causal[None, :, :]
    direct = jnp.einsum("cij,cnj->cni", toeplitz, blocks, precision=HIGHEST_PRECISION)
    leading = residues[:, :, None] * jnp.exp(
        -decay_rates[:, :, None] * (offsets + 1.0)[None, None, :]
    )
    return direct + jnp.einsum("cnm,cmb->cnb", entering, leading, precision=HIGHEST_PRECISION)


def per_device(tokens, w_query, w_key, w_value, decay_rate, residue, carried):
    gathered = lax.all_gather(tokens, ("chan", "rep"), axis=1, tiled=True)
    pieces = (
        lax.all_gather(w_query, "seq", axis=0, tiled=True),
        lax.all_gather(w_key, "seq", axis=0, tiled=True),
        lax.all_gather(w_value, "seq", axis=0, tiled=True),
    )
    query_acc, key_acc, value_acc = tuple(
        (
            lax.dot_general(
                weight_piece, gathered, (((0,), (1,)), ((), ())), preferred_element_type=jnp.float32
            )
            for weight_piece in pieces
        )
    )
    query_rows = query_acc.astype(jnp.bfloat16)
    key_rows = key_acc.astype(jnp.bfloat16)
    value_rows = value_acc.astype(jnp.bfloat16)
    query_rows, key_rows, value_rows = lax.optimization_barrier((query_rows, key_rows, value_rows))
    product = (key_rows.astype(jnp.float32) * value_rows.astype(jnp.float32)).astype(jnp.bfloat16)
    owned = lax.all_to_all(product, "seq", split_axis=0, concat_axis=1, tiled=True)
    own_chan = owned.shape[0]
    blocks = owned.astype(jnp.float32).reshape(own_chan, -1, BLOCK)
    block_end = local_ends(blocks, decay_rate)
    running = block_sums(block_end, decay_rate, BLOCK)
    entering, new_state = entering_states(running, decay_rate, carried, BLOCK)
    conv_out = (
        block_convolve(blocks, decay_rate, residue, entering)
        .reshape(own_chan, -1)
        .astype(jnp.bfloat16)
    )
    conv_back = lax.all_to_all(conv_out, "seq", split_axis=1, concat_axis=0, tiled=True)
    conv_back = lax.optimization_barrier(conv_back)
    gated_rows = (query_rows.astype(jnp.float32) * conv_back.astype(jnp.float32)).astype(
        jnp.bfloat16
    )
    return (gated_rows.T, new_state)


PIECES = 4
SIDE_LAG = (1, 1)
LAG = (2, 2)
SHIFT = 0
CAP = 2
UNROLL = 8


def block_orders(count):
    if count == 4:
        return ((1, 2, 3), (0, 2, 3), (3, 0, 1), (2, 0, 1))
    return tuple(
        tuple(sorted((b for b in range(count) if b != z), key=lambda b: (abs(b - z), b)))
        for z in range(count)
    )


def one_less_exp(x):
    series = jnp.ones_like(x)
    for n in range(9, 1, -1):
        series = 1.0 - series * x * (1.0 / n)
    return jnp.where(x < 0.25, x * series, 1.0 - jnp.exp(-x))


def release_table(count):
    if count != 4:
        return ((0,) * count,) * count
    last = (count - 1) * PIECES
    return (
        (0, 0, last - 2, 0),
        (last - 1, 0, last + 1, last - 1),
        (last, 0, 0, last - 2),
        (last - 1, 0, 0, 0),
    )


def reach_table(orders):
    count = len(orders)
    last = (count - 1) * PIECES
    table = []
    for z, order in enumerate(orders):
        when = {}
        for p in range(PIECES):
            when[z, p] = when[order[0], p] = PIECES + p + (0 if z in (0, count - 1) else SHIFT)
            for n in range(1, count - 1):
                when[order[n], p] = n * PIECES + p + LAG[0 if z in (0, count - 1) else 1]
        row = [0]
        for k in range(PIECES, last + LAG[1]):
            g = row[-1]
            top = g + CAP if k < last else count * PIECES
            while g < min(top, count * PIECES) and when[divmod(g, PIECES)] <= k:
                g += 1
            row.append(g)
        table.append(row)
    return table


def layer_kernel(count, tokens_ref, query_ref, key_ref, value_ref, rate_hbm, residue_hbm,
                 carried_hbm, out_ref, state_ref,
                 all_ref, weights_ref, query_rows, signal, conv, gated_ref, ends, entering,
                 rate_ref, scale_ref, residue_ref, carried_ref, decay_ref, weight_ref, step_ref,
                 fill_sem, hop_send, hop_recv, side_send, side_recv, core_recv,
                 part_recv, layer_send, layer_recv, out_send, out_recv, own_sem):
    part, seq, chan, rep = (lax.axis_index(a) for a in ("parts", "seq", "chan", "rep"))
    rows, columns = tokens_ref.shape
    depth, outer = query_ref.shape
    width = outer // count
    half = depth // 2
    piece = rows // PIECES
    modes = rate_ref.shape[0]
    own_columns = pl.ds(pl.multiple_of(seq * width, width), width)
    matrices = (query_ref, key_ref, value_ref)

    barrier = pltpu.get_barrier_semaphore()
    mates = ({"parts": 1 - part}, {"chan": 1 - chan}, {"rep": 1 - rep})
    for mate in mates:
        pl.semaphore_signal(barrier, inc=1, device_id=mate, device_id_type=MESH)
    for step in range(1, count):
        pl.semaphore_signal(
            barrier, inc=1, device_id={"seq": lax.rem(seq + step, count)}, device_id_type=MESH
        )

    fills = [
        pltpu.make_async_copy(
            tokens_ref,
            all_ref.at[pl.ds(pl.multiple_of(seq * rows, rows), rows),
                       pl.ds(pl.multiple_of((chan * 2 + rep) * columns, columns), columns)],
            fill_sem.at[0])
    ] + [
        pltpu.make_async_copy(
            matrices[m].at[:, own_columns],
            weights_ref.at[pl.ds(pl.multiple_of(seq * depth, depth), depth), pl.ds(m * width, width)],
            fill_sem.at[1 + m])
        for m in range(3)
    ] + [
        pltpu.make_async_copy(source, target, fill_sem.at[4 + n])
        for n, (source, target) in enumerate((
            (rate_hbm, rate_ref), (residue_hbm, residue_ref), (carried_hbm, carried_ref),
        ))
    ]

    def remote(source, target, send, recv, device):
        return pltpu.make_async_remote_copy(
            src_ref=source, dst_ref=target, send_sem=send, recv_sem=recv,
            device_id=device, device_id_type=MESH,
        )

    def token_block(block, side, core, p):
        top = pl.multiple_of(block * rows + p * piece, piece)
        left = pl.multiple_of((side * 2 + core) * columns, columns)
        return all_ref.at[pl.ds(top, piece), pl.ds(left, columns)]

    def own_piece(p):
        return tokens_ref.at[pl.ds(p * piece, piece), :]

    def hop(block, p, way, source=None):
        here = token_block(block, chan, rep, p)
        return remote(here if source is None else source, here,
                      hop_send.at[block, (1 - way) // 2], hop_recv.at[block, p], {"seq": seq + way})

    def side(block, p, source=None):
        here = token_block(block, chan, rep, p)
        return remote(here if source is None else source, here,
                      side_send.at[block], side_recv.at[block, p], {"chan": 1 - chan})

    def side_arrival(block, p):
        there = token_block(block, 1 - chan, rep, p)
        return remote(there, there, side_send.at[block], side_recv.at[block, p], {"chan": 1 - chan})

    def core(block, which, p, source=None):
        here = token_block(block, chan if which == 0 else 1 - chan, rep, p)
        return remote(here if source is None else source, here,
                      side_send.at[block], core_recv.at[block, p], {"rep": 1 - rep})

    def core_arrivals(block, p):
        top = pl.multiple_of(block * rows + p * piece, piece)
        there = all_ref.at[pl.ds(top, piece), pl.ds(0, 2 * columns)]
        return remote(there, there, side_send.at[block], core_recv.at[block, p], {"rep": 1 - rep})

    def sent(semaphore, other, wide):
        there = all_ref.at[pl.ds(0, rows), pl.ds(0, wide * columns)]
        return remote(there, there, semaphore, hop_recv.at[other, 0], {"rep": 1 - rep})

    def swapped(other):
        there = weights_ref.at[pl.ds(pl.multiple_of(other * depth + (1 - part) * half, half), half), :]
        return remote(there, there, layer_send.at[other], part_recv.at[other], {"parts": 1 - part})

    def weights_sent(other):
        there = weights_ref.at[pl.ds(pl.multiple_of(other * depth, depth), depth), :]
        return remote(there, there, layer_send.at[other], layer_recv.at[other, 0], {"seq": other})

    def weight_block(block, m, part_of):
        top = pl.multiple_of(block * depth + part_of * half, half)
        return weights_ref.at[pl.ds(top, half), pl.ds(m * width, width)]

    def spread(target, m):
        source = matrices[m].at[
            pl.ds(pl.multiple_of(part * half, half), half),
            pl.ds(pl.multiple_of(target * width, width), width),
        ]
        return remote(source, weight_block(seq, m, part),
                      layer_send.at[target], layer_recv.at[seq, m], {"seq": target})

    def spread_arrival(block, m):
        here = weight_block(block, m, part)
        return remote(here, here, layer_send.at[block], layer_recv.at[block, m], {"seq": block})

    def swap(block, m):
        here = weight_block(block, m, part)
        return remote(here, here, layer_send.at[block], part_recv.at[block], {"parts": 1 - part})

    def result_rows(p):
        return pl.ds(pl.multiple_of(p * piece, piece), piece)

    def result_columns(source):
        return pl.ds(pl.multiple_of(source * width, width), width)

    def gated_rows(block, p):
        return gated_ref.at[pl.ds(pl.multiple_of(block * rows + p * piece, piece), piece), :]

    def give(block, p):
        return remote(gated_rows(block, p), out_ref.at[result_rows(p), result_columns(seq)],
                      out_send.at[block], out_recv.at[seq], {"seq": block})

    def take(source):
        here = out_ref.at[:, result_columns(source)]
        return remote(here, here, out_send.at[source], out_recv.at[source], {"seq": source})

    def keep(p):
        return pltpu.make_async_copy(
            gated_rows(seq, p), out_ref.at[result_rows(p), result_columns(seq)], own_sem.at[0]
        )

    def inside(other):
        return (other >= 0) & (other < count)

    def pick(values, index):
        found = values[0]
        for n in range(1, len(values)):
            found = jnp.where(index == n, values[n], found)
        return found

    def by_plane(table, index):
        flat = [value for row in table for value in row]
        return pick(flat, seq * len(table[0]) + index)

    orders = block_orders(count)
    ready = reach_table(orders)
    is_first, is_last = seq == 0, seq == count - 1
    is_end = is_first | is_last
    deferred = (seq == 1) if count == 4 else (seq == count)

    pl.semaphore_wait(barrier, count - 1 + len(mates))

    def send_weights(way, distances):
        for distance in distances:
            other = seq + way * distance

            @pl.when(inside(other))
            def _():
                for m in range(3):
                    spread(other, m).start()

    def send_own(way):
        for p in range(PIECES):
            hop(seq, p, way, own_piece(p)).start()

    for way, at_end in ((1, is_first), (-1, is_last)):
        @pl.when(at_end)
        def _():
            send_weights(way, (1,))
            send_own(way)
            send_weights(way, range(2, count))

        @pl.when(jnp.logical_not(at_end) & inside(seq + way))
        def _():
            send_weights(way, range(count - 1, 0, -1))
            if way == 1:
                @pl.when(jnp.logical_not(deferred))
                def _():
                    send_own(way)
            else:
                send_own(way)

    for p in range(PIECES):
        side(seq, p, own_piece(p)).start()
        core(seq, 0, p, own_piece(p)).start()
    for fill in fills:
        fill.start()

    def relay(block, p):
        way = jnp.where(block < seq, 1, -1)
        hop(block, p, way).wait_recv()

        @pl.when(inside(seq + way))
        def _():
            hop(block, p, way).start()

        side(block, p).start()
        core(block, 0, p).start()

    def pass_side(block, p):
        side_arrival(block, p).wait_recv()
        core(block, 1, p).start()

    def pass_weights(other, m):
        @pl.when(inside(other))
        def _():
            spread_arrival(other, m).wait_recv()
            swap(other, m).start()

    toward = jnp.where(2 * seq < count, -1, 1)
    side_lag = jnp.where(is_end, SIDE_LAG[0], SIDE_LAG[1])
    lag = jnp.where(is_end, LAG[0], LAG[1])
    shift = jnp.where(is_end, 0, SHIFT)
    first_block = by_plane(orders, 0)

    far, between = count - 1, range(count - 2, 1, -1)

    @pl.when(is_end)
    def _():
        for m in range(3):
            pass_side(seq, m)
            for distance in between:
                pass_weights(seq - toward * distance, m)
        for p in range(3, PIECES):
            pass_side(seq, p)
        for m in range(3):
            pass_weights(seq - toward, m)
        for p in range(PIECES):
            relay(first_block, p)
        if far > 1:
            for m in range(3):
                pass_weights(seq - toward * far, m)

    @pl.when(jnp.logical_not(is_end))
    def _():
        for m in range(3):
            pass_weights(seq + toward, m)
            pass_side(seq, m)
        for p in range(3, PIECES):
            pass_side(seq, p)
        for p in range(PIECES):
            relay(first_block, p)
            if p < 3:
                pass_weights(seq - toward, p)

        @pl.when(deferred)
        def _():
            send_own(1)

        for p in range(PIECES - SIDE_LAG[1]):
            pass_side(first_block, p)
        for m in range(3):
            for distance in between:
                pass_weights(seq - toward * distance, m)
                pass_weights(seq + toward * distance, m)

    for p in range(PIECES - SIDE_LAG[0]):
        @pl.when(is_end)
        def _():
            pass_side(first_block, p)

    for fill in fills:
        fill.wait()

    scale_ref[...] = jnp.sqrt(one_less_exp(2.0 * rate_ref[...]))
    lane_groups = width // LANES
    chunk = piece // CHUNKS
    step_ref[...] = jnp.exp(-rate_ref[...] * chunk)
    for group in range(lane_groups):
        lanes = pl.ds(group * LANES, LANES)
        decay = jnp.exp(-rate_ref[:, lanes])
        weight = residue_ref[:, lanes] * scale_ref[:, lanes]
        for m in range(modes):
            decay_ref[group, m] = jnp.broadcast_to(decay[m : m + 1, :], (CHUNKS, LANES))
            weight_ref[group, m] = jnp.broadcast_to(weight[m : m + 1, :], (CHUNKS, LANES))

    def project(block, p):
        core_arrivals(block, p).wait_recv()
        top = pl.ds(pl.multiple_of(block * rows + p * piece, piece), piece)
        found = jnp.dot(all_ref[top, :], weights_ref[...], preferred_element_type=jnp.float32)
        found = found.astype(jnp.bfloat16)
        query_rows[top, :] = found[:, :width]
        product = (
            found[:, width : 2 * width].astype(jnp.float32) * found[:, 2 * width :].astype(jnp.float32)
        )
        product = product.astype(jnp.bfloat16).astype(jnp.float32)
        for group in range(lane_groups):
            signal[group, top, :] = product[:, group * LANES : (group + 1) * LANES]

    def scan(g, _):
        block, p = g // PIECES, lax.rem(g, PIECES)
        top = pl.multiple_of(g * piece, piece)
        for group in range(lane_groups):
            lanes = pl.ds(group * LANES, LANES)
            residues = residue_ref[:, lanes]
            scale = scale_ref[:, lanes]
            chunk_decay = step_ref[:, lanes]
            decays = [decay_ref[group, m] for m in range(modes)]
            weights = [weight_ref[group, m] for m in range(modes)]

            def sums(step, states):
                here = signal[group, pl.ds(top + step, CHUNKS, stride=chunk), :]
                return tuple(d * s + here for d, s in zip(decays, states))

            zero = jnp.zeros((CHUNKS, LANES), jnp.float32)
            finals = lax.fori_loop(0, chunk, sums, (zero,) * modes, unroll=UNROLL)
            for m in range(modes):
                ends[pl.ds(m, CHUNKS, stride=modes), :] = finals[m]
            state = carried_ref[:, lanes]
            for c in range(CHUNKS):
                at = pl.ds(c * modes, modes)
                entering[at, :] = residues * state
                state = chunk_decay * state + scale * ends[at, :]
            carried_ref[:, lanes] = state

            def outputs(step, states):
                here = signal[group, pl.ds(top + step, CHUNKS, stride=chunk), :]
                states = tuple(d * s + w * here for d, s, w in zip(decays, states, weights))
                terms = list(states)
                while len(terms) > 1:
                    terms = [a + b for a, b in zip(terms[::2], terms[1::2])] + (
                        [terms[-1]] if len(terms) % 2 else []
                    )
                conv[group, pl.ds(step, CHUNKS, stride=chunk), :] = terms[0]
                return states

            starts = tuple(entering[pl.ds(m, CHUNKS, stride=modes), :] for m in range(modes))
            lax.fori_loop(0, chunk, outputs, starts, unroll=UNROLL)
            rounded = conv[group].astype(jnp.bfloat16).astype(jnp.float32)
            gated_ref[pl.ds(top, piece), lanes] = (
                query_rows[pl.ds(top, piece), lanes].astype(jnp.float32) * rounded
            ).astype(jnp.bfloat16)

        @pl.when(block == seq)
        def _():
            keep(p).start()

        return 0

    def scan_and_send(g, k):
        scan(g, 0)

        block = g // PIECES

        @pl.when((block != seq) & (k >= release(block)))
        def _():
            give(block, lax.rem(g, PIECES)).start()

        return k

    releases = release_table(count)

    def release(block):
        return by_plane(releases, block)

    def send_held(k, done):
        for block in range(count):
            due = pick([row[block] for row in releases], seq)

            @pl.when((seq != block) & (due == k))
            def _():
                def send(p, _):
                    @pl.when(block * PIECES + p < done)
                    def _():
                        give(block, p).start()

                    return 0

                lax.fori_loop(0, PIECES, send, 0)

    last = (count - 1) * PIECES

    def block_of(k):
        return by_plane(orders, k // PIECES)

    def slot(k, _):
        @pl.when((k < last) & (k >= PIECES))
        def _():
            relay(block_of(k), lax.rem(k, PIECES))

        @pl.when(k == PIECES + shift)
        def _():
            for distance in range(1, count):
                for other in (seq - distance, seq + distance):
                    @pl.when(inside(other))
                    def _():
                        swapped(other).wait_recv()

        def next_side():
            pass_side(block_of(k - side_lag), lax.rem(k - side_lag, PIECES))

        first = is_end & (k > last)

        @pl.when(first & (k < last + side_lag))
        def _():
            next_side()

        def one(which, _):
            early = which < 2
            n = jnp.where(early, k - PIECES - shift, k - lag)
            block = jnp.where(which == 0, seq, jnp.where(which == 1, first_block, block_of(k - lag)))
            known = (early & (n >= 0) & (n < PIECES)) | (jnp.logical_not(early) & (n >= PIECES) & (n < last))

            @pl.when(known)
            def _():
                project(block, lax.rem(n, PIECES))

            return 0

        lax.fori_loop(0, 3, one, 0)
        done, reach = by_plane(ready, k - PIECES), by_plane(ready, k - PIECES + 1)
        lax.fori_loop(done, reach, scan_and_send, k)

        @pl.when((k >= last - 2) & (k <= last + 1))
        def _():
            send_held(k, done)

        @pl.when(jnp.logical_not(first) & (k < last + side_lag))
        def _():
            next_side()

        return 0

    lax.fori_loop(PIECES, last + LAG[1], slot, 0)
    state_ref[...] = carried_ref[...]

    @pl.when(seq > 0)
    def _():
        sent(hop_send.at[seq, 1], seq, 1).wait_send()

    @pl.when(seq + 1 < count)
    def _():
        sent(hop_send.at[seq, 0], seq, 1).wait_send()

    sent(side_send.at[seq], seq, 3).wait_send()
    others = [
        (other, way)
        for distance in range(1, count)
        for other, way in ((seq - distance, 1), (seq + distance, -1))
    ]
    for other, way in others:
        @pl.when(inside(other))
        def _():
            @pl.when(inside(seq + way))
            def _():
                sent(hop_send.at[other, (1 - way) // 2], other, 1).wait_send()

            sent(side_send.at[other], other, 3).wait_send()
            weights_sent(other).wait_send()
    kept = out_ref.at[:, result_columns(seq)]
    pltpu.make_async_copy(kept, kept, own_sem.at[0]).wait()
    for other, way in others:
        @pl.when(inside(other))
        def _():
            take(other).wait_send()
    for other, way in others:
        @pl.when(inside(other))
        def _():
            take(other).wait_recv()


def whole_layer(tokens, w_query, w_key, w_value, rate, residue, carried, count):
    rows, columns = tokens.shape
    depth, outer = w_query.shape
    width, modes = rate.shape
    length = rows * count
    vmem = pl.BlockSpec(memory_space=pltpu.VMEM)
    anywhere = pl.BlockSpec(memory_space=pl.ANY)
    dma = pltpu.SemaphoreType.DMA
    table = pltpu.VMEM((modes, width), jnp.float32)
    operands = (tokens, w_query, w_key, w_value, rate.T, residue.T, carried.T)
    gated, state = pl.pallas_call(
        functools.partial(layer_kernel, count),
        out_shape=(
            jax.ShapeDtypeStruct((rows, outer), jnp.bfloat16),
            jax.ShapeDtypeStruct((modes, width), jnp.float32),
        ),
        in_specs=[anywhere] * 7,
        out_specs=(anywhere, vmem),
        scratch_shapes=[
            pltpu.VMEM((length, columns * 4), jnp.bfloat16),
            pltpu.VMEM((depth * count, 3 * width), jnp.bfloat16),
            pltpu.VMEM((length, width), jnp.bfloat16),
            pltpu.VMEM((width // LANES, length, LANES), jnp.float32),
            pltpu.VMEM((width // LANES, rows // PIECES, LANES), jnp.float32),
            pltpu.VMEM((length, width), jnp.bfloat16),
            pltpu.VMEM((CHUNKS * modes, LANES), jnp.float32),
            pltpu.VMEM((CHUNKS * modes, LANES), jnp.float32),
        ] + [table] * 4 + [
            pltpu.VMEM((width // LANES, modes, CHUNKS, LANES), jnp.float32),
            pltpu.VMEM((width // LANES, modes, CHUNKS, LANES), jnp.float32),
            table,
            dma((7,)),
            dma((count, 2)), dma((count, PIECES)),
            dma((count,)), dma((count, PIECES)),
            dma((count, PIECES)),
            dma((count,)),
            dma((count,)), dma((count, 3)),
            dma((count,)), dma((count,)),
            dma((1,)),
        ],
        compiler_params=pltpu.CompilerParams(
            collective_id=0, has_side_effects=True, vmem_limit_bytes=40 * 2**20
        ),
    )(*(pltpu.with_memory_space_constraint(array, pltpu.HBM) for array in operands))
    return settle(gated, state)


def settle_kernel(gated_ref, state_ref, out_ref, final_ref, sem):
    rows = gated_ref.shape[0]
    part = rows // PIECES
    copies = [
        pltpu.make_async_copy(
            gated_ref.at[pl.ds(p * part, part), :], out_ref.at[pl.ds(p * part, part), :], sem.at[p]
        )
        for p in range(PIECES)
    ] + [pltpu.make_async_copy(state_ref, final_ref, sem.at[PIECES])]
    for copy in copies:
        copy.start()
    for copy in copies:
        copy.wait()


def settle(gated, state):
    anywhere = pl.BlockSpec(memory_space=pl.ANY)
    out, final = pl.pallas_call(
        settle_kernel,
        out_shape=(
            jax.ShapeDtypeStruct(gated.shape, gated.dtype),
            jax.ShapeDtypeStruct(state.shape, state.dtype),
        ),
        in_specs=[anywhere] * 2,
        out_specs=(anywhere, anywhere),
        scratch_shapes=[pltpu.SemaphoreType.DMA((PIECES + 1,))],
        compiler_params=pltpu.CompilerParams(vmem_limit_bytes=2**20),
    )(gated, state)
    return out, final.T


def per_device_channels(tokens, w_query, w_key, w_value, decay_rate, residue, carried):
    count = lax.axis_size("seq")
    return whole_layer(tokens, w_query, w_key, w_value, decay_rate, residue, carried, count)


def solution(mesh):
    in_specs = (
        P(("parts", "seq"), ("chan", "rep")),
        P("seq", ("chan", "rep")),
        P("seq", ("chan", "rep")),
        P("seq", ("chan", "rep")),
        P(("chan", "rep", "seq"), None),
        P(("chan", "rep", "seq"), None),
        P(("parts", "chan", "rep", "seq"), None),
    )
    out_specs = (P(("parts", "seq"), ("chan", "rep")), P(("parts", "chan", "rep", "seq"), None))

    def body(*arrays):
        own_channels = arrays[4].shape[0]
        mates = all(mesh.shape[a] == 2 for a in ("parts", "chan", "rep"))
        chosen = per_device_channels if own_channels % LANES == 0 and mates else per_device
        return chosen(*arrays)

    return jax.shard_map(body, mesh=mesh, in_specs=in_specs, out_specs=out_specs, check_vma=False)
```

```python
import functools

import jax
import jax.numpy as jnp
from jax import lax
from jax.experimental import pallas as pl
from jax.experimental.pallas import tpu as pltpu
from jax.sharding import PartitionSpec as P

BLOCK = 128
LANES = 128
CHUNKS = 8
MESH = pl.DeviceIdType.MESH


HIGHEST_PRECISION = lax.Precision.HIGHEST


def mode_scale(decay_rates):
    return jnp.sqrt(-jnp.expm1(-2.0 * decay_rates))


def local_ends(blocks, decay_rates):
    block_width = blocks.shape[2]
    offsets = jnp.arange(block_width, dtype=jnp.float32)
    tail_powers = jnp.exp(-decay_rates[:, :, None] * (block_width - 1.0 - offsets)[None, None, :])
    sums_here = jnp.einsum("cnb,cmb->cnm", blocks, tail_powers, precision=HIGHEST_PRECISION)
    return mode_scale(decay_rates)[:, None, :] * sums_here


def combine_states(earlier, later):
    return (earlier[0] * later[0], later[0] * earlier[1] + later[1])


def block_sums(block_ends, decay_rates, block_width):
    step_decay = jnp.broadcast_to(jnp.exp(-decay_rates * block_width)[:, None, :], block_ends.shape)
    unused_decay, running = lax.associative_scan(combine_states, (step_decay, block_ends), axis=1)
    return running


def entering_states(running, decay_rates, start_state, block_width):
    count_blocks = running.shape[1]
    block_starts = jnp.arange(count_blocks, dtype=jnp.float32) * block_width
    decayed = (
        jnp.exp(-decay_rates[:, None, :] * block_starts[None, :, None]) * start_state[:, None, :]
    )
    earlier_sums = jnp.concatenate([jnp.zeros_like(running[:, :1]), running[:, :-1]], axis=1)
    final_state = (
        jnp.exp(-decay_rates * (count_blocks * block_width)) * start_state + running[:, -1]
    )
    return (decayed + earlier_sums, final_state)


def block_convolve(blocks, decay_rates, residues, entering):
    block_width = blocks.shape[2]
    offsets = jnp.arange(block_width, dtype=jnp.float32)
    powers = jnp.exp(-decay_rates[:, :, None] * offsets[None, None, :])
    kernel = jnp.sum((residues * mode_scale(decay_rates))[:, :, None] * powers, axis=1)
    out_index = jnp.arange(block_width, dtype=jnp.int32)[:, None]
    in_index = jnp.arange(block_width, dtype=jnp.int32)[None, :]
    lag = jnp.maximum(out_index - in_index, 0)
    causal = (out_index >= in_index).astype(jnp.float32)
    toeplitz = kernel[:, lag] * causal[None, :, :]
    direct = jnp.einsum("cij,cnj->cni", toeplitz, blocks, precision=HIGHEST_PRECISION)
    leading = residues[:, :, None] * jnp.exp(
        -decay_rates[:, :, None] * (offsets + 1.0)[None, None, :]
    )
    return direct + jnp.einsum("cnm,cmb->cnb", entering, leading, precision=HIGHEST_PRECISION)


def per_device(tokens, w_query, w_key, w_value, decay_rate, residue, carried):
    gathered = lax.all_gather(tokens, ("chan", "rep"), axis=1, tiled=True)
    pieces = (
        lax.all_gather(w_query, "seq", axis=0, tiled=True),
        lax.all_gather(w_key, "seq", axis=0, tiled=True),
        lax.all_gather(w_value, "seq", axis=0, tiled=True),
    )
    query_acc, key_acc, value_acc = tuple(
        (
            lax.dot_general(
                weight_piece, gathered, (((0,), (1,)), ((), ())), preferred_element_type=jnp.float32
            )
            for weight_piece in pieces
        )
    )
    query_rows = query_acc.astype(jnp.bfloat16)
    key_rows = key_acc.astype(jnp.bfloat16)
    value_rows = value_acc.astype(jnp.bfloat16)
    query_rows, key_rows, value_rows = lax.optimization_barrier((query_rows, key_rows, value_rows))
    product = (key_rows.astype(jnp.float32) * value_rows.astype(jnp.float32)).astype(jnp.bfloat16)
    owned = lax.all_to_all(product, "seq", split_axis=0, concat_axis=1, tiled=True)
    own_chan = owned.shape[0]
    blocks = owned.astype(jnp.float32).reshape(own_chan, -1, BLOCK)
    block_end = local_ends(blocks, decay_rate)
    running = block_sums(block_end, decay_rate, BLOCK)
    entering, new_state = entering_states(running, decay_rate, carried, BLOCK)
    conv_out = (
        block_convolve(blocks, decay_rate, residue, entering)
        .reshape(own_chan, -1)
        .astype(jnp.bfloat16)
    )
    conv_back = lax.all_to_all(conv_out, "seq", split_axis=1, concat_axis=0, tiled=True)
    conv_back = lax.optimization_barrier(conv_back)
    gated_rows = (query_rows.astype(jnp.float32) * conv_back.astype(jnp.float32)).astype(
        jnp.bfloat16
    )
    return (gated_rows.T, new_state)


PIECES = 4
SIDE_LAG = (1, 1)
LAG = (2, 2)
SHIFT = 0
CAP = 2
UNROLL = 8


def block_orders(count):
    if count == 4:
        return ((1, 2, 3), (0, 2, 3), (3, 0, 1), (2, 0, 1))
    return tuple(
        tuple(sorted((b for b in range(count) if b != z), key=lambda b: (abs(b - z), b)))
        for z in range(count)
    )


def one_less_exp(x):
    series = jnp.ones_like(x)
    for n in range(9, 1, -1):
        series = 1.0 - series * x * (1.0 / n)
    return jnp.where(x < 0.25, x * series, 1.0 - jnp.exp(-x))


def release_table(count):
    if count != 4:
        return ((0,) * count,) * count
    last = (count - 1) * PIECES
    return (
        (0, 0, last - 2, 0),
        (last - 1, 0, last + 1, last - 1),
        (last, 0, 0, 0),
        (last - 1, 0, 0, 0),
    )


def reach_table(orders):
    count = len(orders)
    last = (count - 1) * PIECES
    table = []
    for z, order in enumerate(orders):
        when = {}
        for p in range(PIECES):
            when[z, p] = when[order[0], p] = PIECES + p + (0 if z in (0, count - 1) else SHIFT)
            for n in range(1, count - 1):
                when[order[n], p] = n * PIECES + p + LAG[0 if z in (0, count - 1) else 1]
        row = [0]
        for k in range(PIECES, last + LAG[1]):
            g = row[-1]
            top = g + CAP if k < last else count * PIECES
            while g < min(top, count * PIECES) and when[divmod(g, PIECES)] <= k:
                g += 1
            row.append(g)
        table.append(row)
    return table


def layer_kernel(count, tokens_ref, query_ref, key_ref, value_ref, rate_hbm, residue_hbm,
                 carried_hbm, out_ref, state_ref,
                 all_ref, weights_ref, query_rows, signal, conv, gated_ref, ends, entering,
                 rate_ref, scale_ref, residue_ref, carried_ref, decay_ref, weight_ref, step_ref,
                 fill_sem, hop_send, hop_recv, side_send, side_recv, core_recv,
                 part_recv, layer_send, layer_recv, out_send, out_recv, own_sem):
    part, seq, chan, rep = (lax.axis_index(a) for a in ("parts", "seq", "chan", "rep"))
    rows, columns = tokens_ref.shape
    depth, outer = query_ref.shape
    width = outer // count
    half = depth // 2
    piece = rows // PIECES
    modes = rate_ref.shape[0]
    own_columns = pl.ds(pl.multiple_of(seq * width, width), width)
    matrices = (query_ref, key_ref, value_ref)

    barrier = pltpu.get_barrier_semaphore()
    mates = ({"parts": 1 - part}, {"chan": 1 - chan}, {"rep": 1 - rep})
    for mate in mates:
        pl.semaphore_signal(barrier, inc=1, device_id=mate, device_id_type=MESH)
    for step in range(1, count):
        pl.semaphore_signal(
            barrier, inc=1, device_id={"seq": lax.rem(seq + step, count)}, device_id_type=MESH
        )

    fills = [
        pltpu.make_async_copy(
            tokens_ref,
            all_ref.at[pl.ds(pl.multiple_of(seq * rows, rows), rows),
                       pl.ds(pl.multiple_of((chan * 2 + rep) * columns, columns), columns)],
            fill_sem.at[0])
    ] + [
        pltpu.make_async_copy(
            matrices[m].at[:, own_columns],
            weights_ref.at[pl.ds(pl.multiple_of(seq * depth, depth), depth), pl.ds(m * width, width)],
            fill_sem.at[1 + m])
        for m in range(3)
    ] + [
        pltpu.make_async_copy(source, target, fill_sem.at[4 + n])
        for n, (source, target) in enumerate((
            (rate_hbm, rate_ref), (residue_hbm, residue_ref), (carried_hbm, carried_ref),
        ))
    ]

    def remote(source, target, send, recv, device):
        return pltpu.make_async_remote_copy(
            src_ref=source, dst_ref=target, send_sem=send, recv_sem=recv,
            device_id=device, device_id_type=MESH,
        )

    def token_block(block, side, core, p):
        top = pl.multiple_of(block * rows + p * piece, piece)
        left = pl.multiple_of((side * 2 + core) * columns, columns)
        return all_ref.at[pl.ds(top, piece), pl.ds(left, columns)]

    def own_piece(p):
        return tokens_ref.at[pl.ds(p * piece, piece), :]

    def hop(block, p, way, source=None):
        here = token_block(block, chan, rep, p)
        return remote(here if source is None else source, here,
                      hop_send.at[block, (1 - way) // 2], hop_recv.at[block, p], {"seq": seq + way})

    def side(block, p, source=None):
        here = token_block(block, chan, rep, p)
        return remote(here if source is None else source, here,
                      side_send.at[block], side_recv.at[block, p], {"chan": 1 - chan})

    def side_arrival(block, p):
        there = token_block(block, 1 - chan, rep, p)
        return remote(there, there, side_send.at[block], side_recv.at[block, p], {"chan": 1 - chan})

    def core(block, which, p, source=None):
        here = token_block(block, chan if which == 0 else 1 - chan, rep, p)
        return remote(here if source is None else source, here,
                      side_send.at[block], core_recv.at[block, p], {"rep": 1 - rep})

    def core_arrivals(block, p):
        top = pl.multiple_of(block * rows + p * piece, piece)
        there = all_ref.at[pl.ds(top, piece), pl.ds(0, 2 * columns)]
        return remote(there, there, side_send.at[block], core_recv.at[block, p], {"rep": 1 - rep})

    def sent(semaphore, other, wide):
        there = all_ref.at[pl.ds(0, rows), pl.ds(0, wide * columns)]
        return remote(there, there, semaphore, hop_recv.at[other, 0], {"rep": 1 - rep})

    def swapped(other):
        there = weights_ref.at[pl.ds(pl.multiple_of(other * depth + (1 - part) * half, half), half), :]
        return remote(there, there, layer_send.at[other], part_recv.at[other], {"parts": 1 - part})

    def weights_sent(other):
        there = weights_ref.at[pl.ds(pl.multiple_of(other * depth, depth), depth), :]
        return remote(there, there, layer_send.at[other], layer_recv.at[other, 0], {"seq": other})

    def weight_block(block, m, part_of):
        top = pl.multiple_of(block * depth + part_of * half, half)
        return weights_ref.at[pl.ds(top, half), pl.ds(m * width, width)]

    def spread(target, m):
        source = matrices[m].at[
            pl.ds(pl.multiple_of(part * half, half), half),
            pl.ds(pl.multiple_of(target * width, width), width),
        ]
        return remote(source, weight_block(seq, m, part),
                      layer_send.at[target], layer_recv.at[seq, m], {"seq": target})

    def spread_arrival(block, m):
        here = weight_block(block, m, part)
        return remote(here, here, layer_send.at[block], layer_recv.at[block, m], {"seq": block})

    def swap(block, m):
        here = weight_block(block, m, part)
        return remote(here, here, layer_send.at[block], part_recv.at[block], {"parts": 1 - part})

    def result_rows(p):
        return pl.ds(pl.multiple_of(p * piece, piece), piece)

    def result_columns(source):
        return pl.ds(pl.multiple_of(source * width, width), width)

    def gated_rows(block, p):
        return gated_ref.at[pl.ds(pl.multiple_of(block * rows + p * piece, piece), piece), :]

    def give(block, p):
        return remote(gated_rows(block, p), out_ref.at[result_rows(p), result_columns(seq)],
                      out_send.at[block], out_recv.at[seq], {"seq": block})

    def take(source):
        here = out_ref.at[:, result_columns(source)]
        return remote(here, here, out_send.at[source], out_recv.at[source], {"seq": source})

    def keep(p):
        return pltpu.make_async_copy(
            gated_rows(seq, p), out_ref.at[result_rows(p), result_columns(seq)], own_sem.at[0]
        )

    def inside(other):
        return (other >= 0) & (other < count)

    def pick(values, index):
        found = values[0]
        for n in range(1, len(values)):
            found = jnp.where(index == n, values[n], found)
        return found

    def by_plane(table, index):
        flat = [value for row in table for value in row]
        return pick(flat, seq * len(table[0]) + index)

    orders = block_orders(count)
    ready = reach_table(orders)
    is_first, is_last = seq == 0, seq == count - 1
    is_end = is_first | is_last
    deferred = (seq == 1) if count == 4 else (seq == count)

    pl.semaphore_wait(barrier, count - 1 + len(mates))

    def send_weights(way, distances):
        for distance in distances:
            other = seq + way * distance

            @pl.when(inside(other))
            def _():
                for m in range(3):
                    spread(other, m).start()

    def send_own(way):
        for p in range(PIECES):
            hop(seq, p, way, own_piece(p)).start()

    for way, at_end in ((1, is_first), (-1, is_last)):
        @pl.when(at_end)
        def _():
            send_weights(way, (1,))
            send_own(way)
            send_weights(way, range(2, count))

        @pl.when(jnp.logical_not(at_end) & inside(seq + way))
        def _():
            send_weights(way, range(count - 1, 0, -1))
            if way == 1:
                @pl.when(jnp.logical_not(deferred))
                def _():
                    send_own(way)
            else:
                send_own(way)

    for p in range(PIECES):
        side(seq, p, own_piece(p)).start()
        core(seq, 0, p, own_piece(p)).start()
    for fill in fills:
        fill.start()

    def relay(block, p):
        way = jnp.where(block < seq, 1, -1)
        hop(block, p, way).wait_recv()

        @pl.when(inside(seq + way))
        def _():
            hop(block, p, way).start()

        side(block, p).start()
        core(block, 0, p).start()

    def pass_side(block, p):
        side_arrival(block, p).wait_recv()
        core(block, 1, p).start()

    def pass_weights(other, m):
        @pl.when(inside(other))
        def _():
            spread_arrival(other, m).wait_recv()
            swap(other, m).start()

    toward = jnp.where(2 * seq < count, -1, 1)
    side_lag = jnp.where(is_end, SIDE_LAG[0], SIDE_LAG[1])
    lag = jnp.where(is_end, LAG[0], LAG[1])
    shift = jnp.where(is_end, 0, SHIFT)
    first_block = by_plane(orders, 0)

    far, between = count - 1, range(count - 2, 1, -1)

    @pl.when(is_end)
    def _():
        for m in range(3):
            pass_side(seq, m)
            for distance in between:
                pass_weights(seq - toward * distance, m)
        for p in range(3, PIECES):
            pass_side(seq, p)
        for m in range(3):
            pass_weights(seq - toward, m)
        for p in range(PIECES):
            relay(first_block, p)
        if far > 1:
            for m in range(3):
                pass_weights(seq - toward * far, m)

    @pl.when(jnp.logical_not(is_end))
    def _():
        for m in range(3):
            pass_weights(seq + toward, m)
            pass_side(seq, m)
        for p in range(3, PIECES):
            pass_side(seq, p)
        for p in range(PIECES):
            relay(first_block, p)
            if p < 3:
                pass_weights(seq - toward, p)

        @pl.when(deferred)
        def _():
            send_own(1)

        for p in range(PIECES - SIDE_LAG[1]):
            pass_side(first_block, p)
        for m in range(3):
            for distance in between:
                pass_weights(seq - toward * distance, m)
                pass_weights(seq + toward * distance, m)

    for p in range(PIECES - SIDE_LAG[0]):
        @pl.when(is_end)
        def _():
            pass_side(first_block, p)

    for fill in fills:
        fill.wait()

    scale_ref[...] = jnp.sqrt(one_less_exp(2.0 * rate_ref[...]))
    lane_groups = width // LANES
    chunk = piece // CHUNKS
    step_ref[...] = jnp.exp(-rate_ref[...] * chunk)
    for group in range(lane_groups):
        lanes = pl.ds(group * LANES, LANES)
        decay = jnp.exp(-rate_ref[:, lanes])
        weight = residue_ref[:, lanes] * scale_ref[:, lanes]
        for m in range(modes):
            decay_ref[group, m] = jnp.broadcast_to(decay[m : m + 1, :], (CHUNKS, LANES))
            weight_ref[group, m] = jnp.broadcast_to(weight[m : m + 1, :], (CHUNKS, LANES))

    def project(block, p):
        core_arrivals(block, p).wait_recv()
        top = pl.ds(pl.multiple_of(block * rows + p * piece, piece), piece)
        found = jnp.dot(all_ref[top, :], weights_ref[...], preferred_element_type=jnp.float32)
        found = found.astype(jnp.bfloat16)
        query_rows[top, :] = found[:, :width]
        product = (
            found[:, width : 2 * width].astype(jnp.float32) * found[:, 2 * width :].astype(jnp.float32)
        )
        product = product.astype(jnp.bfloat16).astype(jnp.float32)
        for group in range(lane_groups):
            signal[group, top, :] = product[:, group * LANES : (group + 1) * LANES]

    def scan(g, _):
        block, p = g // PIECES, lax.rem(g, PIECES)
        top = pl.multiple_of(g * piece, piece)
        for group in range(lane_groups):
            lanes = pl.ds(group * LANES, LANES)
            residues = residue_ref[:, lanes]
            scale = scale_ref[:, lanes]
            chunk_decay = step_ref[:, lanes]
            decays = [decay_ref[group, m] for m in range(modes)]
            weights = [weight_ref[group, m] for m in range(modes)]

            def sums(step, states):
                here = signal[group, pl.ds(top + step, CHUNKS, stride=chunk), :]
                return tuple(d * s + here for d, s in zip(decays, states))

            zero = jnp.zeros((CHUNKS, LANES), jnp.float32)
            finals = lax.fori_loop(0, chunk, sums, (zero,) * modes, unroll=UNROLL)
            for m in range(modes):
                ends[pl.ds(m, CHUNKS, stride=modes), :] = finals[m]
            state = carried_ref[:, lanes]
            for c in range(CHUNKS):
                at = pl.ds(c * modes, modes)
                entering[at, :] = residues * state
                state = chunk_decay * state + scale * ends[at, :]
            carried_ref[:, lanes] = state

            def outputs(step, states):
                here = signal[group, pl.ds(top + step, CHUNKS, stride=chunk), :]
                states = tuple(d * s + w * here for d, s, w in zip(decays, states, weights))
                terms = list(states)
                while len(terms) > 1:
                    terms = [a + b for a, b in zip(terms[::2], terms[1::2])] + (
                        [terms[-1]] if len(terms) % 2 else []
                    )
                conv[group, pl.ds(step, CHUNKS, stride=chunk), :] = terms[0]
                return states

            starts = tuple(entering[pl.ds(m, CHUNKS, stride=modes), :] for m in range(modes))
            lax.fori_loop(0, chunk, outputs, starts, unroll=UNROLL)
            rounded = conv[group].astype(jnp.bfloat16).astype(jnp.float32)
            gated_ref[pl.ds(top, piece), lanes] = (
                query_rows[pl.ds(top, piece), lanes].astype(jnp.float32) * rounded
            ).astype(jnp.bfloat16)

        @pl.when(block == seq)
        def _():
            keep(p).start()

        return 0

    def scan_and_send(g, k):
        scan(g, 0)

        block = g // PIECES

        @pl.when((block != seq) & (k >= release(block)))
        def _():
            give(block, lax.rem(g, PIECES)).start()

        return k

    releases = release_table(count)

    def release(block):
        return by_plane(releases, block)

    def send_held(k, done):
        for block in range(count):
            due = pick([row[block] for row in releases], seq)

            @pl.when((seq != block) & (due == k))
            def _():
                def send(p, _):
                    @pl.when(block * PIECES + p < done)
                    def _():
                        give(block, p).start()

                    return 0

                lax.fori_loop(0, PIECES, send, 0)

    last = (count - 1) * PIECES

    def block_of(k):
        return by_plane(orders, k // PIECES)

    def slot(k, _):
        @pl.when((k < last) & (k >= PIECES))
        def _():
            relay(block_of(k), lax.rem(k, PIECES))

        @pl.when(k == PIECES + shift)
        def _():
            for distance in range(1, count):
                for other in (seq - distance, seq + distance):
                    @pl.when(inside(other))
                    def _():
                        swapped(other).wait_recv()

        def next_side():
            pass_side(block_of(k - side_lag), lax.rem(k - side_lag, PIECES))

        first = is_end & (k > last)

        @pl.when(first & (k < last + side_lag))
        def _():
            next_side()

        def one(which, _):
            early = which < 2
            n = jnp.where(early, k - PIECES - shift, k - lag)
            block = jnp.where(which == 0, seq, jnp.where(which == 1, first_block, block_of(k - lag)))
            known = (early & (n >= 0) & (n < PIECES)) | (jnp.logical_not(early) & (n >= PIECES) & (n < last))

            @pl.when(known)
            def _():
                project(block, lax.rem(n, PIECES))

            return 0

        lax.fori_loop(0, 3, one, 0)
        done, reach = by_plane(ready, k - PIECES), by_plane(ready, k - PIECES + 1)
        lax.fori_loop(done, reach, scan_and_send, k)

        @pl.when((k >= last - 2) & (k <= last + 1))
        def _():
            send_held(k, done)

        @pl.when(jnp.logical_not(first) & (k < last + side_lag))
        def _():
            next_side()

        return 0

    lax.fori_loop(PIECES, last + LAG[1], slot, 0)
    state_ref[...] = carried_ref[...]

    @pl.when(seq > 0)
    def _():
        sent(hop_send.at[seq, 1], seq, 1).wait_send()

    @pl.when(seq + 1 < count)
    def _():
        sent(hop_send.at[seq, 0], seq, 1).wait_send()

    sent(side_send.at[seq], seq, 3).wait_send()
    others = [
        (other, way)
        for distance in range(1, count)
        for other, way in ((seq - distance, 1), (seq + distance, -1))
    ]
    for other, way in others:
        @pl.when(inside(other))
        def _():
            @pl.when(inside(seq + way))
            def _():
                sent(hop_send.at[other, (1 - way) // 2], other, 1).wait_send()

            sent(side_send.at[other], other, 3).wait_send()
            weights_sent(other).wait_send()
    kept = out_ref.at[:, result_columns(seq)]
    pltpu.make_async_copy(kept, kept, own_sem.at[0]).wait()
    for other, way in others:
        @pl.when(inside(other))
        def _():
            take(other).wait_send()
    for other, way in others:
        @pl.when(inside(other))
        def _():
            take(other).wait_recv()


def whole_layer(tokens, w_query, w_key, w_value, rate, residue, carried, count):
    rows, columns = tokens.shape
    depth, outer = w_query.shape
    width, modes = rate.shape
    length = rows * count
    vmem = pl.BlockSpec(memory_space=pltpu.VMEM)
    anywhere = pl.BlockSpec(memory_space=pl.ANY)
    dma = pltpu.SemaphoreType.DMA
    table = pltpu.VMEM((modes, width), jnp.float32)
    operands = (tokens, w_query, w_key, w_value, rate.T, residue.T, carried.T)
    gated, state = pl.pallas_call(
        functools.partial(layer_kernel, count),
        out_shape=(
            jax.ShapeDtypeStruct((rows, outer), jnp.bfloat16),
            jax.ShapeDtypeStruct((modes, width), jnp.float32),
        ),
        in_specs=[anywhere] * 7,
        out_specs=(anywhere, vmem),
        scratch_shapes=[
            pltpu.VMEM((length, columns * 4), jnp.bfloat16),
            pltpu.VMEM((depth * count, 3 * width), jnp.bfloat16),
            pltpu.VMEM((length, width), jnp.bfloat16),
            pltpu.VMEM((width // LANES, length, LANES), jnp.float32),
            pltpu.VMEM((width // LANES, rows // PIECES, LANES), jnp.float32),
            pltpu.VMEM((length, width), jnp.bfloat16),
            pltpu.VMEM((CHUNKS * modes, LANES), jnp.float32),
            pltpu.VMEM((CHUNKS * modes, LANES), jnp.float32),
        ] + [table] * 4 + [
            pltpu.VMEM((width // LANES, modes, CHUNKS, LANES), jnp.float32),
            pltpu.VMEM((width // LANES, modes, CHUNKS, LANES), jnp.float32),
            table,
            dma((7,)),
            dma((count, 2)), dma((count, PIECES)),
            dma((count,)), dma((count, PIECES)),
            dma((count, PIECES)),
            dma((count,)),
            dma((count,)), dma((count, 3)),
            dma((count,)), dma((count,)),
            dma((1,)),
        ],
        compiler_params=pltpu.CompilerParams(
            collective_id=0, has_side_effects=True, vmem_limit_bytes=40 * 2**20
        ),
    )(*(pltpu.with_memory_space_constraint(array, pltpu.HBM) for array in operands))
    return settle(gated, state)


def settle_kernel(gated_ref, state_ref, out_ref, final_ref, sem):
    rows = gated_ref.shape[0]
    part = rows // PIECES
    copies = [
        pltpu.make_async_copy(
            gated_ref.at[pl.ds(p * part, part), :], out_ref.at[pl.ds(p * part, part), :], sem.at[p]
        )
        for p in range(PIECES)
    ] + [pltpu.make_async_copy(state_ref, final_ref, sem.at[PIECES])]
    for copy in copies:
        copy.start()
    for copy in copies:
        copy.wait()


def settle(gated, state):
    anywhere = pl.BlockSpec(memory_space=pl.ANY)
    out, final = pl.pallas_call(
        settle_kernel,
        out_shape=(
            jax.ShapeDtypeStruct(gated.shape, gated.dtype),
            jax.ShapeDtypeStruct(state.shape, state.dtype),
        ),
        in_specs=[anywhere] * 2,
        out_specs=(anywhere, anywhere),
        scratch_shapes=[pltpu.SemaphoreType.DMA((PIECES + 1,))],
        compiler_params=pltpu.CompilerParams(vmem_limit_bytes=2**20),
    )(gated, state)
    return out, final.T


def per_device_channels(tokens, w_query, w_key, w_value, decay_rate, residue, carried):
    count = lax.axis_size("seq")
    return whole_layer(tokens, w_query, w_key, w_value, decay_rate, residue, carried, count)


def solution(mesh):
    in_specs = (
        P(("parts", "seq"), ("chan", "rep")),
        P("seq", ("chan", "rep")),
        P("seq", ("chan", "rep")),
        P("seq", ("chan", "rep")),
        P(("chan", "rep", "seq"), None),
        P(("chan", "rep", "seq"), None),
        P(("parts", "chan", "rep", "seq"), None),
    )
    out_specs = (P(("parts", "seq"), ("chan", "rep")), P(("parts", "chan", "rep", "seq"), None))

    def body(*arrays):
        own_channels = arrays[4].shape[0]
        mates = all(mesh.shape[a] == 2 for a in ("parts", "chan", "rep"))
        chosen = per_device_channels if own_channels % LANES == 0 and mates else per_device
        return chosen(*arrays)

    return jax.shard_map(body, mesh=mesh, in_specs=in_specs, out_specs=out_specs, check_vma=False)
```
